512 devices in a mesh: gx: 32 (over z, core), gy: 4 (over x), gz: 4 (over y).
Axes of the slice: x: 4, y: 4, z: 16, core: 2. Of those that a mesh axis runs over, the one named last changes fastest.
Arguments:
- adjoint_final: float32 [16, 512, 512], P('gz', 'gx', 'gy'), may hold values from -6 to 6
- conductivity: float32 [3, 16, 512, 512], P(None, 'gz', 'gx', 'gy'), may hold values from 0.05 to 1
- step_ratio: float32 [16, 512, 512], P('gz', 'gx', 'gy'), may hold values from 0.04 to 0.16
- refine_rate: float32 [16, 512, 512], P('gz', 'gx', 'gy'), may hold values from 0.05 to 0.24
- residual: float32 [4, 8192], P(None, ('gx', 'gy')), may hold values from -6 to 6
- sensor_tile: int32 [8192], P(('gx', 'gy')), may hold values from 0 to 127, as said below
- sensor_cell: int32 [8192], P(('gx', 'gy')), may hold values from 0 to 32767
- substeps: int32 [32, 4], replicated, may hold values from 1 to 6, as said below
Outputs:
- adjoint_start: float32 [16, 512, 512], P('gz', 'gx', 'gy')
- sensitivity: float32 [16, 512, 512], P('gz', 'gx', 'gy')
The draws below stay inside these ranges and needn't reach their ends.
Inputs may be any that keep to these rules, and one draw needn't show every extreme that they name: `sensor_tile`: tiles are numbered ix * 4 + iy. Among the 64 sensors of each aligned block at most 4 name one tile, and in every block some tile is named by exactly 4 of them. `substeps`: some tile takes 6 sub-steps in every draw.
All inputs are finite; a program needn't handle non-finite values.
Results may differ from the reference program's by a relative error of at most 0.000079.
Values sent between devices are 32-bit elements; how exact they have to be, the bound alone decides.
No kernel may reach another device: no remote copies, remote signals or barrier semaphores. Data moves between devices by JAX's collectives and lax.ppermute only.
A program may use at most 64 MiB of HBM per device.

```python
import math
import jax
import jax.numpy as jnp

CX = 16
CY = 128
NS_DEV = 64
STEPS = 4
MAXSUB = 6
TGX = 32
TGY = 4
TILES = 128
NX = 512
NY = 512
NZ = 16
SENSORS = 8192
SLOTS = 4
N_GX = 32
N_GY = 4


def draw_sensor_tile(key, part):
    key_hot, key_other, key_order = jax.random.split(key, 3)
    hottest = jax.random.randint(key_hot, (), 0, TILES)
    others = jax.vmap(lambda sub: jax.random.permutation(sub, TILES - 1))(jax.random.split(key_other, TILES))
    places = jnp.arange(NS_DEV)
    picked = others[:, (places - SLOTS) % (TILES - 1)]
    picked = picked + (picked >= hottest).astype(jnp.int32)
    tiles = jnp.where(places[None, :] < SLOTS, hottest, picked)
    orders = jax.vmap(lambda sub: jax.random.permutation(sub, NS_DEV))(jax.random.split(key_order, TILES))
    tiles = jnp.take_along_axis(tiles, orders, axis=1)
    return tiles.reshape(-1).astype(jnp.int32)


def draw_substeps(key, part):
    key_base, key_hot, key_force = jax.random.split(key, 3)
    baseline = jax.random.randint(key_base, (TGX, TGY), 1, 3)
    heated = jax.random.randint(key_hot, (TGX, TGY), 0, 8) == 0
    forced = jax.random.randint(key_force, (), 0, TILES)
    heated = heated.reshape(-1) | (jnp.arange(TILES) == forced)
    return jnp.where(heated.reshape(TGX, TGY), MAXSUB, baseline).astype(jnp.int32)


def set_ends(values, key, low, top_value):
    dims = values.shape
    place = [jax.random.randint(jax.random.fold_in(key, axis), (), 0, dims[axis]) for axis in range(len(dims))]
    values = values.at[tuple(place)].set(low)
    longest = dims.index(max(dims))
    place[longest] = (place[longest] + 1) % dims[longest]
    return values.at[tuple(place)].set(top_value)


def levels(rng, dims, shards, low, largest):
    level = 1.0
    for axis_at, shards_of in shards:
        draws = jax.random.uniform(jax.random.fold_in(jax.random.fold_in(rng, 6), axis_at), (shards_of,), jnp.float32, low / len(shards), largest / len(shards))
        level = level * jnp.repeat(jnp.exp(draws), dims[axis_at] // shards_of).reshape((-1,) + (1,) * (len(dims) - 1 - axis_at))
    return level


def gaussian(key, dims, spread, reach, shards=(), dtype=jnp.bfloat16):
    result = jax.random.normal(key, dims, jnp.float32) * spread
    if len(shards) > 0:
        result = levels(key, dims, shards, -0.22, 0.18) * result
    return jnp.clip(result, min=-reach, max=reach).astype(dtype)


def setup_inputs(seed: int = 0) -> dict:
    seeds = jax.random.split(jax.random.key(seed), 9)
    return {
        "adjoint_final": gaussian(seeds[0], (NZ, NX, NY), 1.0, 6.0, ((0, 4), (1, 32), (2, 4)), jnp.float32),
        "conductivity": jnp.clip(jnp.exp(math.log(1.0) - 2.9957323 * jax.random.uniform(seeds[1], (3, NZ, NX, NY), jnp.float32) ** levels(seeds[1], (3, NZ, NX, NY), ((1, 4), (2, 32), (3, 4)), -0.2, 0.2)), 0.05, 1.0),
        "step_ratio": jnp.clip(jnp.exp(math.log(0.16) - 1.3862944 * jax.random.uniform(seeds[2], (NZ, NX, NY), jnp.float32) ** levels(seeds[2], (NZ, NX, NY), ((0, 4), (1, 32), (2, 4)), -0.2, 0.2)), 0.04, 0.16),
        "refine_rate": jnp.clip(jnp.exp(math.log(0.24) - 1.5686159 * jax.random.uniform(seeds[3], (NZ, NX, NY), jnp.float32) ** levels(seeds[3], (NZ, NX, NY), ((0, 4), (1, 32), (2, 4)), -0.2, 0.2)), 0.05, 0.24),
        "residual": gaussian(seeds[4], (STEPS, SENSORS), 1.0, 6.0, ((1, 128),), jnp.float32),
        "sensor_tile": draw_sensor_tile(jax.random.fold_in(seeds[8], 71), 0),
        "sensor_cell": set_ends(jax.random.randint(seeds[6], (SENSORS,), 0, NZ * CX * CY), jax.random.fold_in(seeds[6], 1), 0, (NZ * CX * CY) - 1).astype(jnp.int32),
        "substeps": draw_substeps(jax.random.fold_in(seeds[8], 71), 0),
    }


def harmonic(first, second):
    return 2.0 * first * second / (first + second)


def lateral_tiles(field):
    down_diff = field[:, :, 1:] - field[:, :, :-1]
    side_diff = field[..., 1:] - field[..., :-1]
    rows_part = jnp.pad(down_diff, ((0, 0), (0, 0), (0, 1), (0, 0), (0, 0))) - jnp.pad(down_diff, ((0, 0), (0, 0), (1, 0), (0, 0), (0, 0)))
    cols_part = jnp.pad(side_diff, ((0, 0), (0, 0), (0, 0), (0, 0), (0, 1))) - jnp.pad(side_diff, ((0, 0), (0, 0), (0, 0), (0, 0), (1, 0)))
    return rows_part + cols_part


def reference(adjoint_final, conductivity, step_ratio, refine_rate, residual, sensor_tile, sensor_cell, substeps):
    padded = jnp.pad(conductivity, ((0, 0), (1, 1), (1, 1), (1, 1)))
    row_up = harmonic(conductivity[0], padded[0, 1:-1, 2:, 1:-1])
    row_down = harmonic(conductivity[0], padded[0, 1:-1, :-2, 1:-1])
    col_up = harmonic(conductivity[1], padded[1, 1:-1, 1:-1, 2:])
    col_down = harmonic(conductivity[1], padded[1, 1:-1, 1:-1, :-2])
    layer_up = harmonic(conductivity[2], padded[2, 2:, 1:-1, 1:-1])
    layer_down = harmonic(conductivity[2], padded[2, :-2, 1:-1, 1:-1])
    tile_row = sensor_tile // N_GY
    tile_col = sensor_tile % N_GY
    layer_of = sensor_cell // (CX * CY)
    within = sensor_cell % (CX * CY)
    grid_row = tile_row * CX + within // CY
    grid_col = tile_col * CY + within % CY
    target = (layer_of * (NX * NY) + grid_row * NY + grid_col).astype(jnp.int32)
    counts = substeps[None, :, None, :, None]
    rates = refine_rate.reshape(NZ, N_GX, CX, N_GY, CY)
    adjoint = adjoint_final
    sensitivity = jnp.zeros_like(adjoint_final)
    for step_index in range(STEPS - 1, -1, -1):
        flat = adjoint.reshape(-1).at[target].add(residual[step_index])
        adjoint = flat.reshape(NZ, NX, NY)
        weighted = step_ratio * adjoint
        wpad = jnp.pad(weighted, 1)
        adjoint = adjoint + (row_up * (wpad[1:-1, 2:, 1:-1] - weighted) + row_down * (wpad[1:-1, :-2, 1:-1] - weighted)
                             + col_up * (wpad[1:-1, 1:-1, 2:] - weighted) + col_down * (wpad[1:-1, 1:-1, :-2] - weighted)
                             + layer_up * (wpad[2:, 1:-1, 1:-1] - weighted) + layer_down * (wpad[:-2, 1:-1, 1:-1] - weighted))
        tiled = adjoint.reshape(NZ, N_GX, CX, N_GY, CY)
        for turn in range(MAXSUB):
            tiled = jnp.where(counts > turn, tiled + lateral_tiles(rates * tiled), tiled)
        adjoint = tiled.reshape(NZ, NX, NY)
        sensitivity = sensitivity + step_ratio * adjoint
    return adjoint, sensitivity
```

```python
import functools

import jax
import jax.numpy as jnp
from jax import lax
from jax.experimental import pallas as pl
from jax.experimental.pallas import tpu as pltpu
from jax.sharding import PartitionSpec as P

F32 = jnp.float32
BF16 = jnp.bfloat16
LANES = 128
WIDE = 32
QUART = LANES // WIDE
SLOTS = 4
FIELDS = 6
TINY = 1e-30
LIMIT = 24 * 2**20


def iota(shape, dim):
    return lax.broadcasted_iota(jnp.int32, shape, dim)


def harmonic(first, second):
    return 2.0 * first * second / jnp.maximum(first + second, TINY)


def swap(field):
    return jnp.concatenate([field[:, 1:2], field[:, 0:1]], axis=1)


def call(kernel, outs, name, cost=20000):
    vmem = pl.BlockSpec(memory_space=pltpu.VMEM)
    smem = pl.BlockSpec(memory_space=pltpu.SMEM)

    def run(*args):
        return pl.pallas_call(
            kernel,
            out_shape=[jax.ShapeDtypeStruct(o, F32) for o in outs],
            in_specs=[smem if a.dtype == jnp.int32 and a.ndim == 2 and a.shape[0] > 1 else vmem for a in args],
            out_specs=[vmem] * len(outs),
            name=name,
            compiler_params=pltpu.CompilerParams(vmem_limit_bytes=LIMIT),
            cost_estimate=pl.CostEstimate(flops=cost, bytes_accessed=cost, transcendentals=0),
        )(*args)

    return run


def pack_sensors(gy, residual_ref, tile_ref, cell_ref, out_ref):
    count = residual_ref.shape[1]
    tiles = out_ref.shape[0]
    eye = iota((count, count), 0) == iota((count, count), 1)

    def column(row):
        return jnp.sum(jnp.where(eye, jnp.broadcast_to(row, (count, count)), 0.0), axis=1, keepdims=True)

    tile_row = tile_ref[...].astype(F32)
    tile_col = column(tile_row)
    same = (tile_col == tile_row) & (iota((count, count), 1) < iota((count, count), 0))
    rank = jnp.sum(same.astype(F32), axis=1, keepdims=True).astype(jnp.int32)
    values = [column(residual_ref[s : s + 1, :]) for s in range(4)]
    values.append(column(cell_ref[...].astype(F32) + 1.0))
    lane = iota((count, LANES), 1)
    within = lane % 8
    spread = jnp.zeros((count, LANES), F32)
    for place, value in enumerate(values):
        spread = jnp.where(within == place, value, spread)
    spread = jnp.where((lane % 32) // 8 == rank, spread, 0.0)
    tile_at = iota((tiles, count), 0)
    named = tile_row.astype(jnp.int32)
    total = jnp.zeros((tiles, LANES), F32)
    for group, (step, edge) in enumerate(((0, -1), (-1, 0), (1, gy - 1))):
        hit = (named == tile_at + step) & (tile_at % gy != edge)
        part = jnp.where(lane // 32 == group, spread, 0.0)
        total = total + jnp.dot(hit.astype(F32), part, precision=lax.Precision.HIGHEST, preferred_element_type=F32)
    out_ref[...] = total


def stacked(refs, field, layer):
    each = refs[0].shape[1]
    return refs[layer // each][field, layer % each]


def pack_columns(below_ref, own_ref, above_ref, left_ref, right_ref):
    refs = (below_ref, own_ref, above_ref)
    layers = 3 * own_ref.shape[1]
    rows = own_ref.shape[2]
    quarter = iota((rows, LANES), 1) // WIDE
    for j in range(FIELDS * layers // QUART):
        left = right = None
        for q in range(QUART):
            p = j * QUART + q
            plane = stacked(refs, p // layers, p % layers)
            to_left = plane if q == 0 else pltpu.roll(plane, WIDE * q, 1)
            shift = (WIDE * q + WIDE) % LANES
            to_right = plane if shift == 0 else pltpu.roll(plane, shift, 1)
            left = to_left if q == 0 else jnp.where(quarter == q, to_left, left)
            right = to_right if q == 0 else jnp.where(quarter == q, to_right, right)
        left_ref[j] = left
        right_ref[j] = right


def scatter(got, got_t, row_base, rows_out, groups):
    blocks = got.shape[0]
    lane = iota((blocks, LANES), 1)
    row_at = iota((rows_out, blocks), 0)
    onehot, first, second, third = [], [], [], []
    for group, low, high in groups:
        for slot in range(SLOTS):
            base = group * 32 + slot * 8
            cell_row = got_t[base + 4 : base + 5, :].astype(jnp.int32) - 1
            cell_col = got[:, base + 4 : base + 5].astype(jnp.int32) - 1
            hit = (cell_row >> 7) - row_base == row_at
            onehot.append(hit.astype(F32).astype(BF16))
            at = (cell_col & 127) == lane
            if low > 0:
                at = at & (lane >= low)
            if high < LANES:
                at = at & (lane < high)
            parts = []
            for s in range(4):
                parts.append(jnp.where(at, got[:, base + s : base + s + 1], 0.0))
            value = jnp.concatenate(parts, axis=1)
            one = value.astype(BF16)
            rest = value - one.astype(F32)
            two = rest.astype(BF16)
            three = (rest - two.astype(F32)).astype(BF16)
            first.append(one)
            second.append(two)
            third.append(three)
    onehot = jnp.concatenate(onehot, axis=1)
    total = None
    for part in (first, second, third):
        term = jnp.dot(onehot, jnp.concatenate(part, axis=0), preferred_element_type=F32)
        total = term if total is None else total + term
    return total


def prepare(layer_axis, below_ref, own_ref, above_ref, left_ref, right_ref, sensors_ref, state_ref, fixed_ref, source_ref, up_ref, down_ref):
    refs = (below_ref, own_ref, above_ref)
    own = own_ref.shape[1]
    layers = 3 * own
    rows = own_ref.shape[2]
    lane = iota((rows, LANES), 1)

    def field(f):
        planes = []
        for l in range(layers):
            p = f * layers + l
            j, q = p // QUART, p % QUART
            from_left = pltpu.roll(left_ref[j], (LANES - WIDE - WIDE * q) % LANES, 1) if q != QUART - 1 else left_ref[j]
            from_right = pltpu.roll(right_ref[j], LANES - WIDE * q, 1) if q != 0 else right_ref[j]
            side = jnp.where(lane < WIDE, from_right, jnp.where(lane >= LANES - WIDE, from_left, 0.0))
            planes.append(jnp.stack([stacked(refs, f, l), side], axis=0))
        return jnp.stack(planes, axis=0)

    shape = (layers, 2, rows, LANES)
    row = iota(shape, 2)
    col = iota(shape, 3)
    adjoint, along_rows, along_cols, along_layers, ratio, rate = [field(f) for f in range(FIELDS)]
    fixed_ref[0] = harmonic(along_rows, jnp.where(row == rows - 1, 0.0, pltpu.roll(along_rows, rows - 1, 2)))
    rolled = pltpu.roll(along_cols, LANES - 1, 3)
    fixed_ref[1] = harmonic(along_cols, jnp.where(col == LANES - 1, swap(rolled), rolled))
    fixed_ref[2, : layers - 1] = harmonic(along_layers[: layers - 1], along_layers[1:])
    fixed_ref[2, layers - 1 :] = jnp.zeros((1, 2, rows, LANES), F32)
    fixed_ref[3] = ratio
    fixed_ref[4] = rate
    row_base = (lax.axis_index(layer_axis) * own - own) * rows
    got = sensors_ref[...]
    got_t = got.T
    centre = scatter(got, got_t, row_base, layers * rows, ((0, 0, LANES),))
    side = scatter(got, got_t, row_base, layers * rows, ((1, LANES - WIDE, LANES), (2, 0, WIDE)))
    source = []
    for s in range(4):
        parts = [m[:, s * LANES : (s + 1) * LANES].reshape(layers, 1, rows, LANES) for m in (centre, side)]
        source.append(jnp.concatenate(parts, axis=1))
    for s in range(3):
        source_ref[s] = source[s]
    adjoint = adjoint + source[3]
    state_ref[...] = adjoint
    weighted = ratio * adjoint
    up_ref[0] = weighted[:, :, 0:1, :]
    up_ref[1] = along_rows[:, :, 0:1, :]
    down_ref[0] = weighted[:, :, rows - 1 :, :]
    down_ref[1] = along_rows[:, :, rows - 1 :, :]


def step(axes, turn, *refs):
    first, last = turn == 3, turn == 0
    refs = list(refs)
    substeps_ref, state_ref, fixed_ref, above_ref, below_ref = refs[:5]
    refs = refs[5:]
    if first:
        own_up_ref, own_down_ref = refs[:2]
    else:
        row_edge_ref, sens_ref = refs[:2]
    refs = refs[2:]
    if not last:
        source_ref = refs[0]
        refs = refs[1:]
    if first:
        state_out, up_out, down_out, sens_out, edge_out = refs
    elif not last:
        state_out, up_out, down_out, sens_out = refs
    else:
        state_out, sens_out = refs
    gx, gy = axes
    at_x, at_y = lax.axis_index(gx), lax.axis_index(gy)
    n_x, n_y = lax.axis_size(gx), lax.axis_size(gy)
    layers, _, rows, _ = state_ref.shape
    total = fixed_ref.shape[1]
    low = (total - layers) // 2
    span = slice(low, low + layers)
    inner = slice(low + 1, low + layers - 1)
    state = state_ref[...]
    weighted = fixed_ref[3, span] * state
    if first:
        edges = []
        for mine, other, there in ((own_up_ref, above_ref, at_x > 0), (own_down_ref, below_ref, at_x < n_x - 1)):
            edges.append(harmonic(mine[1], jnp.where(there, other[1], 0.0)))
        edge_out[0] = edges[0]
        edge_out[1] = edges[1]
        over, under = edges[0][1:-1], edges[1][1:-1]
    else:
        over, under = row_edge_ref[0, inner], row_edge_ref[1, inner]
    shape = (layers - 2, 2, rows, LANES)
    row, col = iota(shape, 2), iota(shape, 3)
    across = weighted[1:-1]
    halo_over = above_ref[0, 1:-1]
    halo_under = below_ref[0, 1:-1]
    flux = fixed_ref[0, inner] * (pltpu.roll(across, rows - 1, 2) - across)
    edge_low = over * (across[:, :, 0:1, :] - halo_over)
    edge_high = under * (halo_under - across[:, :, rows - 1 :, :])
    flux = jnp.where(row == rows - 1, edge_high, flux)
    change = flux - jnp.where(row == 0, edge_low, pltpu.roll(flux, 1, 2))
    rolled = pltpu.roll(across, LANES - 1, 3)
    flux = fixed_ref[1, inner] * (jnp.where(col == LANES - 1, swap(rolled), rolled) - across)
    rolled = pltpu.roll(flux, 1, 3)
    change = change + (flux - jnp.where(col == 0, swap(rolled), rolled))
    flux = fixed_ref[2, low : low + layers - 1] * (weighted[1:] - weighted[:-1])
    change = change + (flux[1:] - flux[:-1])
    state = state[1:-1] + change
    mine = substeps_ref[at_y, at_x]
    if last:
        state = state[:, 0:1]
        rate = fixed_ref[4, inner, 0:1]
        most = mine
    else:
        rate = fixed_ref[4, inner]
        to_left = substeps_ref[jnp.maximum(at_y - 1, 0), at_x]
        to_right = substeps_ref[jnp.minimum(at_y + 1, n_y - 1), at_x]
        most = jnp.maximum(mine, jnp.maximum(to_left, to_right))
        side = iota((1, 1, rows, LANES), 3)
        counts = jnp.concatenate(
            [jnp.full((1, 1, rows, LANES), mine, jnp.int32), jnp.where(side < LANES // 2, to_right, to_left)],
            axis=1,
        )
    row, col = iota(state.shape, 2), iota(state.shape, 3)

    def one_turn(at, now):
        v = rate * now
        near = jnp.where(row == rows - 1, v, pltpu.roll(v, rows - 1, 2)) + jnp.where(row == 0, v, pltpu.roll(v, 1, 2))
        near = near + jnp.where(col == LANES - 1, v, pltpu.roll(v, LANES - 1, 3))
        near = near + jnp.where(col == 0, v, pltpu.roll(v, 1, 3))
        after = now + (near - 4.0 * v)
        if last:
            return after
        return jnp.where(at < counts, after, now)

    state = lax.fori_loop(jnp.int32(0), most, one_turn, state)
    own = total // 3
    keep = slice((layers - 2 - own) // 2, (layers - 2 - own) // 2 + own)
    addend = fixed_ref[3, own : 2 * own, 0] * state[keep, 0]
    sens_out[...] = addend if first else sens_ref[...] + addend
    if last:
        state_out[...] = state[:, 0]
        return
    state = state + source_ref[turn - 1, inner]
    state_out[...] = state
    weighted = fixed_ref[3, inner] * state
    up_out[0] = weighted[:, :, 0:1, :]
    down_out[0] = weighted[:, :, rows - 1 :, :]


def shift(cells, axis, by, wrap):
    count = lax.axis_size(axis)
    pairs = [(i, (i + by) % count) for i in range(count) if wrap or 0 <= i + by < count]
    return lax.ppermute(cells, axis, pairs)


def body(adjoint_final, conductivity, step_ratio, refine_rate, residual, sensor_tile, sensor_cell, substeps):
    own, rows, cols = adjoint_final.shape
    layers = 3 * own
    n_y = lax.axis_size("gy")
    tiles = lax.axis_size("gx") * n_y
    listed = sensor_tile.shape[0]
    fields = jnp.concatenate([adjoint_final[None], conductivity, step_ratio[None], refine_rate[None]], axis=0)
    below = shift(fields, "gz", 1, False)
    above = shift(fields, "gz", -1, False)
    (message,) = call(functools.partial(pack_sensors, n_y), [(tiles, LANES)], "pack_sensors")(
        residual, sensor_tile.reshape(1, listed), sensor_cell.reshape(1, listed)
    )
    sensors = lax.all_to_all(message, ("gx", "gy"), 0, 0, tiled=True)
    packed = (FIELDS * layers // QUART, rows, LANES)
    to_left, to_right = call(pack_columns, [packed, packed], "pack_columns")(below, fields, above)
    from_left = shift(to_right, "gy", 1, False)
    from_right = shift(to_left, "gy", -1, False)
    block = (layers, 2, rows, LANES)
    state, fixed, source, up, down = call(
        functools.partial(prepare, "gz"),
        [block, (5,) + block, (3,) + block, (2, layers, 2, 1, LANES), (2, layers, 2, 1, LANES)],
        "prepare",
    )(below, fields, above, from_left, from_right, sensors)
    sens = edge = None
    for turn in range(3, -1, -1):
        over = shift(down, "gx", 1, True)
        under = shift(up, "gx", -1, True)
        depth = state.shape[0] - 2
        args = [substeps.T, state, fixed]
        args += [over, under] + ([up, down] if turn == 3 else [edge, sens])
        if turn > 0:
            args += [source]
        face = (1, depth, 2, 1, LANES)
        if turn == 0:
            outs = [(own, rows, cols), (own, rows, cols)]
        else:
            outs = [(depth, 2, rows, LANES), face, face, (own, rows, cols)]
            if turn == 3:
                outs += [(2, layers, 2, 1, LANES)]
        got = call(functools.partial(step, ("gx", "gy"), turn), outs, "step")(*args)
        if turn == 3:
            state, up, down, sens, edge = got
        elif turn > 0:
            state, up, down, sens = got
        else:
            return tuple(got)


def solution(mesh):
    return jax.shard_map(
        body,
        mesh=mesh,
        in_specs=(
            P("gz", "gx", "gy"),
            P(None, "gz", "gx", "gy"),
            P("gz", "gx", "gy"),
            P("gz", "gx", "gy"),
            P(None, ("gx", "gy")),
            P(("gx", "gy")),
            P(("gx", "gy")),
            P(),
        ),
        out_specs=(P("gz", "gx", "gy"), P("gz", "gx", "gy")),
        check_vma=False,
    )
```

```python
import functools

import jax
import jax.numpy as jnp
from jax import lax
from jax.experimental import pallas as pl
from jax.experimental.pallas import tpu as pltpu
from jax.sharding import PartitionSpec as P

F32 = jnp.float32
BF16 = jnp.bfloat16
LANES = 128
WIDE = 32
QUART = LANES // WIDE
SLOTS = 4
FIELDS = 6
TINY = 1e-30
LIMIT = 24 * 2**20


def iota(shape, dim):
    return lax.broadcasted_iota(jnp.int32, shape, dim)


def harmonic(first, second):
    return 2.0 * first * second / jnp.maximum(first + second, TINY)


def swap(field):
    return jnp.concatenate([field[:, 1:2], field[:, 0:1]], axis=1)


def call(kernel, outs, name, cost=20000, aliases={}):
    vmem = pl.BlockSpec(memory_space=pltpu.VMEM)
    smem = pl.BlockSpec(memory_space=pltpu.SMEM)
    untouched = pl.BlockSpec(memory_space=pl.ANY)

    def run(*args):
        return pl.pallas_call(
            kernel,
            out_shape=[jax.ShapeDtypeStruct(o, F32) for o in outs],
            in_specs=[
                untouched if at in aliases else smem if a.dtype == jnp.int32 and a.shape[0] > 1 else vmem
                for at, a in enumerate(args)
            ],
            input_output_aliases=aliases,
            out_specs=[untouched if at in aliases.values() else vmem for at in range(len(outs))],
            name=name,
            compiler_params=pltpu.CompilerParams(vmem_limit_bytes=LIMIT),
            cost_estimate=pl.CostEstimate(flops=cost, bytes_accessed=cost, transcendentals=0),
        )(*args)

    return run


def pack(gy, fields_in, residual_ref, tile_ref, cell_ref, fields_out, out_ref):
    count = residual_ref.shape[1]
    tiles = out_ref.shape[0]
    eye = iota((count, count), 0) == iota((count, count), 1)

    def column(row):
        return jnp.sum(jnp.where(eye, jnp.broadcast_to(row, (count, count)), 0.0), axis=1, keepdims=True)

    named = tile_ref[...]
    tile_row = named.astype(F32)
    tile_col = column(tile_row)
    same = (tile_col == tile_row) & (iota((count, count), 1) < iota((count, count), 0))
    rank = jnp.sum(same.astype(F32), axis=1, keepdims=True).astype(jnp.int32)
    values = [column(residual_ref[s : s + 1, :]) for s in range(4)]
    values.append(column(cell_ref[...].astype(F32) + 1.0))
    lane = iota((count, LANES), 1)
    within = lane % 8
    spread = jnp.zeros((count, LANES), F32)
    for place, value in enumerate(values):
        spread = jnp.where(within == place, value, spread)
    spread = jnp.where((lane % 32) // 8 == rank, spread, 0.0)
    tile_at = iota((tiles, count), 0)
    total = jnp.zeros((tiles, LANES), F32)
    for group, (step, edge) in enumerate(((0, -1), (-1, 0), (1, gy - 1))):
        hit = (named == tile_at + step) & (tile_at % gy != edge)
        part = jnp.where(lane // 32 == group, spread, 0.0)
        total = total + jnp.dot(hit.astype(F32), part, precision=lax.Precision.HIGHEST, preferred_element_type=F32)
    out_ref[...] = total


def stacked(refs, field, layer):
    each = refs[0].shape[1]
    return refs[layer // each][field, layer % each]


def pack_columns(substeps_ref, below_ref, own_ref, above_ref, left_ref, right_ref):
    refs = (below_ref, own_ref, above_ref)
    layers = 3 * own_ref.shape[1]
    rows = own_ref.shape[2]
    quarter = iota((rows, LANES), 1) // WIDE
    for j in range(FIELDS * layers // QUART):
        left = right = None
        for q in range(QUART):
            p = j * QUART + q
            plane = stacked(refs, p // layers, p % layers)
            to_left = plane if q == 0 else pltpu.roll(plane, WIDE * q, 1)
            shift = (WIDE * q + WIDE) % LANES
            to_right = plane if shift == 0 else pltpu.roll(plane, shift, 1)
            left = to_left if q == 0 else jnp.where(quarter == q, to_left, left)
            right = to_right if q == 0 else jnp.where(quarter == q, to_right, right)
        left_ref[j] = left
        right_ref[j] = right


def scatter(got, got_t, row_base, rows_out, groups, steps):
    blocks = got.shape[0]
    lane = iota((blocks, LANES), 1)
    row_at = iota((rows_out, blocks), 0)
    onehot, first, second, third = [], [], [], []
    for group, low, high in groups:
        for slot in range(SLOTS):
            base = group * 32 + slot * 8
            cell_row = got_t[base + 4 : base + 5, :].astype(jnp.int32) - 1
            cell_col = got[:, base + 4 : base + 5].astype(jnp.int32) - 1
            hit = (cell_row >> 7) - row_base == row_at
            onehot.append(hit.astype(F32).astype(BF16))
            at = (cell_col & 127) == lane
            if low > 0:
                at = at & (lane >= low)
            if high < LANES:
                at = at & (lane < high)
            value = jnp.concatenate([jnp.where(at, got[:, base + s : base + s + 1], 0.0) for s in steps], axis=1)
            one = value.astype(BF16)
            rest = value - one.astype(F32)
            two = rest.astype(BF16)
            three = (rest - two.astype(F32)).astype(BF16)
            first.append(one)
            second.append(two)
            third.append(three)
    onehot = jnp.concatenate(onehot, axis=1)
    total = None
    for part in (first, second, third):
        term = jnp.dot(onehot, jnp.concatenate(part, axis=0), preferred_element_type=F32)
        total = term if total is None else total + term
    return total


def sources(layer_axis, own, layers, rows, sensors_ref, steps):
    row_base = (lax.axis_index(layer_axis) * own - own) * rows
    got = sensors_ref[...]
    got_t = got.T
    centre = scatter(got, got_t, row_base, layers * rows, ((0, 0, LANES),), steps)
    side = scatter(got, got_t, row_base, layers * rows, ((1, LANES - WIDE, LANES), (2, 0, WIDE)), steps)
    out = []
    for s in range(len(steps)):
        parts = [m[:, s * LANES : (s + 1) * LANES].reshape(layers, 1, rows, LANES) for m in (centre, side)]
        out.append(jnp.concatenate(parts, axis=1))
    return out


def prepare(below_ref, own_ref, above_ref, left_ref, right_ref, state_ref, fixed_ref, edge_ref):
    refs = (below_ref, own_ref, above_ref)
    own = own_ref.shape[1]
    layers = 3 * own
    rows = own_ref.shape[2]
    lane = iota((rows, LANES), 1)

    def field(f):
        planes = []
        for l in range(layers):
            p = f * layers + l
            j, q = p // QUART, p % QUART
            from_left = pltpu.roll(left_ref[j], (LANES - WIDE - WIDE * q) % LANES, 1) if q != QUART - 1 else left_ref[j]
            from_right = pltpu.roll(right_ref[j], LANES - WIDE * q, 1) if q != 0 else right_ref[j]
            side = jnp.where(lane < WIDE, from_right, jnp.where(lane >= LANES - WIDE, from_left, 0.0))
            planes.append(jnp.stack([stacked(refs, f, l), side], axis=0))
        return jnp.stack(planes, axis=0)

    shape = (layers, 2, rows, LANES)
    row = iota(shape, 2)
    col = iota(shape, 3)
    state_ref[...] = field(0)
    along_rows = field(1)
    edge_ref[0] = along_rows[:, :, 0:1, :]
    edge_ref[1] = along_rows[:, :, rows - 1 :, :]
    fixed_ref[0] = harmonic(along_rows, jnp.where(row == rows - 1, 0.0, pltpu.roll(along_rows, rows - 1, 2)))
    along_cols = field(2)
    rolled = pltpu.roll(along_cols, LANES - 1, 3)
    fixed_ref[1] = harmonic(along_cols, jnp.where(col == LANES - 1, swap(rolled), rolled))
    along_layers = field(3)
    fixed_ref[2, : layers - 1] = harmonic(along_layers[: layers - 1], along_layers[1:])
    fixed_ref[2, layers - 1 :] = jnp.zeros((1, 2, rows, LANES), F32)
    fixed_ref[3] = field(4)
    fixed_ref[4] = field(5)


def first_source(layer_axis, own, state_in, fixed_ref, edge_ref, sensors_ref, state_ref, up_ref, down_ref):
    layers, _, rows, _ = state_ref.shape
    (source,) = sources(layer_axis, own, layers, rows, sensors_ref, (3,))
    state = state_in[...] + source
    state_ref[...] = state
    weighted = fixed_ref[3] * state
    up_ref[0] = weighted[:, :, 0:1, :]
    up_ref[1] = edge_ref[0]
    down_ref[0] = weighted[:, :, rows - 1 :, :]
    down_ref[1] = edge_ref[1]


def other_sources(layer_axis, own, sensors_ref, source_ref):
    _, layers, _, rows, _ = source_ref.shape
    for s, source in enumerate(sources(layer_axis, own, layers, rows, sensors_ref, (0, 1, 2))):
        source_ref[s] = source


def step(axes, turn, *refs):
    first, last = turn == 3, turn == 0
    refs = list(refs)
    substeps_ref, state_ref, fixed_ref, above_ref, below_ref = refs[:5]
    refs = refs[5:]
    if first:
        own_up_ref, own_down_ref = refs[:2]
    else:
        row_edge_ref, sens_ref = refs[:2]
    refs = refs[2:]
    if not last:
        source_ref = refs[0]
        refs = refs[1:]
    if first:
        state_out, up_out, down_out, sens_out, edge_out = refs
    elif not last:
        state_out, up_out, down_out, sens_out = refs
    else:
        state_out, sens_out = refs
    gx, gy = axes
    at_x, at_y = lax.axis_index(gx), lax.axis_index(gy)
    n_x, n_y = lax.axis_size(gx), lax.axis_size(gy)
    layers, _, rows, _ = state_ref.shape
    total = fixed_ref.shape[1]
    low = (total - layers) // 2
    span = slice(low, low + layers)
    inner = slice(low + 1, low + layers - 1)
    state = state_ref[...]
    weighted = fixed_ref[3, span] * state
    if first:
        edges = []
        for mine, other, there in ((own_up_ref, above_ref, at_x > 0), (own_down_ref, below_ref, at_x < n_x - 1)):
            edges.append(harmonic(mine[1], jnp.where(there, other[1], 0.0)))
        edge_out[0] = edges[0]
        edge_out[1] = edges[1]
        over, under = edges[0][1:-1], edges[1][1:-1]
    else:
        over, under = row_edge_ref[0, inner], row_edge_ref[1, inner]
    shape = (layers - 2, 2, rows, LANES)
    row, col = iota(shape, 2), iota(shape, 3)
    across = weighted[1:-1]
    halo_over = above_ref[0, 1:-1]
    halo_under = below_ref[0, 1:-1]
    flux = fixed_ref[0, inner] * (pltpu.roll(across, rows - 1, 2) - across)
    edge_low = over * (across[:, :, 0:1, :] - halo_over)
    edge_high = under * (halo_under - across[:, :, rows - 1 :, :])
    flux = jnp.where(row == rows - 1, edge_high, flux)
    change = flux - jnp.where(row == 0, edge_low, pltpu.roll(flux, 1, 2))
    rolled = pltpu.roll(across, LANES - 1, 3)
    flux = fixed_ref[1, inner] * (jnp.where(col == LANES - 1, swap(rolled), rolled) - across)
    rolled = pltpu.roll(flux, 1, 3)
    change = change + (flux - jnp.where(col == 0, swap(rolled), rolled))
    flux = fixed_ref[2, low : low + layers - 1] * (weighted[1:] - weighted[:-1])
    change = change + (flux[1:] - flux[:-1])
    state = state[1:-1] + change
    mine = substeps_ref[at_y, at_x]
    if last:
        state = state[:, 0:1]
        rate = fixed_ref[4, inner, 0:1]
        most = mine
    else:
        rate = fixed_ref[4, inner]
        to_left = substeps_ref[jnp.maximum(at_y - 1, 0), at_x]
        to_right = substeps_ref[jnp.minimum(at_y + 1, n_y - 1), at_x]
        most = jnp.maximum(mine, jnp.maximum(to_left, to_right))
        side = iota((1, 1, rows, LANES), 3)
        counts = jnp.concatenate(
            [jnp.full((1, 1, rows, LANES), mine, jnp.int32), jnp.where(side < LANES // 2, to_right, to_left)],
            axis=1,
        )
    keep_own = 1.0 - 4.0 * rate
    half = rows // 2
    part = state.shape[:2] + (half, LANES)
    row, col = iota(part, 2), iota(part, 3)

    def one_turn(at, now):
        top, low_half = (rate[:, :, h : h + half] * now[:, :, h : h + half] for h in (0, half))
        up = pltpu.roll(top, half - 1, 2), pltpu.roll(low_half, half - 1, 2)
        down = pltpu.roll(top, 1, 2), pltpu.roll(low_half, 1, 2)
        near = (
            jnp.where(row == half - 1, up[1], up[0]) + jnp.where(row == 0, top, down[0]),
            jnp.where(row == half - 1, low_half, up[1]) + jnp.where(row == 0, down[0], down[1]),
        )
        parts = []
        for h, (v, rowwise) in enumerate(zip((top, low_half), near)):
            colwise = jnp.where(col == LANES - 1, v, pltpu.roll(v, LANES - 1, 3)) + jnp.where(col == 0, v, pltpu.roll(v, 1, 3))
            here = slice(h * half, (h + 1) * half)
            after = keep_own[:, :, here] * now[:, :, here] + (rowwise + colwise)
            if not last:
                after = jnp.where(at < counts[:, :, here], after, now[:, :, here])
            parts.append(after)
        return jnp.concatenate(parts, axis=2)

    state = lax.fori_loop(jnp.int32(0), most, one_turn, state)
    own = total // 3
    keep = slice((layers - 2 - own) // 2, (layers - 2 - own) // 2 + own)
    addend = fixed_ref[3, own : 2 * own, 0] * state[keep, 0]
    sens_out[...] = addend if first else sens_ref[...] + addend
    if last:
        state_out[...] = state[:, 0]
        return
    state = state + source_ref[turn - 1, inner]
    state_out[...] = state
    weighted = fixed_ref[3, inner] * state
    up_out[0] = weighted[:, :, 0:1, :]
    down_out[0] = weighted[:, :, rows - 1 :, :]


def shift(cells, axis, by, wrap):
    count = lax.axis_size(axis)
    pairs = [(i, (i + by) % count) for i in range(count) if wrap or 0 <= i + by < count]
    return lax.ppermute(cells, axis, pairs)


def body(adjoint_final, conductivity, step_ratio, refine_rate, residual, sensor_tile, sensor_cell, substeps):
    own, rows, cols = adjoint_final.shape
    layers = 3 * own
    n_y = lax.axis_size("gy")
    tiles = lax.axis_size("gx") * n_y
    listed = sensor_tile.shape[0]
    counts = substeps.T
    fields = jnp.concatenate([adjoint_final[None], conductivity, step_ratio[None], refine_rate[None]], axis=0)
    fields, message = call(functools.partial(pack, n_y), [fields.shape, (tiles, LANES)], "pack", aliases={0: 0})(
        fields, residual, sensor_tile.reshape(1, listed), sensor_cell.reshape(1, listed)
    )
    below = shift(fields, "gz", 1, False)
    above = shift(fields, "gz", -1, False)
    sensors = lax.all_to_all(message, ("gx", "gy"), 0, 0, tiled=True)
    packed = (FIELDS * layers // QUART, rows, LANES)
    to_left, to_right = call(pack_columns, [packed, packed], "pack_columns")(counts, below, fields, above)
    from_left = shift(to_right, "gy", 1, False)
    from_right = shift(to_left, "gy", -1, False)
    block = (layers, 2, rows, LANES)
    faces = (2, layers, 2, 1, LANES)
    state, fixed, edges = call(prepare, [block, (5,) + block, faces], "prepare")(below, fields, above, from_left, from_right)
    state, up, down = call(functools.partial(first_source, "gz", own), [block, faces, faces], "first_source")(state, fixed, edges, sensors)
    (source,) = call(functools.partial(other_sources, "gz", own), [(3,) + block], "other_sources")(sensors)
    sens = edge = None
    for turn in range(3, -1, -1):
        over = shift(down, "gx", 1, True)
        under = shift(up, "gx", -1, True)
        depth = state.shape[0] - 2
        args = [counts, state, fixed]
        args += [over, under] + ([up, down] if turn == 3 else [edge, sens])
        if turn > 0:
            args += [source]
        face = (1, depth, 2, 1, LANES)
        if turn == 0:
            outs = [(own, rows, cols), (own, rows, cols)]
        else:
            outs = [(depth, 2, rows, LANES), face, face, (own, rows, cols)]
            if turn == 3:
                outs += [(2, layers, 2, 1, LANES)]
        got = call(functools.partial(step, ("gx", "gy"), turn), outs, "step")(*args)
        if turn == 3:
            state, up, down, sens, edge = got
        elif turn > 0:
            state, up, down, sens = got
        else:
            return tuple(got)


def solution(mesh):
    return jax.shard_map(
        body,
        mesh=mesh,
        in_specs=(
            P("gz", "gx", "gy"),
            P(None, "gz", "gx", "gy"),
            P("gz", "gx", "gy"),
            P("gz", "gx", "gy"),
            P(None, ("gx", "gy")),
            P(("gx", "gy")),
            P(("gx", "gy")),
            P(),
        ),
        out_specs=(P("gz", "gx", "gy"), P("gz", "gx", "gy")),
        check_vma=False,
    )
```

```python
import functools

import jax
import jax.numpy as jnp
from jax import lax
from jax.experimental import pallas as pl
from jax.experimental.pallas import tpu as pltpu
from jax.sharding import PartitionSpec as P

F32 = jnp.float32
BF16 = jnp.bfloat16
LANES = 128
WIDE = 32
QUART = LANES // WIDE
MAXSUB = 6
SLOTS = 4
FIELDS = 6
TINY = 1e-30
LIMIT = 24 * 2**20


def iota(shape, dim):
    return lax.broadcasted_iota(jnp.int32, shape, dim)


def harmonic(first, second):
    return 2.0 * first * second / jnp.maximum(first + second, TINY)


def swap(field):
    return jnp.concatenate([field[:, 1:2], field[:, 0:1]], axis=1)


def call(kernel, outs, name, cost=20000, aliases={}):
    vmem = pl.BlockSpec(memory_space=pltpu.VMEM)
    untouched = pl.BlockSpec(memory_space=pl.ANY)

    def run(*args):
        return pl.pallas_call(
            kernel,
            out_shape=[jax.ShapeDtypeStruct(o, F32) for o in outs],
            in_specs=[
                untouched if at in aliases else vmem for at in range(len(args))
            ],
            input_output_aliases=aliases,
            out_specs=[untouched if at in aliases.values() else vmem for at in range(len(outs))],
            name=name,
            compiler_params=pltpu.CompilerParams(vmem_limit_bytes=LIMIT),
            cost_estimate=pl.CostEstimate(flops=cost, bytes_accessed=cost, transcendentals=0),
        )(*args)

    return run


def pack(gy, fields_in, residual_ref, tile_ref, cell_ref, fields_out, out_ref):
    count = residual_ref.shape[1]
    tiles = out_ref.shape[0]
    eye = iota((count, count), 0) == iota((count, count), 1)

    def column(row):
        return jnp.sum(jnp.where(eye, jnp.broadcast_to(row, (count, count)), 0.0), axis=1, keepdims=True)

    named = tile_ref[...]
    tile_row = named.astype(F32)
    tile_col = column(tile_row)
    same = (tile_col == tile_row) & (iota((count, count), 1) < iota((count, count), 0))
    rank = jnp.sum(same.astype(F32), axis=1, keepdims=True).astype(jnp.int32)
    values = [column(residual_ref[s : s + 1, :]) for s in range(4)]
    values.append(column(cell_ref[...].astype(F32) + 1.0))
    lane = iota((count, LANES), 1)
    within = lane % 8
    spread = jnp.zeros((count, LANES), F32)
    for place, value in enumerate(values):
        spread = jnp.where(within == place, value, spread)
    spread = jnp.where((lane % 32) // 8 == rank, spread, 0.0)
    tile_at = iota((tiles, count), 0)
    total = jnp.zeros((tiles, LANES), F32)
    for group, (step, edge) in enumerate(((0, -1), (-1, 0), (1, gy - 1))):
        hit = (named == tile_at + step) & (tile_at % gy != edge)
        part = jnp.where(lane // 32 == group, spread, 0.0)
        total = total + jnp.dot(hit.astype(F32), part, precision=lax.Precision.HIGHEST, preferred_element_type=F32)
    out_ref[...] = total


def stacked(refs, field, layer):
    each = refs[0].shape[1]
    return refs[layer // each][field, layer % each]


def pack_columns(below_ref, own_ref, above_ref, left_ref, right_ref):
    refs = (below_ref, own_ref, above_ref)
    layers = 3 * own_ref.shape[1]
    rows = own_ref.shape[2]
    quarter = iota((rows, LANES), 1) // WIDE
    for j in range(FIELDS * layers // QUART):
        left = right = None
        for q in range(QUART):
            p = j * QUART + q
            plane = stacked(refs, p // layers, p % layers)
            to_left = plane if q == 0 else pltpu.roll(plane, WIDE * q, 1)
            shift = (WIDE * q + WIDE) % LANES
            to_right = plane if shift == 0 else pltpu.roll(plane, shift, 1)
            left = to_left if q == 0 else jnp.where(quarter == q, to_left, left)
            right = to_right if q == 0 else jnp.where(quarter == q, to_right, right)
        left_ref[j] = left
        right_ref[j] = right


def spread_column(columns, at, shape):
    return jnp.broadcast_to(columns[:, at : at + 1], shape)


def sources(layer_axis, own, layers, rows, sensors_ref, steps):
    got = sensors_ref[...]
    blocks = got.shape[0]
    lane = iota((blocks, LANES), 1)
    lane_at = lane.astype(F32)
    cell = got.astype(jnp.int32) - 1
    row_base = (lax.axis_index(layer_axis) * own - own) * rows
    cell_row = ((cell >> 7) - row_base).astype(F32).T
    cell_col = cell & (LANES - 1)
    half = LANES // 2
    group_of = lane // 32
    cell_col = jnp.where(
        group_of == 0,
        cell_col,
        jnp.where(
            group_of == 1,
            jnp.where(cell_col >= LANES - WIDE, cell_col - half, -LANES),
            jnp.where(cell_col < WIDE, cell_col, -LANES),
        ),
    ).astype(F32)
    row_at = iota((layers * rows, blocks), 0).astype(F32)
    high = got.astype(BF16)
    values = (high, (got - high.astype(F32)).astype(BF16))
    onehots, tables = ([], []), ([], [])
    for group in range(3):
        for slot in range(SLOTS):
            base = group * 32 + slot * 8
            onehots[group > 0].append((cell_row[base + 4 : base + 5, :] == row_at).astype(F32).astype(BF16))
            at = spread_column(cell_col, base + 4, lane.shape)
            pairs = (0, half) if group > 0 and len(steps) > 1 else (0,)
            place = [(at == lane_at - by).astype(F32).astype(BF16) for by in pairs]
            line = []
            for part in range(2):
                cells = [spread_column(values[part], base + s, lane.shape) for s in steps]
                for k in range(0, len(cells), len(place)):
                    line.append(functools.reduce(jnp.add, [m * v for m, v in zip(place, cells[k : k + len(place)])]))
            tables[group > 0].append(jnp.concatenate(line, axis=1))
    sums = []
    for onehot, table in zip(onehots, tables):
        both = jnp.dot(jnp.concatenate(onehot, axis=1), jnp.concatenate(table, axis=0), preferred_element_type=F32)
        width = both.shape[1] // 2
        sums.append(both[:, :width] + both[:, width:])
    centre, side = sums
    lane = iota((layers * rows, LANES), 1)
    out = []
    for s in range(len(steps)):
        tile = side[:, (s // 2) * LANES : (s // 2 + 1) * LANES]
        turned = pltpu.roll(tile, half, 1)
        right, left = (tile, turned) if s % 2 == 0 else (turned, tile)
        beside = jnp.where(lane < WIDE, right, jnp.where(lane >= LANES - WIDE, left, 0.0))
        parts = [m.reshape(layers, 1, rows, LANES) for m in (centre[:, s * LANES : (s + 1) * LANES], beside)]
        out.append(jnp.concatenate(parts, axis=1))
    return out


def prepare(axes, substeps_ref, below_ref, own_ref, above_ref, left_ref, right_ref, state_ref, fixed_ref, edge_ref, counts_ref):
    refs = (below_ref, own_ref, above_ref)
    own = own_ref.shape[1]
    layers = 3 * own
    rows = own_ref.shape[2]
    lane = iota((rows, LANES), 1)

    def field(f):
        planes = []
        for l in range(layers):
            p = f * layers + l
            j, q = p // QUART, p % QUART
            from_left = pltpu.roll(left_ref[j], (LANES - WIDE - WIDE * q) % LANES, 1) if q != QUART - 1 else left_ref[j]
            from_right = pltpu.roll(right_ref[j], LANES - WIDE * q, 1) if q != 0 else right_ref[j]
            side = jnp.where(lane < WIDE, from_right, jnp.where(lane >= LANES - WIDE, from_left, 0.0))
            planes.append(jnp.stack([stacked(refs, f, l), side], axis=0))
        return jnp.stack(planes, axis=0)

    at_x, at_y = (lax.axis_index(axis) for axis in axes)
    n_y, n_x = substeps_ref.shape
    named = jnp.where(iota((n_y, n_x), 1) == at_x, substeps_ref[...].astype(F32), 0.0)

    def count(tile):
        rows_of = jnp.sum(jnp.where(iota((n_y, n_x), 0) == tile, named, 0.0), axis=1, keepdims=True)
        return jnp.broadcast_to(jnp.sum(rows_of, axis=0, keepdims=True), (rows, LANES))

    counts_ref[0] = count(at_y)
    counts_ref[1] = jnp.where(lane < LANES // 2, count(at_y + 1), count(at_y - 1))
    shape = (layers, 2, rows, LANES)
    row = iota(shape, 2)
    col = iota(shape, 3)
    state_ref[...] = field(0)
    along_rows = field(1)
    edge_ref[0] = along_rows[:, :, 0:1, :]
    edge_ref[1] = along_rows[:, :, rows - 1 :, :]
    fixed_ref[0] = harmonic(along_rows, jnp.where(row == rows - 1, 0.0, pltpu.roll(along_rows, rows - 1, 2)))
    along_cols = field(2)
    rolled = pltpu.roll(along_cols, LANES - 1, 3)
    fixed_ref[1] = harmonic(along_cols, jnp.where(col == LANES - 1, swap(rolled), rolled))
    along_layers = field(3)
    fixed_ref[2, : layers - 1] = harmonic(along_layers[: layers - 1], along_layers[1:])
    fixed_ref[2, layers - 1 :] = jnp.zeros((1, 2, rows, LANES), F32)
    fixed_ref[3] = field(4)
    fixed_ref[4] = field(5)


def first_source(layer_axis, own, state_in, fixed_ref, edge_ref, sensors_ref, state_ref, up_ref, down_ref):
    layers, _, rows, _ = state_ref.shape
    (source,) = sources(layer_axis, own, layers, rows, sensors_ref, (3,))
    state = state_in[...] + source
    state_ref[...] = state
    weighted = fixed_ref[3] * state
    up_ref[0] = weighted[:, :, 0:1, :]
    up_ref[1] = edge_ref[0]
    down_ref[0] = weighted[:, :, rows - 1 :, :]
    down_ref[1] = edge_ref[1]


def other_sources(layer_axis, own, sensors_ref, source_ref):
    _, layers, _, rows, _ = source_ref.shape
    for s, source in enumerate(sources(layer_axis, own, layers, rows, sensors_ref, (0, 1, 2))):
        source_ref[s] = source


def step(axis, turn, *refs):
    first, last = turn == 3, turn == 0
    refs = list(refs)
    counts_ref, state_ref, fixed_ref, above_ref, below_ref = refs[:5]
    refs = refs[5:]
    if first:
        own_up_ref, own_down_ref = refs[:2]
    else:
        row_edge_ref, sens_ref = refs[:2]
    refs = refs[2:]
    if not last:
        source_ref = refs[0]
        refs = refs[1:]
    if first:
        state_out, up_out, down_out, sens_out, edge_out = refs
    elif not last:
        state_out, up_out, down_out, sens_out = refs
    else:
        state_out, sens_out = refs
    at_x, n_x = lax.axis_index(axis), lax.axis_size(axis)
    layers, _, rows, _ = state_ref.shape
    total = fixed_ref.shape[1]
    low = (total - layers) // 2
    span = slice(low, low + layers)
    inner = slice(low + 1, low + layers - 1)
    state = state_ref[...]
    weighted = fixed_ref[3, span] * state
    if first:
        edges = []
        for mine, other, there in ((own_up_ref, above_ref, at_x > 0), (own_down_ref, below_ref, at_x < n_x - 1)):
            edges.append(harmonic(mine[1], jnp.where(there, other[1], 0.0)))
        edge_out[0] = edges[0]
        edge_out[1] = edges[1]
        over, under = edges[0][1:-1], edges[1][1:-1]
    else:
        over, under = row_edge_ref[0, inner], row_edge_ref[1, inner]
    shape = (layers - 2, 2, rows, LANES)
    row, col = iota(shape, 2), iota(shape, 3)
    across = weighted[1:-1]
    halo_over = above_ref[0, 1:-1]
    halo_under = below_ref[0, 1:-1]
    flux = fixed_ref[0, inner] * (pltpu.roll(across, rows - 1, 2) - across)
    edge_low = over * (across[:, :, 0:1, :] - halo_over)
    edge_high = under * (halo_under - across[:, :, rows - 1 :, :])
    flux = jnp.where(row == rows - 1, edge_high, flux)
    change = flux - jnp.where(row == 0, edge_low, pltpu.roll(flux, 1, 2))
    rolled = pltpu.roll(across, LANES - 1, 3)
    flux = fixed_ref[1, inner] * (jnp.where(col == LANES - 1, swap(rolled), rolled) - across)
    rolled = pltpu.roll(flux, 1, 3)
    change = change + (flux - jnp.where(col == 0, swap(rolled), rolled))
    flux = fixed_ref[2, low : low + layers - 1] * (weighted[1:] - weighted[:-1])
    change = change + (flux[1:] - flux[:-1])
    state = state[1:-1] + change
    kept = slice(0, 1) if last else slice(0, 2)
    state = state[:, kept]
    rate = fixed_ref[4, inner, kept]
    counts = counts_ref[kept][None]
    keep_own = 1.0 - 4.0 * rate
    half = rows // 2
    part = state.shape[:2] + (half, LANES)
    row, col = iota(part, 2), iota(part, 3)

    def one_turn(at, now):
        top, low_half = (rate[:, :, h : h + half] * now[:, :, h : h + half] for h in (0, half))
        up = pltpu.roll(top, half - 1, 2), pltpu.roll(low_half, half - 1, 2)
        down = pltpu.roll(top, 1, 2), pltpu.roll(low_half, 1, 2)
        near = (
            jnp.where(row == half - 1, up[1], up[0]) + jnp.where(row == 0, top, down[0]),
            jnp.where(row == half - 1, low_half, up[1]) + jnp.where(row == 0, down[0], down[1]),
        )
        parts = []
        for h, (v, rowwise) in enumerate(zip((top, low_half), near)):
            colwise = jnp.where(col == LANES - 1, v, pltpu.roll(v, LANES - 1, 3)) + jnp.where(col == 0, v, pltpu.roll(v, 1, 3))
            here = slice(h * half, (h + 1) * half)
            after = keep_own[:, :, here] * now[:, :, here] + (rowwise + colwise)
            parts.append(after if at == 0 else jnp.where(counts[:, :, here] > at, after, now[:, :, here]))
        return jnp.concatenate(parts, axis=2)

    for at in range(MAXSUB):
        state = one_turn(at, state)
    own = total // 3
    keep = slice((layers - 2 - own) // 2, (layers - 2 - own) // 2 + own)
    addend = fixed_ref[3, own : 2 * own, 0] * state[keep, 0]
    sens_out[...] = addend if first else sens_ref[...] + addend
    if last:
        state_out[...] = state[:, 0]
        return
    state = state + source_ref[turn - 1, inner]
    state_out[...] = state
    weighted = fixed_ref[3, inner] * state
    up_out[0] = weighted[:, :, 0:1, :]
    down_out[0] = weighted[:, :, rows - 1 :, :]


def shift(cells, axis, by, wrap):
    count = lax.axis_size(axis)
    pairs = [(i, (i + by) % count) for i in range(count) if wrap or 0 <= i + by < count]
    return lax.ppermute(cells, axis, pairs)


def body(adjoint_final, conductivity, step_ratio, refine_rate, residual, sensor_tile, sensor_cell, substeps):
    own, rows, cols = adjoint_final.shape
    layers = 3 * own
    n_y = lax.axis_size("gy")
    tiles = lax.axis_size("gx") * n_y
    listed = sensor_tile.shape[0]
    fields = jnp.concatenate([adjoint_final[None], conductivity, step_ratio[None], refine_rate[None]], axis=0)
    fields, message = call(functools.partial(pack, n_y), [fields.shape, (tiles, LANES)], "pack", aliases={0: 0})(
        fields, residual, sensor_tile.reshape(1, listed), sensor_cell.reshape(1, listed)
    )
    below = shift(fields, "gz", 1, False)
    above = shift(fields, "gz", -1, False)
    sensors = lax.all_to_all(message, ("gx", "gy"), 0, 0, tiled=True)
    packed = (FIELDS * layers // QUART, rows, LANES)
    to_left, to_right = call(pack_columns, [packed, packed], "pack_columns")(below, fields, above)
    from_left = shift(to_right, "gy", 1, False)
    from_right = shift(to_left, "gy", -1, False)
    block = (layers, 2, rows, LANES)
    faces = (2, layers, 2, 1, LANES)
    state, fixed, edges, counts = call(
        functools.partial(prepare, ("gx", "gy")), [block, (5,) + block, faces, (2, rows, LANES)], "prepare"
    )(substeps.T, below, fields, above, from_left, from_right)
    state, up, down = call(functools.partial(first_source, "gz", own), [block, faces, faces], "first_source")(state, fixed, edges, sensors)
    (source,) = call(functools.partial(other_sources, "gz", own), [(3,) + block], "other_sources")(sensors)
    sens = edge = None
    for turn in range(3, -1, -1):
        over = shift(down, "gx", 1, True)
        under = shift(up, "gx", -1, True)
        depth = state.shape[0] - 2
        args = [counts, state, fixed]
        args += [over, under] + ([up, down] if turn == 3 else [edge, sens])
        if turn > 0:
            args += [source]
        face = (1, depth, 2, 1, LANES)
        if turn == 0:
            outs = [(own, rows, cols), (own, rows, cols)]
        else:
            outs = [(depth, 2, rows, LANES), face, face, (own, rows, cols)]
            if turn == 3:
                outs += [(2, layers, 2, 1, LANES)]
        got = call(functools.partial(step, "gx", turn), outs, "step")(*args)
        if turn == 3:
            state, up, down, sens, edge = got
        elif turn > 0:
            state, up, down, sens = got
        else:
            return tuple(got)


def solution(mesh):
    return jax.shard_map(
        body,
        mesh=mesh,
        in_specs=(
            P("gz", "gx", "gy"),
            P(None, "gz", "gx", "gy"),
            P("gz", "gx", "gy"),
            P("gz", "gx", "gy"),
            P(None, ("gx", "gy")),
            P(("gx", "gy")),
            P(("gx", "gy")),
            P(),
        ),
        out_specs=(P("gz", "gx", "gy"), P("gz", "gx", "gy")),
        check_vma=False,
    )
```

```python
import functools

import jax
import jax.numpy as jnp
from jax import lax
from jax.experimental import pallas as pl
from jax.experimental.pallas import tpu as pltpu
from jax.sharding import PartitionSpec as P


F32 = jnp.float32
BF16 = jnp.bfloat16
LANES = 128
WIDE = 32
QUART = LANES // WIDE
MAXSUB = 6
SLOTS = 4
FIELDS = 6
TINY = 1e-30
LIMIT = 24 * 2**20


def iota(shape, dim):
    return lax.broadcasted_iota(jnp.int32, shape, dim)


def harmonic(first, second):
    return 2.0 * first * second / jnp.maximum(first + second, TINY)


def swap(field):
    return jnp.concatenate([field[:, 1:2], field[:, 0:1]], axis=1)


def call(kernel, outs, cost=20000):
    vmem = pl.BlockSpec(memory_space=pltpu.VMEM)

    def run(*args):
        return pl.pallas_call(
            kernel,
            out_shape=[jax.ShapeDtypeStruct(o, F32) for o in outs],
            in_specs=[vmem] * len(args),
            out_specs=[vmem] * len(outs),
            compiler_params=pltpu.CompilerParams(vmem_limit_bytes=LIMIT),
            cost_estimate=pl.CostEstimate(flops=cost, bytes_accessed=cost, transcendentals=0),
        )(*args)

    return run


def pack(gy, residual_ref, tile_ref, cell_ref, out_ref):
    count = residual_ref.shape[1]
    tiles = out_ref.shape[0]
    eye = iota((count, count), 0) == iota((count, count), 1)

    def column(row):
        return jnp.sum(jnp.where(eye, jnp.broadcast_to(row, (count, count)), 0.0), axis=1, keepdims=True)

    named = tile_ref[...]
    tile_row = named.astype(F32)
    tile_col = column(tile_row)
    same = (tile_col == tile_row) & (iota((count, count), 1) < iota((count, count), 0))
    rank = jnp.sum(same.astype(F32), axis=1, keepdims=True).astype(jnp.int32)
    values = [column(residual_ref[s : s + 1, :]) for s in range(4)]
    values.append(column(cell_ref[...].astype(F32) + 1.0))
    lane = iota((count, LANES), 1)
    within = lane % 8
    spread = jnp.zeros((count, LANES), F32)
    for place, value in enumerate(values):
        spread = jnp.where(within == place, value, spread)
    spread = jnp.where((lane % 32) // 8 == rank, spread, 0.0)
    tile_at = iota((tiles, count), 0)
    total = jnp.zeros((tiles, LANES), F32)
    for group, (step, edge) in enumerate(((0, -1), (-1, 0), (1, gy - 1))):
        hit = (named == tile_at + step) & (tile_at % gy != edge)
        part = jnp.where(lane // 32 == group, spread, 0.0)
        total = total + jnp.dot(hit.astype(F32), part, precision=lax.Precision.HIGHEST, preferred_element_type=F32)
    out_ref[...] = total


def stacked(refs, field, layer):
    each = refs[0].shape[1]
    return refs[layer // each][field, layer % each]


def pack_columns(below_ref, own_ref, above_ref, left_ref, right_ref):
    refs = (below_ref, own_ref, above_ref)
    layers = 3 * own_ref.shape[1]
    rows = own_ref.shape[2]
    quarter = iota((rows, LANES), 1) // WIDE
    for j in range(FIELDS * layers // QUART):
        left = right = None
        for q in range(QUART):
            p = j * QUART + q
            plane = stacked(refs, p // layers, p % layers)
            to_left = plane if q == 0 else pltpu.roll(plane, WIDE * q, 1)
            shift = (WIDE * q + WIDE) % LANES
            to_right = plane if shift == 0 else pltpu.roll(plane, shift, 1)
            left = to_left if q == 0 else jnp.where(quarter == q, to_left, left)
            right = to_right if q == 0 else jnp.where(quarter == q, to_right, right)
        left_ref[j] = left
        right_ref[j] = right


def spread_column(columns, at, shape):
    return jnp.broadcast_to(columns[:, at : at + 1], shape)


def sources(layer_axis, own, layers, rows, sensors_ref, steps):
    got = sensors_ref[...]
    blocks = got.shape[0]
    lane = iota((blocks, LANES), 1)
    lane_at = lane.astype(F32)
    cell = got.astype(jnp.int32) - 1
    row_base = (lax.axis_index(layer_axis) * own - own) * rows
    cell_row = ((cell >> 7) - row_base).astype(F32).T
    cell_col = cell & (LANES - 1)
    half = LANES // 2
    group_of = lane // 32
    cell_col = jnp.where(
        group_of == 0,
        cell_col,
        jnp.where(
            group_of == 1,
            jnp.where(cell_col >= LANES - WIDE, cell_col - half, -LANES),
            jnp.where(cell_col < WIDE, cell_col, -LANES),
        ),
    ).astype(F32)
    row_at = iota((layers * rows, blocks), 0).astype(F32)
    high = got.astype(BF16)
    values = (high, (got - high.astype(F32)).astype(BF16))
    onehots, tables = ([], []), ([], [])
    for group in range(3):
        for slot in range(SLOTS):
            base = group * 32 + slot * 8
            onehots[group > 0].append((cell_row[base + 4 : base + 5, :] == row_at).astype(F32).astype(BF16))
            at = spread_column(cell_col, base + 4, lane.shape)
            pairs = (0, half) if group > 0 and len(steps) > 1 else (0,)
            place = [(at == lane_at - by).astype(F32).astype(BF16) for by in pairs]
            line = []
            for part in range(2):
                cells = [spread_column(values[part], base + s, lane.shape) for s in steps]
                for k in range(0, len(cells), len(place)):
                    line.append(functools.reduce(jnp.add, [m * v for m, v in zip(place, cells[k : k + len(place)])]))
            tables[group > 0].append(jnp.concatenate(line, axis=1))
    sums = []
    for onehot, table in zip(onehots, tables):
        both = jnp.dot(jnp.concatenate(onehot, axis=1), jnp.concatenate(table, axis=0), preferred_element_type=F32)
        width = both.shape[1] // 2
        sums.append(both[:, :width] + both[:, width:])
    centre, side = sums
    lane = iota((layers * rows, LANES), 1)
    out = []
    for s in range(len(steps)):
        tile = side[:, (s // 2) * LANES : (s // 2 + 1) * LANES]
        turned = pltpu.roll(tile, half, 1)
        right, left = (tile, turned) if s % 2 == 0 else (turned, tile)
        beside = jnp.where(lane < WIDE, right, jnp.where(lane >= LANES - WIDE, left, 0.0))
        parts = [m.reshape(layers, 1, rows, LANES) for m in (centre[:, s * LANES : (s + 1) * LANES], beside)]
        out.append(jnp.concatenate(parts, axis=1))
    return out


def prepare(axes, substeps_ref, below_ref, own_ref, above_ref, left_ref, right_ref, state_ref, fixed_ref, edge_ref, counts_ref):
    refs = (below_ref, own_ref, above_ref)
    own = own_ref.shape[1]
    layers = 3 * own
    rows = own_ref.shape[2]
    lane = iota((rows, LANES), 1)

    def field(f):
        planes = []
        for l in range(layers):
            p = f * layers + l
            j, q = p // QUART, p % QUART
            from_left = pltpu.roll(left_ref[j], (LANES - WIDE - WIDE * q) % LANES, 1) if q != QUART - 1 else left_ref[j]
            from_right = pltpu.roll(right_ref[j], LANES - WIDE * q, 1) if q != 0 else right_ref[j]
            side = jnp.where(lane < WIDE, from_right, jnp.where(lane >= LANES - WIDE, from_left, 0.0))
            planes.append(jnp.stack([stacked(refs, f, l), side], axis=0))
        return jnp.stack(planes, axis=0)

    at_x, at_y = (lax.axis_index(axis) for axis in axes)
    n_y, n_x = substeps_ref.shape
    named = jnp.where(iota((n_y, n_x), 1) == at_x, substeps_ref[...].astype(F32), 0.0)

    def count(tile):
        rows_of = jnp.sum(jnp.where(iota((n_y, n_x), 0) == tile, named, 0.0), axis=1, keepdims=True)
        return jnp.broadcast_to(jnp.sum(rows_of, axis=0, keepdims=True), (rows, LANES))

    counts_ref[0] = count(at_y)
    counts_ref[1] = jnp.where(lane < LANES // 2, count(at_y + 1), count(at_y - 1))
    shape = (layers, 2, rows, LANES)
    row = iota(shape, 2)
    col = iota(shape, 3)
    state_ref[...] = field(0)
    along_rows = field(1)
    edge_ref[0] = along_rows[:, :, 0:1, :]
    edge_ref[1] = along_rows[:, :, rows - 1 :, :]
    fixed_ref[0] = harmonic(along_rows, jnp.where(row == rows - 1, 0.0, pltpu.roll(along_rows, rows - 1, 2)))
    along_cols = field(2)
    rolled = pltpu.roll(along_cols, LANES - 1, 3)
    fixed_ref[1] = harmonic(along_cols, jnp.where(col == LANES - 1, swap(rolled), rolled))
    along_layers = field(3)
    fixed_ref[2, : layers - 1] = harmonic(along_layers[: layers - 1], along_layers[1:])
    fixed_ref[2, layers - 1 :] = jnp.zeros((1, 2, rows, LANES), F32)
    fixed_ref[3] = field(4)
    fixed_ref[4] = field(5)


def first_source(layer_axis, own, state_in, fixed_ref, edge_ref, sensors_ref, state_ref, up_ref, down_ref):
    layers, _, rows, _ = state_ref.shape
    (source,) = sources(layer_axis, own, layers, rows, sensors_ref, (3,))
    state = state_in[...] + source
    state_ref[...] = state
    weighted = fixed_ref[3] * state
    up_ref[0] = weighted[:, :, 0:1, :]
    up_ref[1] = edge_ref[0]
    down_ref[0] = weighted[:, :, rows - 1 :, :]
    down_ref[1] = edge_ref[1]


def other_sources(layer_axis, own, sensors_ref, source_ref):
    _, layers, _, rows, _ = source_ref.shape
    for s, source in enumerate(sources(layer_axis, own, layers, rows, sensors_ref, (0, 1, 2))):
        source_ref[s] = source


def step(axis, turn, *refs):
    first, last = turn == 3, turn == 0
    refs = list(refs)
    counts_ref, state_ref, fixed_ref, above_ref, below_ref = refs[:5]
    refs = refs[5:]
    if first:
        own_up_ref, own_down_ref = refs[:2]
    else:
        row_edge_ref, sens_ref = refs[:2]
    refs = refs[2:]
    if not last:
        source_ref = refs[0]
        refs = refs[1:]
    if first:
        state_out, up_out, down_out, sens_out, edge_out = refs
    elif not last:
        state_out, up_out, down_out, sens_out = refs
    else:
        state_out, sens_out = refs
    at_x, n_x = lax.axis_index(axis), lax.axis_size(axis)
    layers, _, rows, _ = state_ref.shape
    total = fixed_ref.shape[1]
    low = (total - layers) // 2
    span = slice(low, low + layers)
    inner = slice(low + 1, low + layers - 1)
    state = state_ref[...]
    weighted = fixed_ref[3, span] * state
    if first:
        edges = []
        for mine, other, there in ((own_up_ref, above_ref, at_x > 0), (own_down_ref, below_ref, at_x < n_x - 1)):
            edges.append(harmonic(mine[1], jnp.where(there, other[1], 0.0)))
        edge_out[0] = edges[0]
        edge_out[1] = edges[1]
        over, under = edges[0][1:-1], edges[1][1:-1]
    else:
        over, under = row_edge_ref[0, inner], row_edge_ref[1, inner]
    shape = (layers - 2, 2, rows, LANES)
    row, col = iota(shape, 2), iota(shape, 3)
    across = weighted[1:-1]
    halo_over = above_ref[0, 1:-1]
    halo_under = below_ref[0, 1:-1]
    flux = fixed_ref[0, inner] * (pltpu.roll(across, rows - 1, 2) - across)
    edge_low = over * (across[:, :, 0:1, :] - halo_over)
    edge_high = under * (halo_under - across[:, :, rows - 1 :, :])
    flux = jnp.where(row == rows - 1, edge_high, flux)
    change = flux - jnp.where(row == 0, edge_low, pltpu.roll(flux, 1, 2))
    rolled = pltpu.roll(across, LANES - 1, 3)
    flux = fixed_ref[1, inner] * (jnp.where(col == LANES - 1, swap(rolled), rolled) - across)
    rolled = pltpu.roll(flux, 1, 3)
    change = change + (flux - jnp.where(col == 0, swap(rolled), rolled))
    flux = fixed_ref[2, low : low + layers - 1] * (weighted[1:] - weighted[:-1])
    change = change + (flux[1:] - flux[:-1])
    state = state[1:-1] + change
    kept = slice(0, 1) if last else slice(0, 2)
    state = state[:, kept]
    rate = fixed_ref[4, inner, kept]
    counts = counts_ref[kept][None]
    keep_own = 1.0 - 4.0 * rate
    half = rows // 2
    part = state.shape[:2] + (half, LANES)
    row, col = iota(part, 2), iota(part, 3)

    def one_turn(at, now):
        top, low_half = (rate[:, :, h : h + half] * now[:, :, h : h + half] for h in (0, half))
        up = pltpu.roll(top, half - 1, 2), pltpu.roll(low_half, half - 1, 2)
        down = pltpu.roll(top, 1, 2), pltpu.roll(low_half, 1, 2)
        near = (
            jnp.where(row == half - 1, up[1], up[0]) + jnp.where(row == 0, top, down[0]),
            jnp.where(row == half - 1, low_half, up[1]) + jnp.where(row == 0, down[0], down[1]),
        )
        parts = []
        for h, (v, rowwise) in enumerate(zip((top, low_half), near)):
            colwise = jnp.where(col == LANES - 1, v, pltpu.roll(v, LANES - 1, 3)) + jnp.where(col == 0, v, pltpu.roll(v, 1, 3))
            here = slice(h * half, (h + 1) * half)
            after = keep_own[:, :, here] * now[:, :, here] + (rowwise + colwise)
            parts.append(after if at == 0 else jnp.where(counts[:, :, here] > at, after, now[:, :, here]))
        return jnp.concatenate(parts, axis=2)

    for at in range(MAXSUB):
        state = one_turn(at, state)
    own = total // 3
    keep = slice((layers - 2 - own) // 2, (layers - 2 - own) // 2 + own)
    addend = fixed_ref[3, own : 2 * own, 0] * state[keep, 0]
    sens_out[...] = addend if first else sens_ref[...] + addend
    if last:
        state_out[...] = state[:, 0]
        return
    state = state + source_ref[turn - 1, inner]
    state_out[...] = state
    weighted = fixed_ref[3, inner] * state
    up_out[0] = weighted[:, :, 0:1, :]
    down_out[0] = weighted[:, :, rows - 1 :, :]


def shift(cells, axis, by, wrap):
    count = lax.axis_size(axis)
    pairs = [(i, (i + by) % count) for i in range(count) if wrap or 0 <= i + by < count]
    return lax.ppermute(cells, axis, pairs)


def body(adjoint_final, conductivity, step_ratio, refine_rate, residual, sensor_tile, sensor_cell, substeps):
    own, rows, cols = adjoint_final.shape
    layers = 3 * own
    n_y = lax.axis_size("gy")
    tiles = lax.axis_size("gx") * n_y
    listed = sensor_tile.shape[0]
    (message,) = call(functools.partial(pack, n_y), [(tiles, LANES)])(
        residual, sensor_tile.reshape(1, listed), sensor_cell.reshape(1, listed)
    )
    sensors = lax.all_to_all(message, ("gx", "gy"), 0, 0, tiled=True)
    fields = jnp.concatenate([adjoint_final[None], conductivity, step_ratio[None], refine_rate[None]], axis=0)
    below = shift(fields, "gz", 1, False)
    above = shift(fields, "gz", -1, False)
    packed = (FIELDS * layers // QUART, rows, LANES)
    to_left, to_right = call(pack_columns, [packed, packed])(below, fields, above)
    from_left = shift(to_right, "gy", 1, False)
    from_right = shift(to_left, "gy", -1, False)
    block = (layers, 2, rows, LANES)
    faces = (2, layers, 2, 1, LANES)
    state, fixed, edges, counts = call(
        functools.partial(prepare, ("gx", "gy")), [block, (5,) + block, faces, (2, rows, LANES)]
    )(substeps.T, below, fields, above, from_left, from_right)
    state, up, down = call(functools.partial(first_source, "gz", own), [block, faces, faces])(state, fixed, edges, sensors)
    (source,) = call(functools.partial(other_sources, "gz", own), [(3,) + block])(sensors)
    sens = edge = None
    for turn in range(3, -1, -1):
        over = shift(down, "gx", 1, True)
        under = shift(up, "gx", -1, True)
        depth = state.shape[0] - 2
        args = [counts, state, fixed]
        args += [over, under] + ([up, down] if turn == 3 else [edge, sens])
        if turn > 0:
            args += [source]
        face = (1, depth, 2, 1, LANES)
        if turn == 0:
            outs = [(own, rows, cols), (own, rows, cols)]
        else:
            outs = [(depth, 2, rows, LANES), face, face, (own, rows, cols)]
            if turn == 3:
                outs += [(2, layers, 2, 1, LANES)]
        got = call(functools.partial(step, "gx", turn), outs)(*args)
        if turn == 3:
            state, up, down, sens, edge = got
        elif turn > 0:
            state, up, down, sens = got
        else:
            return tuple(got)


def solution(mesh):
    return jax.shard_map(
        body,
        mesh=mesh,
        in_specs=(
            P("gz", "gx", "gy"),
            P(None, "gz", "gx", "gy"),
            P("gz", "gx", "gy"),
            P("gz", "gx", "gy"),
            P(None, ("gx", "gy")),
            P(("gx", "gy")),
            P(("gx", "gy")),
            P(),
        ),
        out_specs=(P("gz", "gx", "gy"), P("gz", "gx", "gy")),
        check_vma=False,
    )
```

```python
import functools

import jax
import jax.numpy as jnp
from jax import lax
from jax.experimental import pallas as pl
from jax.experimental.pallas import tpu as pltpu
from jax.sharding import PartitionSpec as P


F32 = jnp.float32
BF16 = jnp.bfloat16
LANES = 128
WIDE = 24
PIECES = LANES // WIDE
MAXSUB = 6
SLOTS = 4
FIELDS = 6
TINY = 1e-30
LIMIT = 24 * 2**20


def iota(shape, dim):
    return lax.broadcasted_iota(jnp.int32, shape, dim)


def harmonic(first, second):
    return 2.0 * first * second / jnp.maximum(first + second, TINY)


def swap(field):
    return jnp.concatenate([field[:, 1:2], field[:, 0:1]], axis=1)


def call(kernel, outs, cost=20000):
    vmem = pl.BlockSpec(memory_space=pltpu.VMEM)

    def run(*args):
        return pl.pallas_call(
            kernel,
            out_shape=[jax.ShapeDtypeStruct(o, F32) for o in outs],
            in_specs=[vmem] * len(args),
            out_specs=[vmem] * len(outs),
            compiler_params=pltpu.CompilerParams(vmem_limit_bytes=LIMIT),
            cost_estimate=pl.CostEstimate(flops=cost, bytes_accessed=cost, transcendentals=0),
        )(*args)

    return run


def pack(gy, residual_ref, tile_ref, cell_ref, out_ref):
    count = residual_ref.shape[1]
    tiles = out_ref.shape[0]
    eye = iota((count, count), 0) == iota((count, count), 1)

    def column(row):
        return jnp.sum(jnp.where(eye, jnp.broadcast_to(row, (count, count)), 0.0), axis=1, keepdims=True)

    named = tile_ref[...]
    tile_row = named.astype(F32)
    tile_col = column(tile_row)
    same = (tile_col == tile_row) & (iota((count, count), 1) < iota((count, count), 0))
    rank = jnp.sum(same.astype(F32), axis=1, keepdims=True).astype(jnp.int32)
    values = [column(residual_ref[s : s + 1, :]) for s in range(4)]
    values.append(column(cell_ref[...].astype(F32) + 1.0))
    lane = iota((count, LANES), 1)
    within = lane % 8
    spread = jnp.zeros((count, LANES), F32)
    for place, value in enumerate(values):
        spread = jnp.where(within == place, value, spread)
    spread = jnp.where((lane % 32) // 8 == rank, spread, 0.0)
    tile_at = iota((tiles, count), 0)
    total = jnp.zeros((tiles, LANES), F32)
    for group, (step, edge) in enumerate(((0, -1), (-1, 0), (1, gy - 1))):
        hit = (named == tile_at + step) & (tile_at % gy != edge)
        part = jnp.where(lane // 32 == group, spread, 0.0)
        total = total + jnp.dot(hit.astype(F32), part, precision=lax.Precision.HIGHEST, preferred_element_type=F32)
    out_ref[...] = total


def needed(layers):
    return [(f, l) for f in range(FIELDS) for l in range(layers) if f in (0, 3, 4) or 0 < l < layers - 1]


def stacked(refs, field, layer):
    each = refs[0].shape[1]
    return refs[layer // each][field, layer % each]


def pack_columns(below_ref, own_ref, above_ref, left_ref, right_ref):
    refs = (below_ref, own_ref, above_ref)
    layers = 3 * own_ref.shape[1]
    rows = own_ref.shape[2]
    piece = iota((rows, LANES), 1) // WIDE
    planes = needed(layers)
    for j in range(left_ref.shape[0]):
        left = right = None
        for q, (f, l) in enumerate(planes[j * PIECES : (j + 1) * PIECES]):
            plane = stacked(refs, f, l)
            to_left = plane if q == 0 else pltpu.roll(plane, WIDE * q, 1)
            to_right = pltpu.roll(plane, WIDE * q + WIDE, 1)
            left = to_left if q == 0 else jnp.where(piece == q, to_left, left)
            right = to_right if q == 0 else jnp.where(piece == q, to_right, right)
        left_ref[j] = left
        right_ref[j] = right


def spread_column(columns, at, shape):
    return jnp.broadcast_to(columns[:, at : at + 1], shape)


def sources(layer_axis, own, layers, rows, sensors_ref, steps):
    got = sensors_ref[...]
    blocks = got.shape[0]
    lane = iota((blocks, LANES), 1)
    lane_at = lane.astype(F32)
    cell = got.astype(jnp.int32) - 1
    row_base = (lax.axis_index(layer_axis) * own - own) * rows
    cell_row = ((cell >> 7) - row_base).astype(F32).T
    cell_col = cell & (LANES - 1)
    half = LANES // 2
    group_of = lane // 32
    cell_col = jnp.where(
        group_of == 0,
        cell_col,
        jnp.where(
            group_of == 1,
            jnp.where(cell_col >= LANES - WIDE, cell_col - half, -LANES),
            jnp.where(cell_col < WIDE, cell_col, -LANES),
        ),
    ).astype(F32)
    row_at = iota((layers * rows, blocks), 0).astype(F32)
    high = got.astype(BF16)
    values = (high, (got - high.astype(F32)).astype(BF16))
    onehots, tables = ([], []), ([], [])
    for group in range(3):
        for slot in range(SLOTS):
            base = group * 32 + slot * 8
            onehots[group > 0].append((cell_row[base + 4 : base + 5, :] == row_at).astype(F32).astype(BF16))
            at = spread_column(cell_col, base + 4, lane.shape)
            pairs = (0, half) if group > 0 and len(steps) > 1 else (0,)
            place = [(at == lane_at - by).astype(F32).astype(BF16) for by in pairs]
            line = []
            for part in range(2):
                cells = [spread_column(values[part], base + s, lane.shape) for s in steps]
                for k in range(0, len(cells), len(place)):
                    line.append(functools.reduce(jnp.add, [m * v for m, v in zip(place, cells[k : k + len(place)])]))
            tables[group > 0].append(jnp.concatenate(line, axis=1))
    sums = []
    for onehot, table in zip(onehots, tables):
        both = jnp.dot(jnp.concatenate(onehot, axis=1), jnp.concatenate(table, axis=0), preferred_element_type=F32)
        width = both.shape[1] // 2
        sums.append(both[:, :width] + both[:, width:])
    centre, side = sums
    lane = iota((layers * rows, LANES), 1)
    out = []
    for s in range(len(steps)):
        tile = side[:, (s // 2) * LANES : (s // 2 + 1) * LANES]
        turned = pltpu.roll(tile, half, 1)
        right, left = (tile, turned) if s % 2 == 0 else (turned, tile)
        beside = jnp.where(lane < WIDE, right, jnp.where(lane >= LANES - WIDE, left, 0.0))
        parts = [m.reshape(layers, 1, rows, LANES) for m in (centre[:, s * LANES : (s + 1) * LANES], beside)]
        out.append(jnp.concatenate(parts, axis=1))
    return out


def prepare(axes, substeps_ref, below_ref, own_ref, above_ref, left_ref, right_ref, state_ref, fixed_ref, edge_ref, counts_ref):
    refs = (below_ref, own_ref, above_ref)
    own = own_ref.shape[1]
    layers = 3 * own
    rows = own_ref.shape[2]
    lane = iota((rows, LANES), 1)

    listed = {plane: at for at, plane in enumerate(needed(layers))}

    def field(f):
        planes = []
        for l in range(layers):
            if (f, l) in listed:
                j, q = divmod(listed[f, l], PIECES)
                from_left = pltpu.roll(left_ref[j], (LANES - WIDE - WIDE * q) % LANES, 1)
                from_right = pltpu.roll(right_ref[j], LANES - WIDE * q, 1) if q != 0 else right_ref[j]
                side = jnp.where(lane < WIDE, from_right, jnp.where(lane >= LANES - WIDE, from_left, 0.0))
            else:
                side = jnp.zeros((rows, LANES), F32)
            planes.append(jnp.stack([stacked(refs, f, l), side], axis=0))
        return jnp.stack(planes, axis=0)

    at_x, at_y = (lax.axis_index(axis) for axis in axes)
    n_y, n_x = substeps_ref.shape
    named = jnp.where(iota((n_y, n_x), 1) == at_x, substeps_ref[...].astype(F32), 0.0)

    def count(tile):
        rows_of = jnp.sum(jnp.where(iota((n_y, n_x), 0) == tile, named, 0.0), axis=1, keepdims=True)
        return jnp.broadcast_to(jnp.sum(rows_of, axis=0, keepdims=True), (rows, LANES))

    counts_ref[0] = count(at_y)
    counts_ref[1] = jnp.where(lane < LANES // 2, count(at_y + 1), count(at_y - 1))
    shape = (layers, 2, rows, LANES)
    row = iota(shape, 2)
    col = iota(shape, 3)
    state_ref[...] = field(0)
    along_rows = field(1)
    edge_ref[0] = along_rows[:, :, 0:1, :]
    edge_ref[1] = along_rows[:, :, rows - 1 :, :]
    fixed_ref[0] = harmonic(along_rows, jnp.where(row == rows - 1, 0.0, pltpu.roll(along_rows, rows - 1, 2)))
    along_cols = field(2)
    rolled = pltpu.roll(along_cols, LANES - 1, 3)
    fixed_ref[1] = harmonic(along_cols, jnp.where(col == LANES - 1, swap(rolled), rolled))
    along_layers = field(3)
    fixed_ref[2, : layers - 1] = harmonic(along_layers[: layers - 1], along_layers[1:])
    fixed_ref[2, layers - 1 :] = jnp.zeros((1, 2, rows, LANES), F32)
    fixed_ref[3] = field(4)
    fixed_ref[4] = field(5)


def first_source(layer_axis, own, state_in, fixed_ref, edge_ref, sensors_ref, state_ref, up_ref, down_ref):
    layers, _, rows, _ = state_ref.shape
    (source,) = sources(layer_axis, own, layers, rows, sensors_ref, (3,))
    state = state_in[...] + source
    state_ref[...] = state
    weighted = fixed_ref[3] * state
    up_ref[0] = weighted[:, :, 0:1, :]
    up_ref[1] = edge_ref[0]
    down_ref[0] = weighted[:, :, rows - 1 :, :]
    down_ref[1] = edge_ref[1]


def other_sources(layer_axis, own, sensors_ref, source_ref):
    _, layers, _, rows, _ = source_ref.shape
    for s, source in enumerate(sources(layer_axis, own, layers, rows, sensors_ref, (0, 1, 2))):
        source_ref[s] = source


def step(axis, turn, *refs):
    first, last = turn == 3, turn == 0
    refs = list(refs)
    counts_ref, state_ref, fixed_ref, above_ref, below_ref = refs[:5]
    refs = refs[5:]
    if first:
        own_up_ref, own_down_ref = refs[:2]
    else:
        row_edge_ref, sens_ref = refs[:2]
    refs = refs[2:]
    if not last:
        source_ref = refs[0]
        refs = refs[1:]
    if first:
        state_out, up_out, down_out, sens_out, edge_out = refs
    elif not last:
        state_out, up_out, down_out, sens_out = refs
    else:
        state_out, sens_out = refs
    at_x, n_x = lax.axis_index(axis), lax.axis_size(axis)
    layers, _, rows, _ = state_ref.shape
    total = fixed_ref.shape[1]
    low = (total - layers) // 2
    span = slice(low, low + layers)
    inner = slice(low + 1, low + layers - 1)
    state = state_ref[...]
    weighted = fixed_ref[3, span] * state
    if first:
        edges = []
        for mine, other, there in ((own_up_ref, above_ref, at_x > 0), (own_down_ref, below_ref, at_x < n_x - 1)):
            edges.append(harmonic(mine[1], jnp.where(there, other[1], 0.0)))
        edge_out[0] = edges[0]
        edge_out[1] = edges[1]
        over, under = edges[0][1:-1], edges[1][1:-1]
    else:
        over, under = row_edge_ref[0, inner], row_edge_ref[1, inner]
    shape = (layers - 2, 2, rows, LANES)
    row, col = iota(shape, 2), iota(shape, 3)
    across = weighted[1:-1]
    halo_over = above_ref[0, 1:-1]
    halo_under = below_ref[0, 1:-1]
    flux = fixed_ref[0, inner] * (pltpu.roll(across, rows - 1, 2) - across)
    edge_low = over * (across[:, :, 0:1, :] - halo_over)
    edge_high = under * (halo_under - across[:, :, rows - 1 :, :])
    flux = jnp.where(row == rows - 1, edge_high, flux)
    change = flux - jnp.where(row == 0, edge_low, pltpu.roll(flux, 1, 2))
    rolled = pltpu.roll(across, LANES - 1, 3)
    flux = fixed_ref[1, inner] * (jnp.where(col == LANES - 1, swap(rolled), rolled) - across)
    rolled = pltpu.roll(flux, 1, 3)
    change = change + (flux - jnp.where(col == 0, swap(rolled), rolled))
    flux = fixed_ref[2, low : low + layers - 1] * (weighted[1:] - weighted[:-1])
    change = change + (flux[1:] - flux[:-1])
    state = state[1:-1] + change
    kept = slice(0, 1) if last else slice(0, 2)
    state = state[:, kept]
    rate = fixed_ref[4, inner, kept]
    counts = counts_ref[kept][None]
    keep_own = 1.0 - 4.0 * rate
    half = rows // 2
    part = state.shape[:2] + (half, LANES)
    row, col = iota(part, 2), iota(part, 3)

    def one_turn(at, now):
        top, low_half = (rate[:, :, h : h + half] * now[:, :, h : h + half] for h in (0, half))
        up = pltpu.roll(top, half - 1, 2), pltpu.roll(low_half, half - 1, 2)
        down = pltpu.roll(top, 1, 2), pltpu.roll(low_half, 1, 2)
        near = (
            jnp.where(row == half - 1, up[1], up[0]) + jnp.where(row == 0, top, down[0]),
            jnp.where(row == half - 1, low_half, up[1]) + jnp.where(row == 0, down[0], down[1]),
        )
        parts = []
        for h, (v, rowwise) in enumerate(zip((top, low_half), near)):
            colwise = jnp.where(col == LANES - 1, v, pltpu.roll(v, LANES - 1, 3)) + jnp.where(col == 0, v, pltpu.roll(v, 1, 3))
            here = slice(h * half, (h + 1) * half)
            after = keep_own[:, :, here] * now[:, :, here] + (rowwise + colwise)
            parts.append(after if at == 0 else jnp.where(counts[:, :, here] > at, after, now[:, :, here]))
        return jnp.concatenate(parts, axis=2)

    for at in range(MAXSUB):
        state = one_turn(at, state)
    own = total // 3
    keep = slice((layers - 2 - own) // 2, (layers - 2 - own) // 2 + own)
    addend = fixed_ref[3, own : 2 * own, 0] * state[keep, 0]
    sens_out[...] = addend if first else sens_ref[...] + addend
    if last:
        state_out[...] = state[:, 0]
        return
    state = state + source_ref[turn - 1, inner]
    state_out[...] = state
    weighted = fixed_ref[3, inner] * state
    up_out[0] = weighted[:, :, 0:1, :]
    down_out[0] = weighted[:, :, rows - 1 :, :]


def shift(cells, axis, by, wrap):
    count = lax.axis_size(axis)
    pairs = [(i, (i + by) % count) for i in range(count) if wrap or 0 <= i + by < count]
    return lax.ppermute(cells, axis, pairs)


def body(adjoint_final, conductivity, step_ratio, refine_rate, residual, sensor_tile, sensor_cell, substeps):
    own, rows, cols = adjoint_final.shape
    layers = 3 * own
    n_y = lax.axis_size("gy")
    tiles = lax.axis_size("gx") * n_y
    listed = sensor_tile.shape[0]
    (message,) = call(functools.partial(pack, n_y), [(tiles, LANES)])(
        residual, sensor_tile.reshape(1, listed), sensor_cell.reshape(1, listed)
    )
    sensors = lax.all_to_all(message, ("gx", "gy"), 0, 0, tiled=True)
    fields = jnp.concatenate([adjoint_final[None], conductivity, step_ratio[None], refine_rate[None]], axis=0)
    below = shift(fields, "gz", 1, False)
    above = shift(fields, "gz", -1, False)
    packed = (pl.cdiv(len(needed(layers)), PIECES), rows, LANES)
    to_left, to_right = call(pack_columns, [packed, packed])(below, fields, above)
    from_left = shift(to_right, "gy", 1, False)
    from_right = shift(to_left, "gy", -1, False)
    block = (layers, 2, rows, LANES)
    faces = (2, layers, 2, 1, LANES)
    state, fixed, edges, counts = call(
        functools.partial(prepare, ("gx", "gy")), [block, (5,) + block, faces, (2, rows, LANES)]
    )(substeps.T, below, fields, above, from_left, from_right)
    state, up, down = call(functools.partial(first_source, "gz", own), [block, faces, faces])(state, fixed, edges, sensors)
    (source,) = call(functools.partial(other_sources, "gz", own), [(3,) + block])(sensors)
    sens = edge = None
    for turn in range(3, -1, -1):
        over = shift(down, "gx", 1, True)
        under = shift(up, "gx", -1, True)
        depth = state.shape[0] - 2
        args = [counts, state, fixed]
        args += [over, under] + ([up, down] if turn == 3 else [edge, sens])
        if turn > 0:
            args += [source]
        face = (1, depth, 2, 1, LANES)
        if turn == 0:
            outs = [(own, rows, cols), (own, rows, cols)]
        else:
            outs = [(depth, 2, rows, LANES), face, face, (own, rows, cols)]
            if turn == 3:
                outs += [(2, layers, 2, 1, LANES)]
        got = call(functools.partial(step, "gx", turn), outs)(*args)
        if turn == 3:
            state, up, down, sens, edge = got
        elif turn > 0:
            state, up, down, sens = got
        else:
            return tuple(got)


def solution(mesh):
    return jax.shard_map(
        body,
        mesh=mesh,
        in_specs=(
            P("gz", "gx", "gy"),
            P(None, "gz", "gx", "gy"),
            P("gz", "gx", "gy"),
            P("gz", "gx", "gy"),
            P(None, ("gx", "gy")),
            P(("gx", "gy")),
            P(("gx", "gy")),
            P(),
        ),
        out_specs=(P("gz", "gx", "gy"), P("gz", "gx", "gy")),
        check_vma=False,
    )
```

```python
import functools

import jax
import jax.numpy as jnp
from jax import lax
from jax.experimental import pallas as pl
from jax.experimental.pallas import tpu as pltpu
from jax.sharding import PartitionSpec as P


F32 = jnp.float32
BF16 = jnp.bfloat16
LANES = 128
WIDE = 24
PIECES = LANES // WIDE
MAXSUB = 6
SLOTS = 4
FIELDS = 6
TINY = 1e-30
LIMIT = 24 * 2**20
WHOLE = 66_800_000


def iota(shape, dim):
    return lax.broadcasted_iota(jnp.int32, shape, dim)


def harmonic(first, second):
    return 2.0 * first * second / jnp.maximum(first + second, TINY)


def swap(field):
    return jnp.concatenate([field[:, 1:2], field[:, 0:1]], axis=1)


def call(kernel, outs, cost=20000, grant=LIMIT):
    vmem = pl.BlockSpec(memory_space=pltpu.VMEM)

    def run(*args):
        return pl.pallas_call(
            kernel,
            out_shape=[jax.ShapeDtypeStruct(o, F32) for o in outs],
            in_specs=[vmem] * len(args),
            out_specs=[vmem] * len(outs),
            compiler_params=pltpu.CompilerParams(vmem_limit_bytes=grant),
            cost_estimate=pl.CostEstimate(flops=cost, bytes_accessed=cost, transcendentals=0),
        )(*args)

    return run


def pack(gy, residual_ref, tile_ref, cell_ref, adjoint_ref, conductivity_ref, ratio_ref, rate_ref, fields_ref, out_ref):
    fields_ref[0] = adjoint_ref[...]
    fields_ref[1:4] = conductivity_ref[...]
    fields_ref[4] = ratio_ref[...]
    fields_ref[5] = rate_ref[...]
    count = residual_ref.shape[1]
    tiles = out_ref.shape[0]
    eye = iota((count, count), 0) == iota((count, count), 1)

    def column(row):
        return jnp.sum(jnp.where(eye, jnp.broadcast_to(row, (count, count)), 0.0), axis=1, keepdims=True)

    named = tile_ref[...]
    tile_row = named.astype(F32)
    tile_col = column(tile_row)
    same = (tile_col == tile_row) & (iota((count, count), 1) < iota((count, count), 0))
    rank = jnp.sum(same.astype(F32), axis=1, keepdims=True).astype(jnp.int32)
    values = [column(residual_ref[s : s + 1, :]) for s in range(4)]
    values.append(column(cell_ref[...].astype(F32) + 1.0))
    lane = iota((count, LANES), 1)
    within = lane % 8
    spread = jnp.zeros((count, LANES), F32)
    for place, value in enumerate(values):
        spread = jnp.where(within == place, value, spread)
    spread = jnp.where((lane % 32) // 8 == rank, spread, 0.0)
    tile_at = iota((tiles, count), 0)
    total = jnp.zeros((tiles, LANES), F32)
    for group, (step, edge) in enumerate(((0, -1), (-1, 0), (1, gy - 1))):
        hit = (named == tile_at + step) & (tile_at % gy != edge)
        part = jnp.where(lane // 32 == group, spread, 0.0)
        total = total + jnp.dot(hit.astype(F32), part, precision=lax.Precision.HIGHEST, preferred_element_type=F32)
    out_ref[...] = total


def needed(layers):
    return [(f, l) for f in range(FIELDS) for l in range(layers) if f in (0, 3, 4) or 0 < l < layers - 1]


def stacked(refs, field, layer):
    each = refs[0].shape[1]
    return refs[layer // each][field, layer % each]


def pack_columns(below_ref, own_ref, above_ref, left_ref, right_ref):
    refs = (below_ref, own_ref, above_ref)
    layers = 3 * own_ref.shape[1]
    rows = own_ref.shape[2]
    piece = iota((rows, LANES), 1) // WIDE
    planes = needed(layers)
    for j in range(left_ref.shape[0]):
        left = right = None
        for q, (f, l) in enumerate(planes[j * PIECES : (j + 1) * PIECES]):
            plane = stacked(refs, f, l)
            to_left = plane if q == 0 else pltpu.roll(plane, WIDE * q, 1)
            to_right = pltpu.roll(plane, WIDE * q + WIDE, 1)
            left = to_left if q == 0 else jnp.where(piece == q, to_left, left)
            right = to_right if q == 0 else jnp.where(piece == q, to_right, right)
        left_ref[j] = left
        right_ref[j] = right


def spread_column(columns, at, shape):
    return jnp.broadcast_to(columns[:, at : at + 1], shape)


def sources(layer_axis, own, layers, rows, sensors_ref, steps):
    got = sensors_ref[...]
    blocks = got.shape[0]
    lane = iota((blocks, LANES), 1)
    lane_at = lane.astype(F32)
    cell = got.astype(jnp.int32) - 1
    row_base = (lax.axis_index(layer_axis) * own - own) * rows
    cell_row = ((cell >> 7) - row_base).astype(F32).T
    cell_col = cell & (LANES - 1)
    half = LANES // 2
    group_of = lane // 32
    cell_col = jnp.where(
        group_of == 0,
        cell_col,
        jnp.where(
            group_of == 1,
            jnp.where(cell_col >= LANES - WIDE, cell_col - half, -LANES),
            jnp.where(cell_col < WIDE, cell_col, -LANES),
        ),
    ).astype(F32)
    row_at = iota((layers * rows, blocks), 0).astype(F32)
    high = got.astype(BF16)
    values = (high, (got - high.astype(F32)).astype(BF16))
    onehots, tables = ([], []), ([], [])
    for group in range(3):
        for slot in range(SLOTS):
            base = group * 32 + slot * 8
            onehots[group > 0].append((cell_row[base + 4 : base + 5, :] == row_at).astype(F32).astype(BF16))
            at = spread_column(cell_col, base + 4, lane.shape)
            pairs = (0, half) if group > 0 and len(steps) > 1 else (0,)
            place = [(at == lane_at - by).astype(F32).astype(BF16) for by in pairs]
            line = []
            for part in range(2):
                cells = [spread_column(values[part], base + s, lane.shape) for s in steps]
                for k in range(0, len(cells), len(place)):
                    line.append(functools.reduce(jnp.add, [m * v for m, v in zip(place, cells[k : k + len(place)])]))
            tables[group > 0].append(jnp.concatenate(line, axis=1))
    sums = []
    for onehot, table in zip(onehots, tables):
        both = jnp.dot(jnp.concatenate(onehot, axis=1), jnp.concatenate(table, axis=0), preferred_element_type=F32)
        width = both.shape[1] // 2
        sums.append(both[:, :width] + both[:, width:])
    centre, side = sums
    lane = iota((layers * rows, LANES), 1)
    out = []
    for s in range(len(steps)):
        tile = side[:, (s // 2) * LANES : (s // 2 + 1) * LANES]
        turned = pltpu.roll(tile, half, 1)
        right, left = (tile, turned) if s % 2 == 0 else (turned, tile)
        beside = jnp.where(lane < WIDE, right, jnp.where(lane >= LANES - WIDE, left, 0.0))
        parts = [m.reshape(layers, 1, rows, LANES) for m in (centre[:, s * LANES : (s + 1) * LANES], beside)]
        out.append(jnp.concatenate(parts, axis=1))
    return out


def prepare(axes, substeps_ref, below_ref, own_ref, above_ref, left_ref, right_ref, state_ref, fixed_ref, edge_ref, counts_ref):
    refs = (below_ref, own_ref, above_ref)
    own = own_ref.shape[1]
    layers = 3 * own
    rows = own_ref.shape[2]
    lane = iota((rows, LANES), 1)

    listed = {plane: at for at, plane in enumerate(needed(layers))}

    def field(f):
        planes = []
        for l in range(layers):
            if (f, l) in listed:
                j, q = divmod(listed[f, l], PIECES)
                from_left = pltpu.roll(left_ref[j], (LANES - WIDE - WIDE * q) % LANES, 1)
                from_right = pltpu.roll(right_ref[j], LANES - WIDE * q, 1) if q != 0 else right_ref[j]
                side = jnp.where(lane < WIDE, from_right, jnp.where(lane >= LANES - WIDE, from_left, 0.0))
            else:
                side = jnp.zeros((rows, LANES), F32)
            planes.append(jnp.stack([stacked(refs, f, l), side], axis=0))
        return jnp.stack(planes, axis=0)

    at_x, at_y = (lax.axis_index(axis) for axis in axes)
    n_y, n_x = substeps_ref.shape
    named = jnp.where(iota((n_y, n_x), 1) == at_x, substeps_ref[...].astype(F32), 0.0)

    def count(tile):
        rows_of = jnp.sum(jnp.where(iota((n_y, n_x), 0) == tile, named, 0.0), axis=1, keepdims=True)
        return jnp.broadcast_to(jnp.sum(rows_of, axis=0, keepdims=True), (rows, LANES))

    counts_ref[0] = count(at_y)
    counts_ref[1] = jnp.where(lane < LANES // 2, count(at_y + 1), count(at_y - 1))
    shape = (layers, 2, rows, LANES)
    row = iota(shape, 2)
    col = iota(shape, 3)
    state_ref[...] = field(0)
    along_rows = field(1)
    edge_ref[0] = along_rows[:, :, 0:1, :]
    edge_ref[1] = along_rows[:, :, rows - 1 :, :]
    fixed_ref[0] = harmonic(along_rows, jnp.where(row == rows - 1, 0.0, pltpu.roll(along_rows, rows - 1, 2)))
    along_cols = field(2)
    rolled = pltpu.roll(along_cols, LANES - 1, 3)
    fixed_ref[1] = harmonic(along_cols, jnp.where(col == LANES - 1, swap(rolled), rolled))
    along_layers = field(3)
    fixed_ref[2, : layers - 1] = harmonic(along_layers[: layers - 1], along_layers[1:])
    fixed_ref[2, layers - 1 :] = jnp.zeros((1, 2, rows, LANES), F32)
    fixed_ref[3] = field(4)
    fixed_ref[4] = field(5)


def first_source(layer_axis, own, state_in, fixed_ref, edge_ref, sensors_ref, state_ref, up_ref, down_ref):
    layers, _, rows, _ = state_ref.shape
    (source,) = sources(layer_axis, own, layers, rows, sensors_ref, (3,))
    state = state_in[...] + source
    state_ref[...] = state
    weighted = fixed_ref[3] * state
    up_ref[0] = weighted[:, :, 0:1, :]
    up_ref[1] = edge_ref[0]
    down_ref[0] = weighted[:, :, rows - 1 :, :]
    down_ref[1] = edge_ref[1]


def other_sources(layer_axis, own, sensors_ref, source_ref):
    _, layers, _, rows, _ = source_ref.shape
    for s, source in enumerate(sources(layer_axis, own, layers, rows, sensors_ref, (0, 1, 2))):
        source_ref[s] = source


def step(axis, turn, *refs):
    first, last = turn == 3, turn == 0
    refs = list(refs)
    counts_ref, state_ref, fixed_ref, above_ref, below_ref = refs[:5]
    refs = refs[5:]
    if first:
        own_up_ref, own_down_ref = refs[:2]
    else:
        row_edge_ref, sens_ref = refs[:2]
    refs = refs[2:]
    if not last:
        source_ref = refs[0]
        refs = refs[1:]
    if first:
        state_out, up_out, down_out, sens_out, edge_out = refs
    elif not last:
        state_out, up_out, down_out, sens_out = refs
    else:
        state_out, sens_out = refs
    at_x, n_x = lax.axis_index(axis), lax.axis_size(axis)
    layers, _, rows, _ = state_ref.shape
    total = fixed_ref.shape[1]
    low = (total - layers) // 2
    span = slice(low, low + layers)
    inner = slice(low + 1, low + layers - 1)
    state = state_ref[...]
    weighted = fixed_ref[3, span] * state
    if first:
        edges = []
        for mine, other, there in ((own_up_ref, above_ref, at_x > 0), (own_down_ref, below_ref, at_x < n_x - 1)):
            edges.append(harmonic(mine[1], jnp.where(there, other[1], 0.0)))
        edge_out[0] = edges[0]
        edge_out[1] = edges[1]
        over, under = edges[0][1:-1], edges[1][1:-1]
    else:
        over, under = row_edge_ref[0, inner], row_edge_ref[1, inner]
    shape = (layers - 2, 2, rows, LANES)
    row, col = iota(shape, 2), iota(shape, 3)
    across = weighted[1:-1]
    halo_over = above_ref[0, 1:-1]
    halo_under = below_ref[0, 1:-1]
    flux = fixed_ref[0, inner] * (pltpu.roll(across, rows - 1, 2) - across)
    edge_low = over * (across[:, :, 0:1, :] - halo_over)
    edge_high = under * (halo_under - across[:, :, rows - 1 :, :])
    flux = jnp.where(row == rows - 1, edge_high, flux)
    change = flux - jnp.where(row == 0, edge_low, pltpu.roll(flux, 1, 2))
    rolled = pltpu.roll(across, LANES - 1, 3)
    flux = fixed_ref[1, inner] * (jnp.where(col == LANES - 1, swap(rolled), rolled) - across)
    rolled = pltpu.roll(flux, 1, 3)
    change = change + (flux - jnp.where(col == 0, swap(rolled), rolled))
    flux = fixed_ref[2, low : low + layers - 1] * (weighted[1:] - weighted[:-1])
    change = change + (flux[1:] - flux[:-1])
    state = state[1:-1] + change
    kept = slice(0, 1) if last else slice(0, 2)
    state = state[:, kept]
    rate = fixed_ref[4, inner, kept]
    counts = counts_ref[kept][None]
    keep_own = 1.0 - 4.0 * rate
    half = rows // 2
    part = state.shape[:2] + (half, LANES)
    row, col = iota(part, 2), iota(part, 3)

    def one_turn(at, now):
        top, low_half = (rate[:, :, h : h + half] * now[:, :, h : h + half] for h in (0, half))
        up = pltpu.roll(top, half - 1, 2), pltpu.roll(low_half, half - 1, 2)
        down = pltpu.roll(top, 1, 2), pltpu.roll(low_half, 1, 2)
        near = (
            jnp.where(row == half - 1, up[1], up[0]) + jnp.where(row == 0, top, down[0]),
            jnp.where(row == half - 1, low_half, up[1]) + jnp.where(row == 0, down[0], down[1]),
        )
        parts = []
        for h, (v, rowwise) in enumerate(zip((top, low_half), near)):
            colwise = jnp.where(col == LANES - 1, v, pltpu.roll(v, LANES - 1, 3)) + jnp.where(col == 0, v, pltpu.roll(v, 1, 3))
            here = slice(h * half, (h + 1) * half)
            after = keep_own[:, :, here] * now[:, :, here] + (rowwise + colwise)
            parts.append(after if at == 0 else jnp.where(counts[:, :, here] > at, after, now[:, :, here]))
        return jnp.concatenate(parts, axis=2)

    for at in range(MAXSUB):
        state = one_turn(at, state)
    own = total // 3
    keep = slice((layers - 2 - own) // 2, (layers - 2 - own) // 2 + own)
    addend = fixed_ref[3, own : 2 * own, 0] * state[keep, 0]
    sens_out[...] = addend if first else sens_ref[...] + addend
    if last:
        state_out[...] = state[:, 0]
        return
    state = state + source_ref[turn - 1, inner]
    state_out[...] = state
    weighted = fixed_ref[3, inner] * state
    up_out[0] = weighted[:, :, 0:1, :]
    down_out[0] = weighted[:, :, rows - 1 :, :]


def shift(cells, axis, by, wrap):
    count = lax.axis_size(axis)
    pairs = [(i, (i + by) % count) for i in range(count) if wrap or 0 <= i + by < count]
    return lax.ppermute(cells, axis, pairs)


def body(adjoint_final, conductivity, step_ratio, refine_rate, residual, sensor_tile, sensor_cell, substeps):
    own, rows, cols = adjoint_final.shape
    layers = 3 * own
    n_y = lax.axis_size("gy")
    tiles = lax.axis_size("gx") * n_y
    listed = sensor_tile.shape[0]
    fields, message = call(functools.partial(pack, n_y), [(FIELDS, own, rows, cols), (tiles, LANES)], grant=WHOLE)(
        residual,
        sensor_tile.reshape(1, listed),
        sensor_cell.reshape(1, listed),
        adjoint_final,
        conductivity,
        step_ratio,
        refine_rate,
    )
    below = shift(fields, "gz", 1, False)
    above = shift(fields, "gz", -1, False)
    sensors = lax.all_to_all(message, ("gx", "gy"), 0, 0, tiled=True)
    packed = (pl.cdiv(len(needed(layers)), PIECES), rows, LANES)
    to_left, to_right = call(pack_columns, [packed, packed])(below, fields, above)
    from_left = shift(to_right, "gy", 1, False)
    from_right = shift(to_left, "gy", -1, False)
    block = (layers, 2, rows, LANES)
    faces = (2, layers, 2, 1, LANES)
    state, fixed, edges, counts = call(
        functools.partial(prepare, ("gx", "gy")), [block, (5,) + block, faces, (2, rows, LANES)]
    )(substeps.T, below, fields, above, from_left, from_right)
    state, up, down = call(functools.partial(first_source, "gz", own), [block, faces, faces])(state, fixed, edges, sensors)
    (source,) = call(functools.partial(other_sources, "gz", own), [(3,) + block])(sensors)
    sens = edge = None
    for turn in range(3, -1, -1):
        over = shift(down, "gx", 1, True)
        under = shift(up, "gx", -1, True)
        depth = state.shape[0] - 2
        args = [counts, state, fixed]
        args += [over, under] + ([up, down] if turn == 3 else [edge, sens])
        if turn > 0:
            args += [source]
        face = (1, depth, 2, 1, LANES)
        if turn == 0:
            outs = [(own, rows, cols), (own, rows, cols)]
        else:
            outs = [(depth, 2, rows, LANES), face, face, (own, rows, cols)]
            if turn == 3:
                outs += [(2, layers, 2, 1, LANES)]
        got = call(functools.partial(step, "gx", turn), outs)(*args)
        if turn == 3:
            state, up, down, sens, edge = got
        elif turn > 0:
            state, up, down, sens = got
        else:
            return tuple(got)


def solution(mesh):
    return jax.shard_map(
        body,
        mesh=mesh,
        in_specs=(
            P("gz", "gx", "gy"),
            P(None, "gz", "gx", "gy"),
            P("gz", "gx", "gy"),
            P("gz", "gx", "gy"),
            P(None, ("gx", "gy")),
            P(("gx", "gy")),
            P(("gx", "gy")),
            P(),
        ),
        out_specs=(P("gz", "gx", "gy"), P("gz", "gx", "gy")),
        check_vma=False,
    )
```

```python
import functools

import jax
import jax.numpy as jnp
from jax import lax
from jax.experimental import pallas as pl
from jax.experimental.pallas import tpu as pltpu
from jax.sharding import PartitionSpec as P


F32 = jnp.float32
BF16 = jnp.bfloat16
LANES = 128
WIDE = 24
PIECES = LANES // WIDE
MAXSUB = 6
SLOTS = 4
FIELDS = 6
TINY = 1e-30
LIMIT = 24 * 2**20
WHOLE = 66_800_000


def iota(shape, dim):
    return lax.broadcasted_iota(jnp.int32, shape, dim)


def harmonic(first, second):
    return 2.0 * first * second / jnp.maximum(first + second, TINY)


def swap(field):
    return jnp.concatenate([field[:, 1:2], field[:, 0:1]], axis=1)


def call(kernel, outs, cost=20000, grant=LIMIT):
    vmem = pl.BlockSpec(memory_space=pltpu.VMEM)

    def run(*args):
        return pl.pallas_call(
            kernel,
            out_shape=[jax.ShapeDtypeStruct(o, F32) for o in outs],
            in_specs=[vmem] * len(args),
            out_specs=[vmem] * len(outs),
            compiler_params=pltpu.CompilerParams(vmem_limit_bytes=grant),
            cost_estimate=pl.CostEstimate(flops=cost, bytes_accessed=cost, transcendentals=0),
        )(*args)

    return run


def pack(gy, residual_ref, tile_ref, cell_ref, adjoint_ref, conductivity_ref, ratio_ref, rate_ref, fields_ref, out_ref):
    fields_ref[0] = adjoint_ref[...]
    fields_ref[1:4] = conductivity_ref[...]
    fields_ref[4] = ratio_ref[...]
    fields_ref[5] = rate_ref[...]
    count = residual_ref.shape[1]
    tiles = out_ref.shape[0]
    eye = iota((count, count), 0) == iota((count, count), 1)

    def column(row):
        return jnp.sum(jnp.where(eye, jnp.broadcast_to(row, (count, count)), 0.0), axis=1, keepdims=True)

    named = tile_ref[...]
    tile_row = named.astype(F32)
    tile_col = column(tile_row)
    same = (tile_col == tile_row) & (iota((count, count), 1) < iota((count, count), 0))
    rank = jnp.sum(same.astype(F32), axis=1, keepdims=True).astype(jnp.int32)
    values = [column(residual_ref[s : s + 1, :]) for s in range(4)]
    values.append(column(cell_ref[...].astype(F32) + 1.0))
    lane = iota((count, LANES), 1)
    within = lane % 8
    spread = jnp.zeros((count, LANES), F32)
    for place, value in enumerate(values):
        spread = jnp.where(within == place, value, spread)
    spread = jnp.where((lane % 32) // 8 == rank, spread, 0.0)
    tile_at = iota((tiles, count), 0)
    total = jnp.zeros((tiles, LANES), F32)
    for group, (step, edge) in enumerate(((0, -1), (-1, 0), (1, gy - 1))):
        hit = (named == tile_at + step) & (tile_at % gy != edge)
        part = jnp.where(lane // 32 == group, spread, 0.0)
        total = total + jnp.dot(hit.astype(F32), part, precision=lax.Precision.HIGHEST, preferred_element_type=F32)
    out_ref[...] = total


def needed(layers):
    return [(f, l) for f in range(FIELDS) for l in range(layers) if f in (0, 3, 4) or 0 < l < layers - 1]


def stacked(refs, field, layer):
    each = refs[0].shape[1]
    return refs[layer // each][field, layer % each]


def pack_columns(below_ref, own_ref, above_ref, left_ref, right_ref):
    refs = (below_ref, own_ref, above_ref)
    layers = 3 * own_ref.shape[1]
    rows = own_ref.shape[2]
    piece = iota((rows, LANES), 1) // WIDE
    planes = needed(layers)
    for j in range(left_ref.shape[0]):
        left = right = None
        for q, (f, l) in enumerate(planes[j * PIECES : (j + 1) * PIECES]):
            plane = stacked(refs, f, l)
            to_left = plane if q == 0 else pltpu.roll(plane, WIDE * q, 1)
            to_right = pltpu.roll(plane, WIDE * q + WIDE, 1)
            left = to_left if q == 0 else jnp.where(piece == q, to_left, left)
            right = to_right if q == 0 else jnp.where(piece == q, to_right, right)
        left_ref[j] = left
        right_ref[j] = right


def spread_column(columns, at, shape):
    return jnp.broadcast_to(columns[:, at : at + 1], shape)


def sources(layer_axis, own, layers, rows, sensors_ref, steps):
    got = sensors_ref[...]
    blocks = got.shape[0]
    lane = iota((blocks, LANES), 1)
    lane_at = lane.astype(F32)
    cell = got.astype(jnp.int32) - 1
    row_base = (lax.axis_index(layer_axis) * own - own) * rows
    cell_row = ((cell >> 7) - row_base).astype(F32).T
    cell_col = cell & (LANES - 1)
    half = LANES // 2
    group_of = lane // 32
    cell_col = jnp.where(
        group_of == 0,
        cell_col,
        jnp.where(
            group_of == 1,
            jnp.where(cell_col >= LANES - WIDE, cell_col - half, -LANES),
            jnp.where(cell_col < WIDE, cell_col, -LANES),
        ),
    ).astype(F32)
    row_at = iota((layers * rows, blocks), 0).astype(F32)
    high = got.astype(BF16)
    values = (high, (got - high.astype(F32)).astype(BF16))
    onehots, tables = ([], []), ([], [])
    for group in range(3):
        for slot in range(SLOTS):
            base = group * 32 + slot * 8
            onehots[group > 0].append((cell_row[base + 4 : base + 5, :] == row_at).astype(F32).astype(BF16))
            at = spread_column(cell_col, base + 4, lane.shape)
            pairs = (0, half) if group > 0 and len(steps) > 1 else (0,)
            place = [(at == lane_at - by).astype(F32).astype(BF16) for by in pairs]
            line = []
            for part in range(2):
                cells = [spread_column(values[part], base + s, lane.shape) for s in steps]
                for k in range(0, len(cells), len(place)):
                    line.append(functools.reduce(jnp.add, [m * v for m, v in zip(place, cells[k : k + len(place)])]))
            tables[group > 0].append(jnp.concatenate(line, axis=1))
    sums = []
    for onehot, table in zip(onehots, tables):
        both = jnp.dot(jnp.concatenate(onehot, axis=1), jnp.concatenate(table, axis=0), preferred_element_type=F32)
        width = both.shape[1] // 2
        sums.append(both[:, :width] + both[:, width:])
    centre, side = sums
    lane = iota((layers * rows, LANES), 1)
    out = []
    for s in range(len(steps)):
        tile = side[:, (s // 2) * LANES : (s // 2 + 1) * LANES]
        turned = pltpu.roll(tile, half, 1)
        right, left = (tile, turned) if s % 2 == 0 else (turned, tile)
        beside = jnp.where(lane < WIDE, right, jnp.where(lane >= LANES - WIDE, left, 0.0))
        parts = [m.reshape(layers, 1, rows, LANES) for m in (centre[:, s * LANES : (s + 1) * LANES], beside)]
        out.append(jnp.concatenate(parts, axis=1))
    return out


def prepare(axes, substeps_ref, below_ref, own_ref, above_ref, left_ref, right_ref, state_ref, fixed_ref, up_ref, down_ref, counts_ref):
    refs = (below_ref, own_ref, above_ref)
    own = own_ref.shape[1]
    layers = 3 * own
    rows = own_ref.shape[2]
    lane = iota((rows, LANES), 1)

    listed = {plane: at for at, plane in enumerate(needed(layers))}

    def field(f):
        planes = []
        for l in range(layers):
            if (f, l) in listed:
                j, q = divmod(listed[f, l], PIECES)
                from_left = pltpu.roll(left_ref[j], (LANES - WIDE - WIDE * q) % LANES, 1)
                from_right = pltpu.roll(right_ref[j], LANES - WIDE * q, 1) if q != 0 else right_ref[j]
                side = jnp.where(lane < WIDE, from_right, jnp.where(lane >= LANES - WIDE, from_left, 0.0))
            else:
                side = jnp.zeros((rows, LANES), F32)
            planes.append(jnp.stack([stacked(refs, f, l), side], axis=0))
        return jnp.stack(planes, axis=0)

    at_x, at_y = (lax.axis_index(axis) for axis in axes)
    n_y, n_x = substeps_ref.shape
    named = substeps_ref[...].astype(F32)

    def count(x, y):
        hit = (iota((n_y, n_x), 1) == x) & (iota((n_y, n_x), 0) == y)
        found = jnp.sum(jnp.where(hit, named, 0.0), axis=1, keepdims=True)
        return jnp.broadcast_to(jnp.sum(found, axis=0, keepdims=True), (rows // 2, LANES))

    for part, x in enumerate((at_x - 1, at_x, at_x, at_x + 1)):
        at_rows = slice(part * (rows // 2), (part + 1) * (rows // 2))
        counts_ref[0, at_rows] = count(x, at_y)
        counts_ref[1, at_rows] = jnp.where(lane[: rows // 2] < LANES // 2, count(x, at_y + 1), count(x, at_y - 1))
    state_ref[...] = field(0)
    half = rows // 2
    for f in range(1, FIELDS):
        values = field(f)
        fixed_ref[f - 1] = values
        up_ref[f - 1] = values[:, :, :half]
        down_ref[f - 1] = values[:, :, half:]


def conduct(axis, own_ref, over_ref, under_ref, fixed_ref):
    at_x, n_x = lax.axis_index(axis), lax.axis_size(axis)

    def deep(f, masked=False):
        over, under = over_ref[f], under_ref[f]
        if masked:
            over = jnp.where(at_x > 0, over, 0.0)
            under = jnp.where(at_x < n_x - 1, under, 0.0)
        return jnp.concatenate([over, own_ref[f], under], axis=2)

    along_rows = deep(0, True)
    shape = along_rows.shape
    layers, _, rows, _ = shape
    row = iota(shape, 2)
    col = iota(shape, 3)
    fixed_ref[0] = harmonic(along_rows, jnp.where(row == rows - 1, 0.0, pltpu.roll(along_rows, rows - 1, 2)))
    along_cols = deep(1)
    rolled = pltpu.roll(along_cols, LANES - 1, 3)
    fixed_ref[1] = harmonic(along_cols, jnp.where(col == LANES - 1, swap(rolled), rolled))
    along_layers = deep(2)
    fixed_ref[2, : layers - 1] = harmonic(along_layers[: layers - 1], along_layers[1:])
    fixed_ref[2, layers - 1 :] = jnp.zeros((1,) + shape[1:], F32)
    fixed_ref[3] = deep(3)
    fixed_ref[4] = deep(4)


def send_rows(state, source, up_ref, down_ref):
    half = state.shape[2] // 2
    up_ref[0] = state[:, :, :half]
    up_ref[1] = source[:, :, :half]
    down_ref[0] = state[:, :, half:]
    down_ref[1] = source[:, :, half:]


def first_sources(layer_axis, own, state_in, sensors_ref, state_ref, source_ref, up_ref, down_ref):
    layers, _, rows, _ = state_ref.shape
    second, first = sources(layer_axis, own, layers, rows, sensors_ref, (2, 3))
    state = state_in[...] + first
    state_ref[...] = state
    source_ref[...] = second
    send_rows(state, second, up_ref, down_ref)


def other_sources(layer_axis, own, sensors_ref, source_ref):
    _, layers, _, rows, _ = source_ref.shape
    for s, source in enumerate(sources(layer_axis, own, layers, rows, sensors_ref, (0, 1))):
        source_ref[s] = source


def diffuse(fixed_ref, low, state, kept):
    layers = state.shape[0]
    span, inner = slice(low, low + layers), slice(low + 1, low + layers - 1)
    weighted = fixed_ref[3, span] * state
    across = weighted[1:-1]
    flux = fixed_ref[0, inner] * (pltpu.roll(across, across.shape[2] - 1, 2) - across)
    change = (flux - pltpu.roll(flux, 1, 2))[:, :, kept]
    weighted, across = weighted[:, :, kept], across[:, :, kept]
    col = iota(across.shape, 3)
    rolled = pltpu.roll(across, LANES - 1, 3)
    flux = fixed_ref[1, inner, :, kept] * (jnp.where(col == LANES - 1, swap(rolled), rolled) - across)
    rolled = pltpu.roll(flux, 1, 3)
    change = change + (flux - jnp.where(col == 0, swap(rolled), rolled))
    flux = fixed_ref[2, low : low + layers - 1, :, kept] * (weighted[1:] - weighted[:-1])
    change = change + (flux[1:] - flux[:-1])
    return state[1:-1, :, kept] + change


def refine(state, rate, counts, tiles):
    size = 8
    shape = state.shape[:2] + (size, LANES)
    row, col = iota(shape, 2), iota(shape, 3)
    pieces = range(state.shape[2] // size)
    at_rows = [slice(p * size, (p + 1) * size) for p in pieces]
    rates = [rate[:, :, r] for r in at_rows]
    keeps = [1.0 - 4.0 * r for r in rates]
    limits = [counts[:, :, r] for r in at_rows]
    now = [state[:, :, r] for r in at_rows]
    for turn in range(MAXSUB):
        scaled = [rates[p] * now[p] for p in pieces]
        later = list(now)
        for tile in tiles:
            ups = {p: pltpu.roll(scaled[p], size - 1, 2) for p in tile}
            downs = {p: pltpu.roll(scaled[p], 1, 2) for p in tile}
            for p in tile:
                v = scaled[p]
                near = jnp.where(row == size - 1, ups[p + 1] if p + 1 in tile else v, ups[p])
                near = near + jnp.where(row == 0, downs[p - 1] if p - 1 in tile else v, downs[p])
                near = near + jnp.where(col == LANES - 1, v, pltpu.roll(v, LANES - 1, 3))
                near = near + jnp.where(col == 0, v, pltpu.roll(v, 1, 3))
                after = keeps[p] * now[p] + near
                later[p] = after if turn == 0 else jnp.where(limits[p] > turn, after, now[p])
        now = later
    return jnp.concatenate(now, axis=2)


def two_steps(last, counts_ref, state_ref, fixed_ref, over_ref, under_ref, between_ref, *refs):
    if last:
        sens_ref, state_out, sens_out = refs
    else:
        rest_ref, state_out, up_out, down_out, sens_out = refs
    layers, _, rows, _ = state_ref.shape
    total = fixed_ref.shape[1]
    own = total // 3
    low = (total - layers) // 2
    half = rows // 2
    mine = slice(half, half + rows)
    everything = slice(0, 2 * rows)

    def deep(field, at):
        return jnp.concatenate([over_ref[at], field, under_ref[at]], axis=2)

    def sensed(state, first_row):
        keep = slice((state.shape[0] - own) // 2, (state.shape[0] - own) // 2 + own)
        return fixed_ref[3, own : 2 * own, 0, mine] * state[keep, 0, first_row : first_row + rows]

    state = diffuse(fixed_ref, low, deep(state_ref[...], 0), everything)
    state = refine(state, fixed_ref[4, low + 1 : low + layers - 1], counts_ref[...][None], ((0,), (1, 2), (3,)))
    sens = sensed(state, half)
    if last:
        sens = sens_ref[...] + sens
    state = state + deep(between_ref[low : low + layers], 1)[1:-1]
    state = diffuse(fixed_ref, low + 1, state, mine)
    halves = slice(0, 1) if last else slice(0, 2)
    inner = slice(low + 2, low + layers - 2)
    state = refine(state[:, halves], fixed_ref[4, inner, halves, mine], counts_ref[halves, mine][None], ((0, 1),))
    sens_out[...] = sens + sensed(state, 0)
    if last:
        state_out[...] = state[:, 0]
        return
    state = state + rest_ref[1, inner]
    state_out[...] = state
    send_rows(state, rest_ref[0, inner], up_out, down_out)


def shift(cells, axis, by, wrap):
    count = lax.axis_size(axis)
    pairs = [(i, (i + by) % count) for i in range(count) if wrap or 0 <= i + by < count]
    return lax.ppermute(cells, axis, pairs)


def body(adjoint_final, conductivity, step_ratio, refine_rate, residual, sensor_tile, sensor_cell, substeps):
    own, rows, cols = adjoint_final.shape
    layers = 3 * own
    n_y = lax.axis_size("gy")
    tiles = lax.axis_size("gx") * n_y
    listed = sensor_tile.shape[0]
    fields, message = call(functools.partial(pack, n_y), [(FIELDS, own, rows, cols), (tiles, LANES)], grant=WHOLE)(
        residual,
        sensor_tile.reshape(1, listed),
        sensor_cell.reshape(1, listed),
        adjoint_final,
        conductivity,
        step_ratio,
        refine_rate,
    )
    below = shift(fields, "gz", 1, False)
    above = shift(fields, "gz", -1, False)
    sensors = lax.all_to_all(message, ("gx", "gy"), 0, 0, tiled=True)
    packed = (pl.cdiv(len(needed(layers)), PIECES), rows, LANES)
    to_left, to_right = call(pack_columns, [packed, packed])(below, fields, above)
    from_left = shift(to_right, "gy", 1, False)
    from_right = shift(to_left, "gy", -1, False)
    block = (layers, 2, rows, LANES)
    halo = (layers, 2, rows // 2, LANES)
    state, fixed, up, down, counts = call(
        functools.partial(prepare, ("gx", "gy")), [block, (5,) + block, (5,) + halo, (5,) + halo, (2, 2 * rows, LANES)]
    )(substeps.T, below, fields, above, from_left, from_right)
    over = shift(down, "gx", 1, True)
    under = shift(up, "gx", -1, True)
    first_state, second, up, down = call(
        functools.partial(first_sources, "gz", own), [block, block, (2,) + halo, (2,) + halo]
    )(state, sensors)
    (fixed,) = call(functools.partial(conduct, "gx"), [(5, layers, 2, 2 * rows, LANES)])(fixed, over, under)
    (rest,) = call(functools.partial(other_sources, "gz", own), [(2,) + block])(sensors)
    over = shift(down, "gx", 1, True)
    under = shift(up, "gx", -1, True)
    depth = layers - 4
    halo = (2, depth, 2, rows // 2, LANES)
    state, up, down, sens = call(
        functools.partial(two_steps, False), [(depth, 2, rows, LANES), halo, halo, (own, rows, cols)]
    )(counts, first_state, fixed, over, under, second, rest)
    over = shift(down, "gx", 1, True)
    under = shift(up, "gx", -1, True)
    return tuple(
        call(functools.partial(two_steps, True), [(own, rows, cols), (own, rows, cols)])(
            counts, state, fixed, over, under, rest[0], sens
        )
    )


def solution(mesh):
    return jax.shard_map(
        body,
        mesh=mesh,
        in_specs=(
            P("gz", "gx", "gy"),
            P(None, "gz", "gx", "gy"),
            P("gz", "gx", "gy"),
            P("gz", "gx", "gy"),
            P(None, ("gx", "gy")),
            P(("gx", "gy")),
            P(("gx", "gy")),
            P(),
        ),
        out_specs=(P("gz", "gx", "gy"), P("gz", "gx", "gy")),
        check_vma=False,
    )
```

```python
import functools

import jax
import jax.numpy as jnp
from jax import lax
from jax.experimental import pallas as pl
from jax.experimental.pallas import tpu as pltpu
from jax.sharding import PartitionSpec as P


F32 = jnp.float32
BF16 = jnp.bfloat16
LANES = 128
WIDE = 24
PIECES = LANES // WIDE
MAXSUB = 6
SLOTS = 4
FIELDS = 6
TINY = 1e-30
LIMIT = 24 * 2**20
WHOLE = 66_800_000


def iota(shape, dim):
    return lax.broadcasted_iota(jnp.int32, shape, dim)


def harmonic(first, second):
    return 2.0 * first * second / jnp.maximum(first + second, TINY)


def swap(field):
    return jnp.concatenate([field[:, 1:2], field[:, 0:1]], axis=1)


def call(kernel, outs, cost=20000, grant=LIMIT):
    vmem = pl.BlockSpec(memory_space=pltpu.VMEM)

    def run(*args):
        return pl.pallas_call(
            kernel,
            out_shape=[jax.ShapeDtypeStruct(o, F32) for o in outs],
            in_specs=[vmem] * len(args),
            out_specs=[vmem] * len(outs),
            compiler_params=pltpu.CompilerParams(vmem_limit_bytes=grant),
            cost_estimate=pl.CostEstimate(flops=cost, bytes_accessed=cost, transcendentals=0),
        )(*args)

    return run


def pack(gy, residual_ref, tile_ref, cell_ref, adjoint_ref, conductivity_ref, ratio_ref, rate_ref, fields_ref, out_ref):
    fields_ref[0] = adjoint_ref[...]
    fields_ref[1:4] = conductivity_ref[...]
    fields_ref[4] = ratio_ref[...]
    fields_ref[5] = rate_ref[...]
    count = residual_ref.shape[1]
    tiles = out_ref.shape[0]
    eye = iota((count, count), 0) == iota((count, count), 1)

    def column(row):
        return jnp.sum(jnp.where(eye, jnp.broadcast_to(row, (count, count)), 0.0), axis=1, keepdims=True)

    named = tile_ref[...]
    tile_row = named.astype(F32)
    tile_col = column(tile_row)
    same = (tile_col == tile_row) & (iota((count, count), 1) < iota((count, count), 0))
    rank = jnp.sum(same.astype(F32), axis=1, keepdims=True).astype(jnp.int32)
    values = [column(residual_ref[s : s + 1, :]) for s in range(4)]
    values.append(column(cell_ref[...].astype(F32) + 1.0))
    lane = iota((count, LANES), 1)
    within = lane % 8
    spread = jnp.zeros((count, LANES), F32)
    for place, value in enumerate(values):
        spread = jnp.where(within == place, value, spread)
    spread = jnp.where((lane % 32) // 8 == rank, spread, 0.0)
    tile_at = iota((tiles, count), 0)
    total = jnp.zeros((tiles, LANES), F32)
    for group, (step, edge) in enumerate(((0, -1), (-1, 0), (1, gy - 1))):
        hit = (named == tile_at + step) & (tile_at % gy != edge)
        part = jnp.where(lane // 32 == group, spread, 0.0)
        total = total + jnp.dot(hit.astype(F32), part, precision=lax.Precision.HIGHEST, preferred_element_type=F32)
    out_ref[...] = total


def needed(layers):
    return [(f, l) for f in range(FIELDS) for l in range(layers) if f in (0, 3, 4) or 0 < l < layers - 1]


def stacked(refs, field, layer):
    each = refs[0].shape[1]
    return refs[layer // each][field, layer % each]


def pack_columns(below_ref, own_ref, above_ref, left_ref, right_ref):
    refs = (below_ref, own_ref, above_ref)
    layers = 3 * own_ref.shape[1]
    rows = own_ref.shape[2]
    piece = iota((rows, LANES), 1) // WIDE
    planes = needed(layers)
    for j in range(left_ref.shape[0]):
        left = right = None
        for q, (f, l) in enumerate(planes[j * PIECES : (j + 1) * PIECES]):
            plane = stacked(refs, f, l)
            to_left = plane if q == 0 else pltpu.roll(plane, WIDE * q, 1)
            to_right = pltpu.roll(plane, WIDE * q + WIDE, 1)
            left = to_left if q == 0 else jnp.where(piece == q, to_left, left)
            right = to_right if q == 0 else jnp.where(piece == q, to_right, right)
        left_ref[j] = left
        right_ref[j] = right


def spread_column(columns, at, shape):
    return jnp.broadcast_to(columns[:, at : at + 1], shape)


def sources(layer_axis, own, layers, rows, sensors_ref, steps):
    got = sensors_ref[...]
    blocks = got.shape[0]
    lane = iota((blocks, LANES), 1)
    lane_at = lane.astype(F32)
    cell = got.astype(jnp.int32) - 1
    row_base = (lax.axis_index(layer_axis) * own - own) * rows
    cell_row = ((cell >> 7) - row_base).astype(F32).T
    cell_col = cell & (LANES - 1)
    half = LANES // 2
    group_of = lane // 32
    cell_col = jnp.where(
        group_of == 0,
        cell_col,
        jnp.where(
            group_of == 1,
            jnp.where(cell_col >= LANES - WIDE, cell_col - half, -LANES),
            jnp.where(cell_col < WIDE, cell_col, -LANES),
        ),
    ).astype(F32)
    row_at = iota((layers * rows, blocks), 0).astype(F32)
    high = got.astype(BF16)
    values = (high, (got - high.astype(F32)).astype(BF16))
    onehots, tables = ([], []), ([], [])
    for group in range(3):
        for slot in range(SLOTS):
            base = group * 32 + slot * 8
            onehots[group > 0].append((cell_row[base + 4 : base + 5, :] == row_at).astype(F32).astype(BF16))
            at = spread_column(cell_col, base + 4, lane.shape)
            pairs = (0, half) if group > 0 and len(steps) > 1 else (0,)
            place = [(at == lane_at - by).astype(F32).astype(BF16) for by in pairs]
            line = []
            for part in range(2):
                cells = [spread_column(values[part], base + s, lane.shape) for s in steps]
                for k in range(0, len(cells), len(place)):
                    line.append(functools.reduce(jnp.add, [m * v for m, v in zip(place, cells[k : k + len(place)])]))
            tables[group > 0].append(jnp.concatenate(line, axis=1))
    sums = []
    for onehot, table in zip(onehots, tables):
        both = jnp.dot(jnp.concatenate(onehot, axis=1), jnp.concatenate(table, axis=0), preferred_element_type=F32)
        width = both.shape[1] // 2
        sums.append(both[:, :width] + both[:, width:])
    centre, side = sums
    lane = iota((layers * rows, LANES), 1)
    out = []
    for s in range(len(steps)):
        tile = side[:, (s // 2) * LANES : (s // 2 + 1) * LANES]
        turned = pltpu.roll(tile, half, 1)
        right, left = (tile, turned) if s % 2 == 0 else (turned, tile)
        beside = jnp.where(lane < WIDE, right, jnp.where(lane >= LANES - WIDE, left, 0.0))
        parts = [m.reshape(layers, 1, rows, LANES) for m in (centre[:, s * LANES : (s + 1) * LANES], beside)]
        out.append(jnp.concatenate(parts, axis=1))
    return out


def prepare(below_ref, own_ref, above_ref, left_ref, right_ref, state_ref, fixed_ref, up_ref, down_ref):
    refs = (below_ref, own_ref, above_ref)
    own = own_ref.shape[1]
    layers = 3 * own
    rows = own_ref.shape[2]
    lane = iota((rows, LANES), 1)

    listed = {plane: at for at, plane in enumerate(needed(layers))}

    def field(f):
        planes = []
        for l in range(layers):
            if (f, l) in listed:
                j, q = divmod(listed[f, l], PIECES)
                from_left = pltpu.roll(left_ref[j], (LANES - WIDE - WIDE * q) % LANES, 1)
                from_right = pltpu.roll(right_ref[j], LANES - WIDE * q, 1) if q != 0 else right_ref[j]
                side = jnp.where(lane < WIDE, from_right, jnp.where(lane >= LANES - WIDE, from_left, 0.0))
            else:
                side = jnp.zeros((rows, LANES), F32)
            planes.append(jnp.stack([stacked(refs, f, l), side], axis=0))
        return jnp.stack(planes, axis=0)

    state_ref[...] = field(0)
    half = rows // 2
    for f in range(1, FIELDS):
        values = field(f)
        fixed_ref[f - 1] = values
        up_ref[f - 1] = fold(values[:, :, :half])
        down_ref[f - 1] = fold(values[:, :, half:])


def fold(block):
    half = block.shape[0] // 2
    lane = iota((half,) + block.shape[2:], 2)
    used = (lane < WIDE) | (lane >= LANES - WIDE)
    low, high = (jnp.where(used, part, 0.0) for part in (block[:half, 1], block[half:, 1]))
    return jnp.concatenate([block[:, 0], low + pltpu.roll(high, LANES // 2, 2)], axis=0)


def unfold(folded):
    layers = folded.shape[0] * 2 // 3
    shared = folded[layers:]
    lane = iota(shared.shape, 2)
    used = (lane < WIDE) | (lane >= LANES - WIDE)
    parts = [jnp.where(used, part, 0.0) for part in (shared, pltpu.roll(shared, LANES // 2, 2))]
    return jnp.stack([folded[:layers], jnp.concatenate(parts, axis=0)], axis=1)


def conduct(axes, substeps_ref, own_ref, over_ref, under_ref, fixed_ref, counts_ref):
    at_x, at_y = (lax.axis_index(axis) for axis in axes)
    n_y, n_x = substeps_ref.shape
    named = substeps_ref[...].astype(F32)
    size = own_ref.shape[3] // 2
    lane = iota((size, LANES), 1)

    def count(x, y):
        hit = (iota((n_y, n_x), 1) == x) & (iota((n_y, n_x), 0) == y)
        found = jnp.sum(jnp.where(hit, named, 0.0), axis=1, keepdims=True)
        return jnp.broadcast_to(jnp.sum(found, axis=0, keepdims=True), (size, LANES))

    for part, x in enumerate((at_x - 1, at_x, at_x, at_x + 1)):
        at_rows = slice(part * size, (part + 1) * size)
        counts_ref[0, at_rows] = count(x, at_y)
        counts_ref[1, at_rows] = jnp.where(lane < LANES // 2, count(x, at_y + 1), count(x, at_y - 1))

    def deep(f, masked=False):
        over, under = unfold(over_ref[f]), unfold(under_ref[f])
        if masked:
            over = jnp.where(at_x > 0, over, 0.0)
            under = jnp.where(at_x < n_x - 1, under, 0.0)
        return jnp.concatenate([over, own_ref[f], under], axis=2)

    along_rows = deep(0, True)
    shape = along_rows.shape
    layers, _, rows, _ = shape
    row = iota(shape, 2)
    col = iota(shape, 3)
    fixed_ref[0] = harmonic(along_rows, jnp.where(row == rows - 1, 0.0, pltpu.roll(along_rows, rows - 1, 2)))
    along_cols = deep(1)
    rolled = pltpu.roll(along_cols, LANES - 1, 3)
    fixed_ref[1] = harmonic(along_cols, jnp.where(col == LANES - 1, swap(rolled), rolled))
    along_layers = deep(2)
    fixed_ref[2, : layers - 1] = harmonic(along_layers[: layers - 1], along_layers[1:])
    fixed_ref[2, layers - 1 :] = jnp.zeros((1,) + shape[1:], F32)
    fixed_ref[3] = deep(3)
    fixed_ref[4] = deep(4)


def send_rows(state, source, up_ref, down_ref):
    half = state.shape[2] // 2
    up_ref[0] = fold(state[:, :, :half])
    up_ref[1] = fold(source[:, :, :half])
    down_ref[0] = fold(state[:, :, half:])
    down_ref[1] = fold(source[:, :, half:])


def first_sources(layer_axis, own, state_in, sensors_ref, state_ref, source_ref, up_ref, down_ref):
    layers, _, rows, _ = state_ref.shape
    second, first = sources(layer_axis, own, layers, rows, sensors_ref, (2, 3))
    state = state_in[...] + first
    state_ref[...] = state
    source_ref[...] = second
    send_rows(state, second, up_ref, down_ref)


def other_sources(layer_axis, own, sensors_ref, source_ref):
    _, layers, _, rows, _ = source_ref.shape
    for s, source in enumerate(sources(layer_axis, own, layers, rows, sensors_ref, (0, 1))):
        source_ref[s] = source


def diffuse(fixed_ref, low, state, kept):
    layers = state.shape[0]
    span, inner = slice(low, low + layers), slice(low + 1, low + layers - 1)
    weighted = fixed_ref[3, span] * state
    across = weighted[1:-1]
    flux = fixed_ref[0, inner] * (pltpu.roll(across, across.shape[2] - 1, 2) - across)
    change = (flux - pltpu.roll(flux, 1, 2))[:, :, kept]
    weighted, across = weighted[:, :, kept], across[:, :, kept]
    col = iota(across.shape, 3)
    rolled = pltpu.roll(across, LANES - 1, 3)
    flux = fixed_ref[1, inner, :, kept] * (jnp.where(col == LANES - 1, swap(rolled), rolled) - across)
    rolled = pltpu.roll(flux, 1, 3)
    change = change + (flux - jnp.where(col == 0, swap(rolled), rolled))
    flux = fixed_ref[2, low : low + layers - 1, :, kept] * (weighted[1:] - weighted[:-1])
    change = change + (flux[1:] - flux[:-1])
    return state[1:-1, :, kept] + change


def refine(state, rate, counts, tiles):
    size = 8
    shape = state.shape[:2] + (size, LANES)
    row, col = iota(shape, 2), iota(shape, 3)
    pieces = range(state.shape[2] // size)
    at_rows = [slice(p * size, (p + 1) * size) for p in pieces]
    rates = [rate[:, :, r] for r in at_rows]
    keeps = [1.0 - 4.0 * r for r in rates]
    limits = [counts[:, :, r] for r in at_rows]
    now = [state[:, :, r] for r in at_rows]
    for turn in range(MAXSUB):
        scaled = [rates[p] * now[p] for p in pieces]
        later = list(now)
        for tile in tiles:
            ups = {p: pltpu.roll(scaled[p], size - 1, 2) for p in tile}
            downs = {p: pltpu.roll(scaled[p], 1, 2) for p in tile}
            for p in tile:
                v = scaled[p]
                near = jnp.where(row == size - 1, ups[p + 1] if p + 1 in tile else v, ups[p])
                near = near + jnp.where(row == 0, downs[p - 1] if p - 1 in tile else v, downs[p])
                near = near + jnp.where(col == LANES - 1, v, pltpu.roll(v, LANES - 1, 3))
                near = near + jnp.where(col == 0, v, pltpu.roll(v, 1, 3))
                after = keeps[p] * now[p] + near
                later[p] = after if turn == 0 else jnp.where(limits[p] > turn, after, now[p])
        now = later
    return jnp.concatenate(now, axis=2)


def two_steps(last, counts_ref, state_ref, fixed_ref, over_ref, under_ref, between_ref, *refs):
    if last:
        sens_ref, state_out, sens_out = refs
    else:
        rest_ref, state_out, up_out, down_out, sens_out = refs
    layers, _, rows, _ = state_ref.shape
    total = fixed_ref.shape[1]
    own = total // 3
    low = (total - layers) // 2
    half = rows // 2
    mine = slice(half, half + rows)
    everything = slice(0, 2 * rows)

    def deep(field, at):
        return jnp.concatenate([unfold(over_ref[at]), field, unfold(under_ref[at])], axis=2)

    def sensed(state, first_row):
        keep = slice((state.shape[0] - own) // 2, (state.shape[0] - own) // 2 + own)
        return fixed_ref[3, own : 2 * own, 0, mine] * state[keep, 0, first_row : first_row + rows]

    state = diffuse(fixed_ref, low, deep(state_ref[...], 0), everything)
    state = refine(state, fixed_ref[4, low + 1 : low + layers - 1], counts_ref[...][None], ((0,), (1, 2), (3,)))
    sens = sensed(state, half)
    if last:
        sens = sens_ref[...] + sens
    state = state + deep(between_ref[low : low + layers], 1)[1:-1]
    state = diffuse(fixed_ref, low + 1, state, mine)
    halves = slice(0, 1) if last else slice(0, 2)
    inner = slice(low + 2, low + layers - 2)
    state = refine(state[:, halves], fixed_ref[4, inner, halves, mine], counts_ref[halves, mine][None], ((0, 1),))
    sens_out[...] = sens + sensed(state, 0)
    if last:
        state_out[...] = state[:, 0]
        return
    state = state + rest_ref[1, inner]
    state_out[...] = state
    send_rows(state, rest_ref[0, inner], up_out, down_out)


def shift(cells, axis, by, wrap):
    count = lax.axis_size(axis)
    pairs = [(i, (i + by) % count) for i in range(count) if wrap or 0 <= i + by < count]
    return lax.ppermute(cells, axis, pairs)


def body(adjoint_final, conductivity, step_ratio, refine_rate, residual, sensor_tile, sensor_cell, substeps):
    own, rows, cols = adjoint_final.shape
    layers = 3 * own
    n_y = lax.axis_size("gy")
    tiles = lax.axis_size("gx") * n_y
    listed = sensor_tile.shape[0]
    fields, message = call(functools.partial(pack, n_y), [(FIELDS, own, rows, cols), (tiles, LANES)], grant=WHOLE)(
        residual,
        sensor_tile.reshape(1, listed),
        sensor_cell.reshape(1, listed),
        adjoint_final,
        conductivity,
        step_ratio,
        refine_rate,
    )
    below = shift(fields, "gz", 1, False)
    above = shift(fields, "gz", -1, False)
    sensors = lax.all_to_all(message, ("gx", "gy"), 0, 0, tiled=True)
    packed = (pl.cdiv(len(needed(layers)), PIECES), rows, LANES)
    to_left, to_right = call(pack_columns, [packed, packed])(below, fields, above)
    from_left = shift(to_right, "gy", 1, False)
    from_right = shift(to_left, "gy", -1, False)
    block = (layers, 2, rows, LANES)
    halo = (layers + layers // 2, rows // 2, LANES)
    state, fixed, up, down = call(prepare, [block, (5,) + block, (5,) + halo, (5,) + halo])(
        below, fields, above, from_left, from_right
    )
    over = shift(down, "gx", 1, True)
    under = shift(up, "gx", -1, True)
    first_state, second, up, down = call(
        functools.partial(first_sources, "gz", own), [block, block, (2,) + halo, (2,) + halo]
    )(state, sensors)
    fixed, counts = call(
        functools.partial(conduct, ("gx", "gy")), [(5, layers, 2, 2 * rows, LANES), (2, 2 * rows, LANES)]
    )(substeps.T, fixed, over, under)
    (rest,) = call(functools.partial(other_sources, "gz", own), [(2,) + block])(sensors)
    over = shift(down, "gx", 1, True)
    under = shift(up, "gx", -1, True)
    depth = layers - 4
    halo = (2, depth + depth // 2, rows // 2, LANES)
    state, up, down, sens = call(
        functools.partial(two_steps, False), [(depth, 2, rows, LANES), halo, halo, (own, rows, cols)]
    )(counts, first_state, fixed, over, under, second, rest)
    over = shift(down, "gx", 1, True)
    under = shift(up, "gx", -1, True)
    return tuple(
        call(functools.partial(two_steps, True), [(own, rows, cols), (own, rows, cols)])(
            counts, state, fixed, over, under, rest[0], sens
        )
    )


def solution(mesh):
    return jax.shard_map(
        body,
        mesh=mesh,
        in_specs=(
            P("gz", "gx", "gy"),
            P(None, "gz", "gx", "gy"),
            P("gz", "gx", "gy"),
            P("gz", "gx", "gy"),
            P(None, ("gx", "gy")),
            P(("gx", "gy")),
            P(("gx", "gy")),
            P(),
        ),
        out_specs=(P("gz", "gx", "gy"), P("gz", "gx", "gy")),
        check_vma=False,
    )
```

```python
import functools

import jax
import jax.numpy as jnp
from jax import lax
from jax.experimental import pallas as pl
from jax.experimental.pallas import tpu as pltpu
from jax.sharding import PartitionSpec as P


F32 = jnp.float32
BF16 = jnp.bfloat16
LANES = 128
WIDE = 24
PIECES = LANES // WIDE
MAXSUB = 6
SLOTS = 4
FIELDS = 6
TINY = 1e-30
LIMIT = 24 * 2**20
WHOLE = 66_800_000


def iota(shape, dim):
    return lax.broadcasted_iota(jnp.int32, shape, dim)


def harmonic(first, second):
    return 2.0 * first * second / jnp.maximum(first + second, TINY)


def swap(field):
    return jnp.concatenate([field[:, 1:2], field[:, 0:1]], axis=1)


def call(kernel, outs, cost=20000, grant=LIMIT):
    vmem = pl.BlockSpec(memory_space=pltpu.VMEM)

    def run(*args):
        return pl.pallas_call(
            kernel,
            out_shape=[jax.ShapeDtypeStruct(o, F32) for o in outs],
            in_specs=[vmem] * len(args),
            out_specs=[vmem] * len(outs),
            compiler_params=pltpu.CompilerParams(vmem_limit_bytes=grant),
            cost_estimate=pl.CostEstimate(flops=cost, bytes_accessed=cost, transcendentals=0),
        )(*args)

    return run


def pack(gy, residual_ref, tile_ref, cell_ref, adjoint_ref, conductivity_ref, ratio_ref, rate_ref, fields_ref, out_ref):
    fields_ref[0] = adjoint_ref[...]
    fields_ref[1:4] = conductivity_ref[...]
    fields_ref[4] = ratio_ref[...]
    fields_ref[5] = rate_ref[...]
    count = residual_ref.shape[1]
    tiles = out_ref.shape[0]
    eye = iota((count, count), 0) == iota((count, count), 1)

    def column(row):
        return jnp.sum(jnp.where(eye, jnp.broadcast_to(row, (count, count)), 0.0), axis=1, keepdims=True)

    named = tile_ref[...]
    tile_row = named.astype(F32)
    tile_col = column(tile_row)
    same = (tile_col == tile_row) & (iota((count, count), 1) < iota((count, count), 0))
    rank = jnp.sum(same.astype(F32), axis=1, keepdims=True).astype(jnp.int32)
    values = [column(residual_ref[s : s + 1, :]) for s in range(4)]
    values.append(column(cell_ref[...].astype(F32) + 1.0))
    lane = iota((count, LANES), 1)
    within = lane % 8
    spread = jnp.zeros((count, LANES), F32)
    for place, value in enumerate(values):
        spread = jnp.where(within == place, value, spread)
    spread = jnp.where((lane % 32) // 8 == rank, spread, 0.0)
    tile_at = iota((tiles, count), 0)
    total = jnp.zeros((tiles, LANES), F32)
    for group, (step, edge) in enumerate(((0, -1), (-1, 0), (1, gy - 1))):
        hit = (named == tile_at + step) & (tile_at % gy != edge)
        part = jnp.where(lane // 32 == group, spread, 0.0)
        total = total + jnp.dot(hit.astype(F32), part, precision=lax.Precision.HIGHEST, preferred_element_type=F32)
    out_ref[...] = total


def needed(layers):
    return [(f, l) for f in range(FIELDS) for l in range(layers) if f in (0, 3, 4) or 0 < l < layers - 1]


def stacked(refs, field, layer):
    each = refs[0].shape[1]
    return refs[layer // each][field, layer % each]


def pack_columns(below_ref, own_ref, above_ref, left_ref, right_ref, up_ref, down_ref):
    refs = (below_ref, own_ref, above_ref)
    layers = 3 * own_ref.shape[1]
    rows = own_ref.shape[2]
    piece = iota((rows, LANES), 1) // WIDE
    planes = needed(layers)
    for j in range(left_ref.shape[0]):
        left = right = None
        for q, (f, l) in enumerate(planes[j * PIECES : (j + 1) * PIECES]):
            plane = stacked(refs, f, l)
            to_left = plane if q == 0 else pltpu.roll(plane, WIDE * q, 1)
            to_right = pltpu.roll(plane, WIDE * q + WIDE, 1)
            left = to_left if q == 0 else jnp.where(piece == q, to_left, left)
            right = to_right if q == 0 else jnp.where(piece == q, to_right, right)
        left_ref[j] = left
        right_ref[j] = right
    for f in range(1, FIELDS):
        for l in range(layers):
            plane = stacked(refs, f, l)
            up_ref[f - 1, l] = plane[: rows // 2]
            down_ref[f - 1, l] = plane[rows // 2 :]


def spread_column(columns, at, shape):
    return jnp.broadcast_to(columns[:, at : at + 1], shape)


def sources(layer_axis, own, layers, rows, sensors_ref, steps):
    got = sensors_ref[...]
    blocks = got.shape[0]
    lane = iota((blocks, LANES), 1)
    lane_at = lane.astype(F32)
    cell = got.astype(jnp.int32) - 1
    row_base = (lax.axis_index(layer_axis) * own - own) * rows
    cell_row = ((cell >> 7) - row_base).astype(F32).T
    cell_col = cell & (LANES - 1)
    half = LANES // 2
    group_of = lane // 32
    cell_col = jnp.where(
        group_of == 0,
        cell_col,
        jnp.where(
            group_of == 1,
            jnp.where(cell_col >= LANES - WIDE, cell_col - half, -LANES),
            jnp.where(cell_col < WIDE, cell_col, -LANES),
        ),
    ).astype(F32)
    row_at = iota((layers * rows, blocks), 0).astype(F32)
    high = got.astype(BF16)
    values = (high, (got - high.astype(F32)).astype(BF16))
    onehots, tables = ([], []), ([], [])
    for group in range(3):
        for slot in range(SLOTS):
            base = group * 32 + slot * 8
            onehots[group > 0].append((cell_row[base + 4 : base + 5, :] == row_at).astype(F32).astype(BF16))
            at = spread_column(cell_col, base + 4, lane.shape)
            pairs = (0, half) if group > 0 and len(steps) > 1 else (0,)
            place = [(at == lane_at - by).astype(F32).astype(BF16) for by in pairs]
            line = []
            for part in range(2):
                cells = [spread_column(values[part], base + s, lane.shape) for s in steps]
                for k in range(0, len(cells), len(place)):
                    line.append(functools.reduce(jnp.add, [m * v for m, v in zip(place, cells[k : k + len(place)])]))
            tables[group > 0].append(jnp.concatenate(line, axis=1))
    sums = []
    for onehot, table in zip(onehots, tables):
        both = jnp.dot(jnp.concatenate(onehot, axis=1), jnp.concatenate(table, axis=0), preferred_element_type=F32)
        width = both.shape[1] // 2
        sums.append(both[:, :width] + both[:, width:])
    centre, side = sums
    lane = iota((layers * rows, LANES), 1)
    out = []
    for s in range(len(steps)):
        tile = side[:, (s // 2) * LANES : (s // 2 + 1) * LANES]
        turned = pltpu.roll(tile, half, 1)
        right, left = (tile, turned) if s % 2 == 0 else (turned, tile)
        beside = jnp.where(lane < WIDE, right, jnp.where(lane >= LANES - WIDE, left, 0.0))
        parts = [m.reshape(layers, 1, rows, LANES) for m in (centre[:, s * LANES : (s + 1) * LANES], beside)]
        out.append(jnp.concatenate(parts, axis=1))
    return out


def prepare(below_ref, own_ref, above_ref, left_ref, right_ref, state_ref, fixed_ref, up_ref, down_ref):
    refs = (below_ref, own_ref, above_ref)
    own = own_ref.shape[1]
    layers = 3 * own
    rows = own_ref.shape[2]
    lane = iota((rows, LANES), 1)

    listed = {plane: at for at, plane in enumerate(needed(layers))}

    def field(f):
        planes = []
        for l in range(layers):
            if (f, l) in listed:
                j, q = divmod(listed[f, l], PIECES)
                from_left = pltpu.roll(left_ref[j], (LANES - WIDE - WIDE * q) % LANES, 1)
                from_right = pltpu.roll(right_ref[j], LANES - WIDE * q, 1) if q != 0 else right_ref[j]
                side = jnp.where(lane < WIDE, from_right, jnp.where(lane >= LANES - WIDE, from_left, 0.0))
            else:
                side = jnp.zeros((rows, LANES), F32)
            planes.append(jnp.stack([stacked(refs, f, l), side], axis=0))
        return jnp.stack(planes, axis=0)

    state_ref[...] = field(0)
    half = rows // 2
    for f in range(1, FIELDS):
        values = field(f)
        fixed_ref[f - 1] = values
        up_ref[f - 1] = fold_side(values[:, 1, :half])
        down_ref[f - 1] = fold_side(values[:, 1, half:])


def fold_side(side):
    half = side.shape[0] // 2
    lane = iota((half,) + side.shape[1:], 2)
    used = (lane < WIDE) | (lane >= LANES - WIDE)
    low, high = (jnp.where(used, part, 0.0) for part in (side[:half], side[half:]))
    return low + pltpu.roll(high, LANES // 2, 2)


def unfold_side(shared):
    lane = iota(shared.shape, 2)
    used = (lane < WIDE) | (lane >= LANES - WIDE)
    parts = [jnp.where(used, part, 0.0) for part in (shared, pltpu.roll(shared, LANES // 2, 2))]
    return jnp.concatenate(parts, axis=0)


def fold(block):
    return jnp.concatenate([block[:, 0], fold_side(block[:, 1])], axis=0)


def unfold(folded):
    layers = folded.shape[0] * 2 // 3
    return jnp.stack([folded[:layers], unfold_side(folded[layers:])], axis=1)


def conduct(axes, substeps_ref, own_ref, over_ref, under_ref, over_side_ref, under_side_ref, fixed_ref, counts_ref):
    at_x, at_y = (lax.axis_index(axis) for axis in axes)
    n_y, n_x = substeps_ref.shape
    named = substeps_ref[...].astype(F32)
    size = own_ref.shape[3] // 2
    lane = iota((size, LANES), 1)

    def count(x, y):
        hit = (iota((n_y, n_x), 1) == x) & (iota((n_y, n_x), 0) == y)
        found = jnp.sum(jnp.where(hit, named, 0.0), axis=1, keepdims=True)
        return jnp.broadcast_to(jnp.sum(found, axis=0, keepdims=True), (size, LANES))

    for part, x in enumerate((at_x - 1, at_x, at_x, at_x + 1)):
        at_rows = slice(part * size, (part + 1) * size)
        counts_ref[0, at_rows] = count(x, at_y)
        counts_ref[1, at_rows] = jnp.where(lane < LANES // 2, count(x, at_y + 1), count(x, at_y - 1))

    pairs = own_ref.shape[1] // 2
    first = over_side_ref.shape[0] - 5 * pairs

    def deep(f, masked=False):
        over, under = (
            jnp.stack([centre[f], unfold_side(side[first + f * pairs : first + (f + 1) * pairs])], axis=1)
            for centre, side in ((over_ref, over_side_ref), (under_ref, under_side_ref))
        )
        if masked:
            over = jnp.where(at_x > 0, over, 0.0)
            under = jnp.where(at_x < n_x - 1, under, 0.0)
        return jnp.concatenate([over, own_ref[f], under], axis=2)

    along_rows = deep(0, True)
    shape = along_rows.shape
    layers, _, rows, _ = shape
    row = iota(shape, 2)
    col = iota(shape, 3)
    fixed_ref[0] = harmonic(along_rows, jnp.where(row == rows - 1, 0.0, pltpu.roll(along_rows, rows - 1, 2)))
    along_cols = deep(1)
    rolled = pltpu.roll(along_cols, LANES - 1, 3)
    fixed_ref[1] = harmonic(along_cols, jnp.where(col == LANES - 1, swap(rolled), rolled))
    along_layers = deep(2)
    fixed_ref[2, : layers - 1] = harmonic(along_layers[: layers - 1], along_layers[1:])
    fixed_ref[2, layers - 1 :] = jnp.zeros((1,) + shape[1:], F32)
    fixed_ref[3] = deep(3)
    fixed_ref[4] = deep(4)


def send_rows(state, source, up_ref, down_ref):
    half = state.shape[2] // 2
    size = state.shape[0] + state.shape[0] // 2
    for ref, rows in ((up_ref, slice(0, half)), (down_ref, slice(half, 2 * half))):
        ref[:size] = fold(state[:, :, rows])
        ref[size : 2 * size] = fold(source[:, :, rows])


def first_sources(layer_axis, own, state_in, sensors_ref, up_side_ref, down_side_ref, state_ref, source_ref, up_ref, down_ref):
    layers, _, rows, _ = state_ref.shape
    second, first = sources(layer_axis, own, layers, rows, sensors_ref, (2, 3))
    state = state_in[...] + first
    state_ref[...] = state
    source_ref[...] = second
    send_rows(state, second, up_ref, down_ref)
    count, pairs = up_side_ref.shape[:2]
    base = up_ref.shape[0] - count * pairs
    for f in range(count):
        up_ref[base + f * pairs : base + (f + 1) * pairs] = up_side_ref[f]
        down_ref[base + f * pairs : base + (f + 1) * pairs] = down_side_ref[f]


def other_sources(layer_axis, own, sensors_ref, source_ref):
    _, layers, _, rows, _ = source_ref.shape
    for s, source in enumerate(sources(layer_axis, own, layers, rows, sensors_ref, (0, 1))):
        source_ref[s] = source


def diffuse(fixed_ref, low, state, kept):
    layers = state.shape[0]
    span, inner = slice(low, low + layers), slice(low + 1, low + layers - 1)
    weighted = fixed_ref[3, span] * state
    across = weighted[1:-1]
    flux = fixed_ref[0, inner] * (pltpu.roll(across, across.shape[2] - 1, 2) - across)
    change = (flux - pltpu.roll(flux, 1, 2))[:, :, kept]
    weighted, across = weighted[:, :, kept], across[:, :, kept]
    col = iota(across.shape, 3)
    rolled = pltpu.roll(across, LANES - 1, 3)
    flux = fixed_ref[1, inner, :, kept] * (jnp.where(col == LANES - 1, swap(rolled), rolled) - across)
    rolled = pltpu.roll(flux, 1, 3)
    change = change + (flux - jnp.where(col == 0, swap(rolled), rolled))
    flux = fixed_ref[2, low : low + layers - 1, :, kept] * (weighted[1:] - weighted[:-1])
    change = change + (flux[1:] - flux[:-1])
    return state[1:-1, :, kept] + change


def refine(state, rate, counts, tiles):
    size = 8
    shape = state.shape[:2] + (size, LANES)
    row, col = iota(shape, 2), iota(shape, 3)
    pieces = range(state.shape[2] // size)
    at_rows = [slice(p * size, (p + 1) * size) for p in pieces]
    rates = [rate[:, :, r] for r in at_rows]
    keeps = [1.0 - 4.0 * r for r in rates]
    limits = [counts[:, :, r] for r in at_rows]
    now = [state[:, :, r] for r in at_rows]
    for turn in range(MAXSUB):
        scaled = [rates[p] * now[p] for p in pieces]
        later = list(now)
        for tile in tiles:
            ups = {p: pltpu.roll(scaled[p], size - 1, 2) for p in tile}
            downs = {p: pltpu.roll(scaled[p], 1, 2) for p in tile}
            for p in tile:
                v = scaled[p]
                near = jnp.where(row == size - 1, ups[p + 1] if p + 1 in tile else v, ups[p])
                near = near + jnp.where(row == 0, downs[p - 1] if p - 1 in tile else v, downs[p])
                near = near + jnp.where(col == LANES - 1, v, pltpu.roll(v, LANES - 1, 3))
                near = near + jnp.where(col == 0, v, pltpu.roll(v, 1, 3))
                after = keeps[p] * now[p] + near
                later[p] = after if turn == 0 else jnp.where(limits[p] > turn, after, now[p])
        now = later
    return jnp.concatenate(now, axis=2)


def two_steps(last, counts_ref, state_ref, fixed_ref, over_ref, under_ref, between_ref, *refs):
    if last:
        sens_ref, state_out, sens_out = refs
    else:
        rest_ref, state_out, up_out, down_out, sens_out = refs
    layers, _, rows, _ = state_ref.shape
    total = fixed_ref.shape[1]
    own = total // 3
    low = (total - layers) // 2
    half = rows // 2
    mine = slice(half, half + rows)
    everything = slice(0, 2 * rows)

    def deep(field, at):
        size = layers + layers // 2
        over, under = (unfold(ref[at * size : (at + 1) * size]) for ref in (over_ref, under_ref))
        return jnp.concatenate([over, field, under], axis=2)

    def sensed(state, first_row):
        keep = slice((state.shape[0] - own) // 2, (state.shape[0] - own) // 2 + own)
        return fixed_ref[3, own : 2 * own, 0, mine] * state[keep, 0, first_row : first_row + rows]

    state = diffuse(fixed_ref, low, deep(state_ref[...], 0), everything)
    state = refine(state, fixed_ref[4, low + 1 : low + layers - 1], counts_ref[...][None], ((0,), (1, 2), (3,)))
    sens = sensed(state, half)
    if last:
        sens = sens_ref[...] + sens
    state = state + deep(between_ref[low : low + layers], 1)[1:-1]
    state = diffuse(fixed_ref, low + 1, state, mine)
    halves = slice(0, 1) if last else slice(0, 2)
    inner = slice(low + 2, low + layers - 2)
    state = refine(state[:, halves], fixed_ref[4, inner, halves, mine], counts_ref[halves, mine][None], ((0, 1),))
    sens_out[...] = sens + sensed(state, 0)
    if last:
        state_out[...] = state[:, 0]
        return
    state = state + rest_ref[1, inner]
    state_out[...] = state
    send_rows(state, rest_ref[0, inner], up_out, down_out)


def shift(cells, axis, by, wrap):
    count = lax.axis_size(axis)
    pairs = [(i, (i + by) % count) for i in range(count) if wrap or 0 <= i + by < count]
    return lax.ppermute(cells, axis, pairs)


def body(adjoint_final, conductivity, step_ratio, refine_rate, residual, sensor_tile, sensor_cell, substeps):
    own, rows, cols = adjoint_final.shape
    layers = 3 * own
    n_y = lax.axis_size("gy")
    tiles = lax.axis_size("gx") * n_y
    listed = sensor_tile.shape[0]
    fields, message = call(functools.partial(pack, n_y), [(FIELDS, own, rows, cols), (tiles, LANES)], grant=WHOLE)(
        residual,
        sensor_tile.reshape(1, listed),
        sensor_cell.reshape(1, listed),
        adjoint_final,
        conductivity,
        step_ratio,
        refine_rate,
    )
    below = shift(fields, "gz", 1, False)
    above = shift(fields, "gz", -1, False)
    sensors = lax.all_to_all(message, ("gx", "gy"), 0, 0, tiled=True)
    packed = (pl.cdiv(len(needed(layers)), PIECES), rows, LANES)
    block = (layers, 2, rows, LANES)
    lines = (rows // 2, LANES)
    centre = (5, layers) + lines
    to_left, to_right, up, down = call(pack_columns, [packed, packed, centre, centre])(below, fields, above)
    from_left = shift(to_right, "gy", 1, False)
    from_right = shift(to_left, "gy", -1, False)
    over_fixed = shift(down, "gx", 1, True)
    under_fixed = shift(up, "gx", -1, True)
    side = (5, layers // 2) + lines
    state, fixed, up, down = call(prepare, [block, (5,) + block, side, side])(
        below, fields, above, from_left, from_right
    )
    halo = (2 * (layers + layers // 2) + 5 * (layers // 2),) + lines
    first_state, second, up, down = call(
        functools.partial(first_sources, "gz", own), [block, block, halo, halo]
    )(state, sensors, up, down)
    (rest,) = call(functools.partial(other_sources, "gz", own), [(2,) + block])(sensors)
    over = shift(down, "gx", 1, True)
    under = shift(up, "gx", -1, True)
    fixed, counts = call(
        functools.partial(conduct, ("gx", "gy")), [(5, layers, 2, 2 * rows, LANES), (2, 2 * rows, LANES)]
    )(substeps.T, fixed, over_fixed, under_fixed, over, under)
    depth = layers - 4
    halo = (2 * (depth + depth // 2),) + lines
    state, up, down, sens = call(
        functools.partial(two_steps, False), [(depth, 2, rows, LANES), halo, halo, (own, rows, cols)]
    )(counts, first_state, fixed, over, under, second, rest)
    over = shift(down, "gx", 1, True)
    under = shift(up, "gx", -1, True)
    return tuple(
        call(functools.partial(two_steps, True), [(own, rows, cols), (own, rows, cols)])(
            counts, state, fixed, over, under, rest[0], sens
        )
    )


def solution(mesh):
    return jax.shard_map(
        body,
        mesh=mesh,
        in_specs=(
            P("gz", "gx", "gy"),
            P(None, "gz", "gx", "gy"),
            P("gz", "gx", "gy"),
            P("gz", "gx", "gy"),
            P(None, ("gx", "gy")),
            P(("gx", "gy")),
            P(("gx", "gy")),
            P(),
        ),
        out_specs=(P("gz", "gx", "gy"), P("gz", "gx", "gy")),
        check_vma=False,
    )
```

```python
import functools

import jax
import jax.numpy as jnp
from jax import lax
from jax.experimental import pallas as pl
from jax.experimental.pallas import tpu as pltpu
from jax.sharding import PartitionSpec as P


F32 = jnp.float32
BF16 = jnp.bfloat16
LANES = 128
WIDE = 24
PIECES = LANES // WIDE
MAXSUB = 6
SLOTS = 4
FIELDS = 6
TINY = 1e-30
LIMIT = 24 * 2**20
WHOLE = 66_800_000


def iota(shape, dim):
    return lax.broadcasted_iota(jnp.int32, shape, dim)


def harmonic(first, second):
    return 2.0 * first * second / jnp.maximum(first + second, TINY)


def swap(field):
    return jnp.concatenate([field[:, 1:2], field[:, 0:1]], axis=1)


def call(kernel, outs, cost=20000, grant=LIMIT):
    vmem = pl.BlockSpec(memory_space=pltpu.VMEM)

    def run(*args):
        return pl.pallas_call(
            kernel,
            out_shape=[jax.ShapeDtypeStruct(o, F32) for o in outs],
            in_specs=[vmem] * len(args),
            out_specs=[vmem] * len(outs),
            compiler_params=pltpu.CompilerParams(vmem_limit_bytes=grant),
            cost_estimate=pl.CostEstimate(flops=cost, bytes_accessed=cost, transcendentals=0),
        )(*args)

    return run


def pack(gy, residual_ref, tile_ref, cell_ref, adjoint_ref, conductivity_ref, ratio_ref, rate_ref, fields_ref, out_ref):
    fields_ref[0] = adjoint_ref[...]
    fields_ref[1:4] = conductivity_ref[...]
    fields_ref[4] = ratio_ref[...]
    fields_ref[5] = rate_ref[...]
    count = residual_ref.shape[1]
    tiles = out_ref.shape[0]
    eye = iota((count, count), 0) == iota((count, count), 1)

    def column(row):
        return jnp.sum(jnp.where(eye, jnp.broadcast_to(row, (count, count)), 0.0), axis=1, keepdims=True)

    named = tile_ref[...]
    tile_row = named.astype(F32)
    tile_col = column(tile_row)
    same = (tile_col == tile_row) & (iota((count, count), 1) < iota((count, count), 0))
    rank = jnp.sum(same.astype(F32), axis=1, keepdims=True).astype(jnp.int32)
    values = [column(residual_ref[s : s + 1, :]) for s in range(4)]
    values.append(column(cell_ref[...].astype(F32) + 1.0))
    lane = iota((count, LANES), 1)
    within = lane % 8
    spread = jnp.zeros((count, LANES), F32)
    for place, value in enumerate(values):
        spread = jnp.where(within == place, value, spread)
    spread = jnp.where((lane % 32) // 8 == rank, spread, 0.0)
    tile_at = iota((tiles, count), 0)
    total = jnp.zeros((tiles, LANES), F32)
    for group, (step, edge) in enumerate(((0, -1), (-1, 0), (1, gy - 1))):
        hit = (named == tile_at + step) & (tile_at % gy != edge)
        part = jnp.where(lane // 32 == group, spread, 0.0)
        total = total + jnp.dot(hit.astype(F32), part, precision=lax.Precision.HIGHEST, preferred_element_type=F32)
    out_ref[...] = total


def needed(layers):
    return [(f, l) for f in range(FIELDS) for l in range(layers) if f in (0, 3, 4) or 0 < l < layers - 1]


def stacked(refs, field, layer):
    each = refs[0].shape[1]
    return refs[layer // each][field, layer % each]


def pack_columns(below_ref, own_ref, above_ref, left_ref, right_ref, up_ref, down_ref):
    refs = (below_ref, own_ref, above_ref)
    layers = 3 * own_ref.shape[1]
    rows = own_ref.shape[2]
    piece = iota((rows, LANES), 1) // WIDE
    planes = needed(layers)
    for j in range(left_ref.shape[0]):
        left = right = None
        for q, (f, l) in enumerate(planes[j * PIECES : (j + 1) * PIECES]):
            plane = stacked(refs, f, l)
            to_left = plane if q == 0 else pltpu.roll(plane, WIDE * q, 1)
            to_right = pltpu.roll(plane, WIDE * q + WIDE, 1)
            left = to_left if q == 0 else jnp.where(piece == q, to_left, left)
            right = to_right if q == 0 else jnp.where(piece == q, to_right, right)
        left_ref[j] = left
        right_ref[j] = right
    for f in range(1, FIELDS):
        for l in range(layers):
            plane = stacked(refs, f, l)
            up_ref[f - 1, l] = plane[: rows // 2]
            down_ref[f - 1, l] = plane[rows // 2 :]


def spread_column(columns, at, shape):
    return jnp.broadcast_to(columns[:, at : at + 1], shape)


def sources(layer_axis, own, layers, rows, sensors_ref, steps):
    got = sensors_ref[...]
    blocks = got.shape[0]
    lane = iota((blocks, LANES), 1)
    lane_at = lane.astype(F32)
    cell = got.astype(jnp.int32) - 1
    row_base = (lax.axis_index(layer_axis) * own - own) * rows
    cell_row = ((cell >> 7) - row_base).astype(F32).T
    cell_col = cell & (LANES - 1)
    half = LANES // 2
    group_of = lane // 32
    cell_col = jnp.where(
        group_of == 0,
        cell_col,
        jnp.where(
            group_of == 1,
            jnp.where(cell_col >= LANES - WIDE, cell_col - half, -LANES),
            jnp.where(cell_col < WIDE, cell_col, -LANES),
        ),
    ).astype(F32)
    row_at = iota((layers * rows, blocks), 0).astype(F32)
    high = got.astype(BF16)
    values = (high, (got - high.astype(F32)).astype(BF16))
    onehots, tables = ([], []), ([], [])
    for group in range(3):
        for slot in range(SLOTS):
            base = group * 32 + slot * 8
            onehots[group > 0].append((cell_row[base + 4 : base + 5, :] == row_at).astype(F32).astype(BF16))
            at = spread_column(cell_col, base + 4, lane.shape)
            pairs = (0, half) if group > 0 and len(steps) > 1 else (0,)
            place = [(at == lane_at - by).astype(F32).astype(BF16) for by in pairs]
            line = []
            for part in range(2):
                cells = [spread_column(values[part], base + s, lane.shape) for s in steps]
                for k in range(0, len(cells), len(place)):
                    line.append(functools.reduce(jnp.add, [m * v for m, v in zip(place, cells[k : k + len(place)])]))
            tables[group > 0].append(jnp.concatenate(line, axis=1))
    sums = []
    for onehot, table in zip(onehots, tables):
        both = jnp.dot(jnp.concatenate(onehot, axis=1), jnp.concatenate(table, axis=0), preferred_element_type=F32)
        width = both.shape[1] // 2
        sums.append(both[:, :width] + both[:, width:])
    centre, side = sums
    lane = iota((layers * rows, LANES), 1)
    out = []
    for s in range(len(steps)):
        tile = side[:, (s // 2) * LANES : (s // 2 + 1) * LANES]
        turned = pltpu.roll(tile, half, 1)
        right, left = (tile, turned) if s % 2 == 0 else (turned, tile)
        beside = jnp.where(lane < WIDE, right, jnp.where(lane >= LANES - WIDE, left, 0.0))
        parts = [m.reshape(layers, 1, rows, LANES) for m in (centre[:, s * LANES : (s + 1) * LANES], beside)]
        out.append(jnp.concatenate(parts, axis=1))
    return out


def prepare(below_ref, own_ref, above_ref, left_ref, right_ref, state_ref, fixed_ref, up_ref, down_ref):
    refs = (below_ref, own_ref, above_ref)
    own = own_ref.shape[1]
    layers = 3 * own
    rows = own_ref.shape[2]
    lane = iota((rows, LANES), 1)

    listed = {plane: at for at, plane in enumerate(needed(layers))}

    def field(f):
        planes = []
        for l in range(layers):
            if (f, l) in listed:
                j, q = divmod(listed[f, l], PIECES)
                from_left = pltpu.roll(left_ref[j], (LANES - WIDE - WIDE * q) % LANES, 1)
                from_right = pltpu.roll(right_ref[j], LANES - WIDE * q, 1) if q != 0 else right_ref[j]
                side = jnp.where(lane < WIDE, from_right, jnp.where(lane >= LANES - WIDE, from_left, 0.0))
            else:
                side = jnp.zeros((rows, LANES), F32)
            planes.append(jnp.stack([stacked(refs, f, l), side], axis=0))
        return jnp.stack(planes, axis=0)

    state_ref[...] = field(0)
    half = rows // 2
    for f in range(1, FIELDS):
        values = field(f)
        fixed_ref[f - 1] = values
        up_ref[f - 1] = fold_side(values[:, 1, :half])
        down_ref[f - 1] = fold_side(values[:, 1, half:])


def fold_side(side):
    half = side.shape[0] // 2
    lane = iota((half,) + side.shape[1:], 2)
    used = (lane < WIDE) | (lane >= LANES - WIDE)
    low, high = (jnp.where(used, part, 0.0) for part in (side[:half], side[half:]))
    return low + pltpu.roll(high, LANES // 2, 2)


def unfold_side(shared):
    lane = iota(shared.shape, 2)
    used = (lane < WIDE) | (lane >= LANES - WIDE)
    parts = [jnp.where(used, part, 0.0) for part in (shared, pltpu.roll(shared, LANES // 2, 2))]
    return jnp.concatenate(parts, axis=0)


def fold(block):
    return jnp.concatenate([block[:, 0], fold_side(block[:, 1])], axis=0)


def unfold(folded):
    layers = folded.shape[0] * 2 // 3
    return jnp.stack([folded[:layers], unfold_side(folded[layers:])], axis=1)


def conduct(axes, substeps_ref, own_ref, over_ref, under_ref, over_side_ref, under_side_ref, fixed_ref, counts_ref):
    at_x, at_y = (lax.axis_index(axis) for axis in axes)
    n_y, n_x = substeps_ref.shape
    named = substeps_ref[...].astype(F32)
    size = own_ref.shape[3] // 2
    lane = iota((size, LANES), 1)

    def count(x, y):
        hit = (iota((n_y, n_x), 1) == x) & (iota((n_y, n_x), 0) == y)
        found = jnp.sum(jnp.where(hit, named, 0.0), axis=1, keepdims=True)
        return jnp.broadcast_to(jnp.sum(found, axis=0, keepdims=True), (size, LANES))

    for part, x in enumerate((at_x - 1, at_x, at_x, at_x + 1)):
        at_rows = slice(part * size, (part + 1) * size)
        counts_ref[0, at_rows] = count(x, at_y)
        counts_ref[1, at_rows] = jnp.where(lane < LANES // 2, count(x, at_y + 1), count(x, at_y - 1))

    def deep(f, masked=False):
        over, under = (
            jnp.stack([centre[f], unfold_side(side[f])], axis=1)
            for centre, side in ((over_ref, over_side_ref), (under_ref, under_side_ref))
        )
        if masked:
            over = jnp.where(at_x > 0, over, 0.0)
            under = jnp.where(at_x < n_x - 1, under, 0.0)
        return jnp.concatenate([over, own_ref[f], under], axis=2)

    along_rows = deep(0, True)
    shape = along_rows.shape
    layers, _, rows, _ = shape
    row = iota(shape, 2)
    col = iota(shape, 3)
    fixed_ref[0] = harmonic(along_rows, jnp.where(row == rows - 1, 0.0, pltpu.roll(along_rows, rows - 1, 2)))
    along_cols = deep(1)
    rolled = pltpu.roll(along_cols, LANES - 1, 3)
    fixed_ref[1] = harmonic(along_cols, jnp.where(col == LANES - 1, swap(rolled), rolled))
    along_layers = deep(2)
    fixed_ref[2, : layers - 1] = harmonic(along_layers[: layers - 1], along_layers[1:])
    fixed_ref[2, layers - 1 :] = jnp.zeros((1,) + shape[1:], F32)
    fixed_ref[3] = deep(3)
    fixed_ref[4] = deep(4)


def send_rows(state, source, up_ref, down_ref):
    half = state.shape[2] // 2
    size = state.shape[0] + state.shape[0] // 2
    for ref, rows in ((up_ref, slice(0, half)), (down_ref, slice(half, 2 * half))):
        ref[:size] = fold(state[:, :, rows])
        ref[size : 2 * size] = fold(source[:, :, rows])


def first_sources(layer_axis, own, state_in, sensors_ref, state_ref, source_ref, up_ref, down_ref):
    layers, _, rows, _ = state_ref.shape
    second, first = sources(layer_axis, own, layers, rows, sensors_ref, (2, 3))
    state = state_in[...] + first
    state_ref[...] = state
    source_ref[...] = second
    send_rows(state, second, up_ref, down_ref)


def other_sources(layer_axis, own, sensors_ref, source_ref):
    _, layers, _, rows, _ = source_ref.shape
    for s, source in enumerate(sources(layer_axis, own, layers, rows, sensors_ref, (0, 1))):
        source_ref[s] = source


def diffuse(fixed_ref, low, state, kept):
    layers = state.shape[0]
    span, inner = slice(low, low + layers), slice(low + 1, low + layers - 1)
    weighted = fixed_ref[3, span] * state
    across = weighted[1:-1]
    flux = fixed_ref[0, inner] * (pltpu.roll(across, across.shape[2] - 1, 2) - across)
    change = (flux - pltpu.roll(flux, 1, 2))[:, :, kept]
    weighted, across = weighted[:, :, kept], across[:, :, kept]
    col = iota(across.shape, 3)
    rolled = pltpu.roll(across, LANES - 1, 3)
    flux = fixed_ref[1, inner, :, kept] * (jnp.where(col == LANES - 1, swap(rolled), rolled) - across)
    rolled = pltpu.roll(flux, 1, 3)
    change = change + (flux - jnp.where(col == 0, swap(rolled), rolled))
    flux = fixed_ref[2, low : low + layers - 1, :, kept] * (weighted[1:] - weighted[:-1])
    change = change + (flux[1:] - flux[:-1])
    return state[1:-1, :, kept] + change


def refine(state, rate, counts, tiles):
    size = 8
    shape = state.shape[:2] + (size, LANES)
    row, col = iota(shape, 2), iota(shape, 3)
    pieces = range(state.shape[2] // size)
    at_rows = [slice(p * size, (p + 1) * size) for p in pieces]
    rates = [rate[:, :, r] for r in at_rows]
    keeps = [1.0 - 4.0 * r for r in rates]
    limits = [counts[:, :, r] for r in at_rows]
    now = [state[:, :, r] for r in at_rows]
    for turn in range(MAXSUB):
        scaled = [rates[p] * now[p] for p in pieces]
        later = list(now)
        for tile in tiles:
            ups = {p: pltpu.roll(scaled[p], size - 1, 2) for p in tile}
            downs = {p: pltpu.roll(scaled[p], 1, 2) for p in tile}
            for p in tile:
                v = scaled[p]
                near = jnp.where(row == size - 1, ups[p + 1] if p + 1 in tile else v, ups[p])
                near = near + jnp.where(row == 0, downs[p - 1] if p - 1 in tile else v, downs[p])
                near = near + jnp.where(col == LANES - 1, v, pltpu.roll(v, LANES - 1, 3))
                near = near + jnp.where(col == 0, v, pltpu.roll(v, 1, 3))
                after = keeps[p] * now[p] + near
                later[p] = after if turn == 0 else jnp.where(limits[p] > turn, after, now[p])
        now = later
    return jnp.concatenate(now, axis=2)


def two_steps(last, counts_ref, state_ref, fixed_ref, over_ref, under_ref, between_ref, *refs):
    if last:
        sens_ref, state_out, sens_out = refs
    else:
        rest_ref, state_out, up_out, down_out, sens_out = refs
    layers, _, rows, _ = state_ref.shape
    total = fixed_ref.shape[1]
    own = total // 3
    low = (total - layers) // 2
    half = rows // 2
    mine = slice(half, half + rows)
    everything = slice(0, 2 * rows)

    def deep(field, at):
        size = layers + layers // 2
        over, under = (unfold(ref[at * size : (at + 1) * size]) for ref in (over_ref, under_ref))
        return jnp.concatenate([over, field, under], axis=2)

    def sensed(state, first_row):
        keep = slice((state.shape[0] - own) // 2, (state.shape[0] - own) // 2 + own)
        return fixed_ref[3, own : 2 * own, 0, mine] * state[keep, 0, first_row : first_row + rows]

    state = diffuse(fixed_ref, low, deep(state_ref[...], 0), everything)
    state = refine(state, fixed_ref[4, low + 1 : low + layers - 1], counts_ref[...][None], ((0,), (1, 2), (3,)))
    sens = sensed(state, half)
    if last:
        sens = sens_ref[...] + sens
    state = state + deep(between_ref[low : low + layers], 1)[1:-1]
    state = diffuse(fixed_ref, low + 1, state, mine)
    halves = slice(0, 1) if last else slice(0, 2)
    inner = slice(low + 2, low + layers - 2)
    state = refine(state[:, halves], fixed_ref[4, inner, halves, mine], counts_ref[halves, mine][None], ((0, 1),))
    sens_out[...] = sens + sensed(state, 0)
    if last:
        state_out[...] = state[:, 0]
        return
    state = state + rest_ref[1, inner]
    state_out[...] = state
    send_rows(state, rest_ref[0, inner], up_out, down_out)


def shift(cells, axis, by, wrap):
    count = lax.axis_size(axis)
    pairs = [(i, (i + by) % count) for i in range(count) if wrap or 0 <= i + by < count]
    return lax.ppermute(cells, axis, pairs)


def body(adjoint_final, conductivity, step_ratio, refine_rate, residual, sensor_tile, sensor_cell, substeps):
    own, rows, cols = adjoint_final.shape
    layers = 3 * own
    n_y = lax.axis_size("gy")
    tiles = lax.axis_size("gx") * n_y
    listed = sensor_tile.shape[0]
    fields, message = call(functools.partial(pack, n_y), [(FIELDS, own, rows, cols), (tiles, LANES)], grant=WHOLE)(
        residual,
        sensor_tile.reshape(1, listed),
        sensor_cell.reshape(1, listed),
        adjoint_final,
        conductivity,
        step_ratio,
        refine_rate,
    )
    below = shift(fields, "gz", 1, False)
    above = shift(fields, "gz", -1, False)
    sensors = lax.all_to_all(message, ("gx", "gy"), 0, 0, tiled=True)
    packed = (pl.cdiv(len(needed(layers)), PIECES), rows, LANES)
    block = (layers, 2, rows, LANES)
    lines = (rows // 2, LANES)
    centre = (5, layers) + lines
    to_left, to_right, up, down = call(pack_columns, [packed, packed, centre, centre])(below, fields, above)
    from_left = shift(to_right, "gy", 1, False)
    from_right = shift(to_left, "gy", -1, False)
    over_fixed = shift(down, "gx", 1, True)
    under_fixed = shift(up, "gx", -1, True)
    side = (5, layers // 2) + lines
    state, fixed, up, down = call(prepare, [block, (5,) + block, side, side])(
        below, fields, above, from_left, from_right
    )
    over_side = shift(down, "gx", 1, True)
    under_side = shift(up, "gx", -1, True)
    halo = (2 * (layers + layers // 2),) + lines
    first_state, second, up, down = call(
        functools.partial(first_sources, "gz", own), [block, block, halo, halo]
    )(state, sensors)
    fixed, counts = call(
        functools.partial(conduct, ("gx", "gy")), [(5, layers, 2, 2 * rows, LANES), (2, 2 * rows, LANES)]
    )(substeps.T, fixed, over_fixed, under_fixed, over_side, under_side)
    (rest,) = call(functools.partial(other_sources, "gz", own), [(2,) + block])(sensors)
    over = shift(down, "gx", 1, True)
    under = shift(up, "gx", -1, True)
    depth = layers - 4
    halo = (2 * (depth + depth // 2),) + lines
    state, up, down, sens = call(
        functools.partial(two_steps, False), [(depth, 2, rows, LANES), halo, halo, (own, rows, cols)]
    )(counts, first_state, fixed, over, under, second, rest)
    over = shift(down, "gx", 1, True)
    under = shift(up, "gx", -1, True)
    return tuple(
        call(functools.partial(two_steps, True), [(own, rows, cols), (own, rows, cols)])(
            counts, state, fixed, over, under, rest[0], sens
        )
    )


def solution(mesh):
    return jax.shard_map(
        body,
        mesh=mesh,
        in_specs=(
            P("gz", "gx", "gy"),
            P(None, "gz", "gx", "gy"),
            P("gz", "gx", "gy"),
            P("gz", "gx", "gy"),
            P(None, ("gx", "gy")),
            P(("gx", "gy")),
            P(("gx", "gy")),
            P(),
        ),
        out_specs=(P("gz", "gx", "gy"), P("gz", "gx", "gy")),
        check_vma=False,
    )
```

```python
import functools

import jax
import jax.numpy as jnp
from jax import lax
from jax.experimental import pallas as pl
from jax.experimental.pallas import tpu as pltpu
from jax.sharding import PartitionSpec as P


F32 = jnp.float32
BF16 = jnp.bfloat16
LANES = 128
WIDE = 24
PIECES = LANES // WIDE
MAXSUB = 6
SLOTS = 4
FIELDS = 6
TINY = 1e-30
LIMIT = 24 * 2**20
WHOLE = 66_800_000


def iota(shape, dim):
    return lax.broadcasted_iota(jnp.int32, shape, dim)


def harmonic(first, second):
    return 2.0 * first * second / jnp.maximum(first + second, TINY)


def swap(field):
    return jnp.concatenate([field[:, 1:2], field[:, 0:1]], axis=1)


def call(kernel, outs, cost=20000, grant=LIMIT):
    vmem = pl.BlockSpec(memory_space=pltpu.VMEM)

    def run(*args):
        return pl.pallas_call(
            kernel,
            out_shape=[jax.ShapeDtypeStruct(o, F32) for o in outs],
            in_specs=[vmem] * len(args),
            out_specs=[vmem] * len(outs),
            compiler_params=pltpu.CompilerParams(vmem_limit_bytes=grant),
            cost_estimate=pl.CostEstimate(flops=cost, bytes_accessed=cost, transcendentals=0),
        )(*args)

    return run


def pack(gy, residual_ref, tile_ref, cell_ref, adjoint_ref, conductivity_ref, ratio_ref, rate_ref, fields_ref, out_ref):
    fields_ref[0] = adjoint_ref[...]
    fields_ref[1:4] = conductivity_ref[...]
    fields_ref[4] = ratio_ref[...]
    fields_ref[5] = rate_ref[...]
    count = residual_ref.shape[1]
    tiles = out_ref.shape[0]
    eye = iota((count, count), 0) == iota((count, count), 1)

    def column(row):
        return jnp.sum(jnp.where(eye, jnp.broadcast_to(row, (count, count)), 0.0), axis=1, keepdims=True)

    named = tile_ref[...]
    tile_row = named.astype(F32)
    tile_col = column(tile_row)
    same = (tile_col == tile_row) & (iota((count, count), 1) < iota((count, count), 0))
    rank = jnp.sum(same.astype(F32), axis=1, keepdims=True).astype(jnp.int32)
    values = [column(residual_ref[s : s + 1, :]) for s in range(4)]
    values.append(column(cell_ref[...].astype(F32) + 1.0))
    lane = iota((count, LANES), 1)
    within = lane % 8
    spread = jnp.zeros((count, LANES), F32)
    for place, value in enumerate(values):
        spread = jnp.where(within == place, value, spread)
    spread = jnp.where((lane % 32) // 8 == rank, spread, 0.0)
    tile_at = iota((tiles, count), 0)
    total = jnp.zeros((tiles, LANES), F32)
    for group, (step, edge) in enumerate(((0, -1), (-1, 0), (1, gy - 1))):
        hit = (named == tile_at + step) & (tile_at % gy != edge)
        part = jnp.where(lane // 32 == group, spread, 0.0)
        total = total + jnp.dot(hit.astype(F32), part, precision=lax.Precision.HIGHEST, preferred_element_type=F32)
    out_ref[...] = total


def needed(layers):
    return [(f, l) for f in range(FIELDS) for l in range(layers) if f in (0, 3, 4) or 0 < l < layers - 1]


def stacked(refs, field, layer):
    each = refs[0].shape[1]
    return refs[layer // each][field, layer % each]


def pack_columns(below_ref, own_ref, above_ref, left_ref, right_ref):
    refs = (below_ref, own_ref, above_ref)
    layers = 3 * own_ref.shape[1]
    rows = own_ref.shape[2]
    piece = iota((rows, LANES), 1) // WIDE
    planes = needed(layers)
    for j in range(left_ref.shape[0]):
        left = right = None
        for q, (f, l) in enumerate(planes[j * PIECES : (j + 1) * PIECES]):
            plane = stacked(refs, f, l)
            to_left = plane if q == 0 else pltpu.roll(plane, WIDE * q, 1)
            to_right = pltpu.roll(plane, WIDE * q + WIDE, 1)
            left = to_left if q == 0 else jnp.where(piece == q, to_left, left)
            right = to_right if q == 0 else jnp.where(piece == q, to_right, right)
        left_ref[j] = left
        right_ref[j] = right


def spread_column(columns, at, shape):
    return jnp.broadcast_to(columns[:, at : at + 1], shape)


def sources(layer_axis, own, layers, rows, sensors_ref, steps):
    got = sensors_ref[...]
    blocks = got.shape[0]
    lane = iota((blocks, LANES), 1)
    lane_at = lane.astype(F32)
    cell = got.astype(jnp.int32) - 1
    row_base = (lax.axis_index(layer_axis) * own - own) * rows
    cell_row = ((cell >> 7) - row_base).astype(F32).T
    cell_col = cell & (LANES - 1)
    half = LANES // 2
    group_of = lane // 32
    cell_col = jnp.where(
        group_of == 0,
        cell_col,
        jnp.where(
            group_of == 1,
            jnp.where(cell_col >= LANES - WIDE, cell_col - half, -LANES),
            jnp.where(cell_col < WIDE, cell_col, -LANES),
        ),
    ).astype(F32)
    row_at = iota((layers * rows, blocks), 0).astype(F32)
    high = got.astype(BF16)
    values = (high, (got - high.astype(F32)).astype(BF16))
    onehots, tables = ([], []), ([], [])
    for group in range(3):
        for slot in range(SLOTS):
            base = group * 32 + slot * 8
            onehots[group > 0].append((cell_row[base + 4 : base + 5, :] == row_at).astype(F32).astype(BF16))
            at = spread_column(cell_col, base + 4, lane.shape)
            pairs = (0, half) if group > 0 and len(steps) > 1 else (0,)
            place = [(at == lane_at - by).astype(F32).astype(BF16) for by in pairs]
            line = []
            for part in range(2):
                cells = [spread_column(values[part], base + s, lane.shape) for s in steps]
                for k in range(0, len(cells), len(place)):
                    line.append(functools.reduce(jnp.add, [m * v for m, v in zip(place, cells[k : k + len(place)])]))
            tables[group > 0].append(jnp.concatenate(line, axis=1))
    sums = []
    for onehot, table in zip(onehots, tables):
        both = jnp.dot(jnp.concatenate(onehot, axis=1), jnp.concatenate(table, axis=0), preferred_element_type=F32)
        width = both.shape[1] // 2
        sums.append(both[:, :width] + both[:, width:])
    centre, side = sums
    lane = iota((layers * rows, LANES), 1)
    out = []
    for s in range(len(steps)):
        tile = side[:, (s // 2) * LANES : (s // 2 + 1) * LANES]
        turned = pltpu.roll(tile, half, 1)
        right, left = (tile, turned) if s % 2 == 0 else (turned, tile)
        beside = jnp.where(lane < WIDE, right, jnp.where(lane >= LANES - WIDE, left, 0.0))
        parts = [m.reshape(layers, 1, rows, LANES) for m in (centre[:, s * LANES : (s + 1) * LANES], beside)]
        out.append(jnp.concatenate(parts, axis=1))
    return out


def prepare(below_ref, own_ref, above_ref, left_ref, right_ref, state_ref, fixed_ref, up_ref, down_ref):
    refs = (below_ref, own_ref, above_ref)
    own = own_ref.shape[1]
    layers = 3 * own
    rows = own_ref.shape[2]
    lane = iota((rows, LANES), 1)

    listed = {plane: at for at, plane in enumerate(needed(layers))}

    def field(f):
        planes = []
        for l in range(layers):
            if (f, l) in listed:
                j, q = divmod(listed[f, l], PIECES)
                from_left = pltpu.roll(left_ref[j], (LANES - WIDE - WIDE * q) % LANES, 1)
                from_right = pltpu.roll(right_ref[j], LANES - WIDE * q, 1) if q != 0 else right_ref[j]
                side = jnp.where(lane < WIDE, from_right, jnp.where(lane >= LANES - WIDE, from_left, 0.0))
            else:
                side = jnp.zeros((rows, LANES), F32)
            planes.append(jnp.stack([stacked(refs, f, l), side], axis=0))
        return jnp.stack(planes, axis=0)

    state_ref[...] = field(0)
    half = rows // 2
    for f in range(1, FIELDS):
        values = field(f)
        fixed_ref[f - 1] = values
        start, stop, trim = sent(f - 1, layers)
        values = values[trim : layers - trim]
        up_ref[start:stop] = fold(values[:, :, :half])
        down_ref[start:stop] = fold(values[:, :, half:])


def sent(field, layers):
    trims = [0 if f in (2, 3) else 1 for f in range(5)]
    sizes = [(layers - 2 * trim) * 3 // 2 for trim in trims]
    start = sum(sizes[:field])
    return start, start + sizes[field], trims[field]


def fold(block):
    half = block.shape[0] // 2
    lane = iota((half,) + block.shape[2:], 2)
    used = (lane < WIDE) | (lane >= LANES - WIDE)
    low, high = (jnp.where(used, part, 0.0) for part in (block[:half, 1], block[half:, 1]))
    return jnp.concatenate([block[:, 0], low + pltpu.roll(high, LANES // 2, 2)], axis=0)


def unfold(folded):
    layers = folded.shape[0] * 2 // 3
    shared = folded[layers:]
    lane = iota(shared.shape, 2)
    used = (lane < WIDE) | (lane >= LANES - WIDE)
    parts = [jnp.where(used, part, 0.0) for part in (shared, pltpu.roll(shared, LANES // 2, 2))]
    return jnp.stack([folded[:layers], jnp.concatenate(parts, axis=0)], axis=1)


def conduct(axes, substeps_ref, own_ref, over_ref, under_ref, fixed_ref, counts_ref):
    at_x, at_y = (lax.axis_index(axis) for axis in axes)
    n_y, n_x = substeps_ref.shape
    named = substeps_ref[...].astype(F32)
    size = own_ref.shape[3] // 2
    lane = iota((size, LANES), 1)

    def count(x, y):
        hit = (iota((n_y, n_x), 1) == x) & (iota((n_y, n_x), 0) == y)
        found = jnp.sum(jnp.where(hit, named, 0.0), axis=1, keepdims=True)
        return jnp.broadcast_to(jnp.sum(found, axis=0, keepdims=True), (size, LANES))

    for part, x in enumerate((at_x - 1, at_x, at_x, at_x + 1)):
        at_rows = slice(part * size, (part + 1) * size)
        counts_ref[0, at_rows] = count(x, at_y)
        counts_ref[1, at_rows] = jnp.where(lane < LANES // 2, count(x, at_y + 1), count(x, at_y - 1))

    def deep(f, masked=False):
        start, stop, trim = sent(f, own_ref.shape[1])
        over, under = unfold(over_ref[start:stop]), unfold(under_ref[start:stop])
        if trim:
            none = jnp.zeros((trim,) + over.shape[1:], F32)
            over, under = (jnp.concatenate([none, part, none], axis=0) for part in (over, under))
        if masked:
            over = jnp.where(at_x > 0, over, 0.0)
            under = jnp.where(at_x < n_x - 1, under, 0.0)
        return jnp.concatenate([over, own_ref[f], under], axis=2)

    along_rows = deep(0, True)
    shape = along_rows.shape
    layers, _, rows, _ = shape
    row = iota(shape, 2)
    col = iota(shape, 3)
    fixed_ref[0] = harmonic(along_rows, jnp.where(row == rows - 1, 0.0, pltpu.roll(along_rows, rows - 1, 2)))
    along_cols = deep(1)
    rolled = pltpu.roll(along_cols, LANES - 1, 3)
    fixed_ref[1] = harmonic(along_cols, jnp.where(col == LANES - 1, swap(rolled), rolled))
    along_layers = deep(2)
    fixed_ref[2, : layers - 1] = harmonic(along_layers[: layers - 1], along_layers[1:])
    fixed_ref[2, layers - 1 :] = jnp.zeros((1,) + shape[1:], F32)
    fixed_ref[3] = deep(3)
    fixed_ref[4] = deep(4)


def send_rows(state, source, up_ref, down_ref):
    half = state.shape[2] // 2
    up_ref[0] = fold(state[:, :, :half])
    up_ref[1] = fold(source[:, :, :half])
    down_ref[0] = fold(state[:, :, half:])
    down_ref[1] = fold(source[:, :, half:])


def first_sources(layer_axis, own, state_in, sensors_ref, state_ref, source_ref, up_ref, down_ref):
    layers, _, rows, _ = state_ref.shape
    second, first = sources(layer_axis, own, layers, rows, sensors_ref, (2, 3))
    state = state_in[...] + first
    state_ref[...] = state
    source_ref[...] = second
    send_rows(state, second, up_ref, down_ref)


def other_sources(layer_axis, own, sensors_ref, source_ref):
    _, layers, _, rows, _ = source_ref.shape
    for s, source in enumerate(sources(layer_axis, own, layers, rows, sensors_ref, (0, 1))):
        source_ref[s] = source


def diffuse(fixed_ref, low, state, kept):
    layers = state.shape[0]
    span, inner = slice(low, low + layers), slice(low + 1, low + layers - 1)
    weighted = fixed_ref[3, span] * state
    across = weighted[1:-1]
    flux = fixed_ref[0, inner] * (pltpu.roll(across, across.shape[2] - 1, 2) - across)
    change = (flux - pltpu.roll(flux, 1, 2))[:, :, kept]
    weighted, across = weighted[:, :, kept], across[:, :, kept]
    col = iota(across.shape, 3)
    rolled = pltpu.roll(across, LANES - 1, 3)
    flux = fixed_ref[1, inner, :, kept] * (jnp.where(col == LANES - 1, swap(rolled), rolled) - across)
    rolled = pltpu.roll(flux, 1, 3)
    change = change + (flux - jnp.where(col == 0, swap(rolled), rolled))
    flux = fixed_ref[2, low : low + layers - 1, :, kept] * (weighted[1:] - weighted[:-1])
    change = change + (flux[1:] - flux[:-1])
    return state[1:-1, :, kept] + change


def refine(state, rate, counts, tiles):
    size = 8
    shape = state.shape[:2] + (size, LANES)
    row, col = iota(shape, 2), iota(shape, 3)
    pieces = range(state.shape[2] // size)
    at_rows = [slice(p * size, (p + 1) * size) for p in pieces]
    rates = [rate[:, :, r] for r in at_rows]
    keeps = [1.0 - 4.0 * r for r in rates]
    limits = [counts[:, :, r] for r in at_rows]
    now = [state[:, :, r] for r in at_rows]
    for turn in range(MAXSUB):
        scaled = [rates[p] * now[p] for p in pieces]
        later = list(now)
        for tile in tiles:
            ups = {p: pltpu.roll(scaled[p], size - 1, 2) for p in tile}
            downs = {p: pltpu.roll(scaled[p], 1, 2) for p in tile}
            for p in tile:
                v = scaled[p]
                near = jnp.where(row == size - 1, ups[p + 1] if p + 1 in tile else v, ups[p])
                near = near + jnp.where(row == 0, downs[p - 1] if p - 1 in tile else v, downs[p])
                near = near + jnp.where(col == LANES - 1, v, pltpu.roll(v, LANES - 1, 3))
                near = near + jnp.where(col == 0, v, pltpu.roll(v, 1, 3))
                after = keeps[p] * now[p] + near
                later[p] = after if turn == 0 else jnp.where(limits[p] > turn, after, now[p])
        now = later
    return jnp.concatenate(now, axis=2)


def two_steps(last, counts_ref, state_ref, fixed_ref, over_ref, under_ref, between_ref, *refs):
    if last:
        sens_ref, state_out, sens_out = refs
    else:
        rest_ref, state_out, up_out, down_out, sens_out = refs
    layers, _, rows, _ = state_ref.shape
    total = fixed_ref.shape[1]
    own = total // 3
    low = (total - layers) // 2
    half = rows // 2
    mine = slice(half, half + rows)
    everything = slice(0, 2 * rows)

    def deep(field, at):
        return jnp.concatenate([unfold(over_ref[at]), field, unfold(under_ref[at])], axis=2)

    def sensed(state, first_row):
        keep = slice((state.shape[0] - own) // 2, (state.shape[0] - own) // 2 + own)
        return fixed_ref[3, own : 2 * own, 0, mine] * state[keep, 0, first_row : first_row + rows]

    state = diffuse(fixed_ref, low, deep(state_ref[...], 0), everything)
    state = refine(state, fixed_ref[4, low + 1 : low + layers - 1], counts_ref[...][None], ((0,), (1, 2), (3,)))
    sens = sensed(state, half)
    if last:
        sens = sens_ref[...] + sens
    state = state + deep(between_ref[low : low + layers], 1)[1:-1]
    state = diffuse(fixed_ref, low + 1, state, mine)
    halves = slice(0, 1) if last else slice(0, 2)
    inner = slice(low + 2, low + layers - 2)
    state = refine(state[:, halves], fixed_ref[4, inner, halves, mine], counts_ref[halves, mine][None], ((0, 1),))
    sens_out[...] = sens + sensed(state, 0)
    if last:
        state_out[...] = state[:, 0]
        return
    state = state + rest_ref[1, inner]
    state_out[...] = state
    send_rows(state, rest_ref[0, inner], up_out, down_out)


def shift(cells, axis, by, wrap):
    count = lax.axis_size(axis)
    pairs = [(i, (i + by) % count) for i in range(count) if wrap or 0 <= i + by < count]
    return lax.ppermute(cells, axis, pairs)


def body(adjoint_final, conductivity, step_ratio, refine_rate, residual, sensor_tile, sensor_cell, substeps):
    own, rows, cols = adjoint_final.shape
    layers = 3 * own
    n_y = lax.axis_size("gy")
    tiles = lax.axis_size("gx") * n_y
    listed = sensor_tile.shape[0]
    fields, message = call(functools.partial(pack, n_y), [(FIELDS, own, rows, cols), (tiles, LANES)], grant=WHOLE)(
        residual,
        sensor_tile.reshape(1, listed),
        sensor_cell.reshape(1, listed),
        adjoint_final,
        conductivity,
        step_ratio,
        refine_rate,
    )
    below = shift(fields, "gz", 1, False)
    above = shift(fields, "gz", -1, False)
    sensors = lax.all_to_all(message, ("gx", "gy"), 0, 0, tiled=True)
    packed = (pl.cdiv(len(needed(layers)), PIECES), rows, LANES)
    to_left, to_right = call(pack_columns, [packed, packed])(below, fields, above)
    from_left = shift(to_right, "gy", 1, False)
    from_right = shift(to_left, "gy", -1, False)
    block = (layers, 2, rows, LANES)
    halo = (layers + layers // 2, rows // 2, LANES)
    state, fixed, up, down = call(prepare, [block, (5,) + block] + [(sent(4, layers)[1],) + halo[1:]] * 2)(
        below, fields, above, from_left, from_right
    )
    over = shift(down, "gx", 1, True)
    under = shift(up, "gx", -1, True)
    first_state, second, up, down = call(
        functools.partial(first_sources, "gz", own), [block, block, (2,) + halo, (2,) + halo]
    )(state, sensors)
    fixed, counts = call(
        functools.partial(conduct, ("gx", "gy")), [(5, layers, 2, 2 * rows, LANES), (2, 2 * rows, LANES)]
    )(substeps.T, fixed, over, under)
    (rest,) = call(functools.partial(other_sources, "gz", own), [(2,) + block])(sensors)
    over = shift(down, "gx", 1, True)
    under = shift(up, "gx", -1, True)
    depth = layers - 4
    halo = (2, depth + depth // 2, rows // 2, LANES)
    state, up, down, sens = call(
        functools.partial(two_steps, False), [(depth, 2, rows, LANES), halo, halo, (own, rows, cols)]
    )(counts, first_state, fixed, over, under, second, rest)
    over = shift(down, "gx", 1, True)
    under = shift(up, "gx", -1, True)
    return tuple(
        call(functools.partial(two_steps, True), [(own, rows, cols), (own, rows, cols)])(
            counts, state, fixed, over, under, rest[0], sens
        )
    )


def solution(mesh):
    return jax.shard_map(
        body,
        mesh=mesh,
        in_specs=(
            P("gz", "gx", "gy"),
            P(None, "gz", "gx", "gy"),
            P("gz", "gx", "gy"),
            P("gz", "gx", "gy"),
            P(None, ("gx", "gy")),
            P(("gx", "gy")),
            P(("gx", "gy")),
            P(),
        ),
        out_specs=(P("gz", "gx", "gy"), P("gz", "gx", "gy")),
        check_vma=False,
    )
```
